32 devices in a mesh: row: 4 (over y, core), col: 8 (over z, x).
Axes of the slice: x: 2, y: 2, z: 4, core: 2. Of those that a mesh axis runs over, the one named last changes fastest.
Arguments:
- precip: float32 [1024, 4096], P('row', 'col'), may hold values from 0.002 to 0.02
- head: float32 [1024, 4096], P('row', 'col'), may hold values from -4 to 4
- trans_coef: float32 [1024, 4096], P('row', 'col'), may hold values from 0.05 to 0.5
- land: int32 [1024, 4096], P('row', 'col'), may hold values 0 or 1
- dest: int32 [1024, 32], P('row', 'col'), may hold values from 0 to 32767, as said below
- moisture: float32 [32768, 16, 128], P(('row', 'col')), may hold values from 0.08 to 0.42
- ksat: float32 [32768, 128], P(('row', 'col')), may hold values from 0.002 to 0.01
Outputs:
- saturation: float32 [32768, 16, 128], P(('row', 'col'))
- head_new: float32 [1024, 4096], P('row', 'col')
The draws below stay inside these ranges and needn't reach their ends.
Inputs may be any that keep to these rules, and one draw needn't show every extreme that they name: dest is a permutation of 0 .. 32767; its value is an owner's index along row+col times 1024 plus a slot. At most 64 blocks of one device's tile go to one owner, and every device sends exactly 64 to some owner; every owner receives 1024 blocks.
All inputs are finite; a program needn't handle non-finite values. No bound on the sum of `land` on one device may be relied on, other than what follows from the above.
Results may differ from the reference program's by a relative error of at most 0.00002.
Values sent between devices are 32-bit elements; how exact they have to be, the bound alone decides.
A program may use at most 192 MiB of HBM per device.

```python
import math
import jax
import jax.numpy as jnp

L = 16
TR = 256
TC = 512
SWEEPS = 4
SLOTS = 1024
CAP = 64
NR = 1024
NC = 4096
NBLK = 32768
N_ROW = 4
N_COL = 8


def permuted_slot_list(subkey):
    return jax.random.permutation(subkey, SLOTS)


def draw_dest(key, part):
    processor_units = N_ROW * N_COL
    tickets_total = processor_units * CAP
    key_shuffle, key_leading, key_local, slot_key_random = jax.random.split(key, 4)
    tickets = jnp.arange(tickets_total, dtype=jnp.int32) // CAP
    shuffled = jax.random.permutation(key_shuffle, tickets)
    leading = jax.random.randint(key_leading, (), 0, processor_units, dtype=jnp.int32)
    scores = (shuffled != leading).astype(jnp.int32) * tickets_total + jnp.arange(tickets_total, dtype=jnp.int32)
    ranking = jnp.argsort(scores)
    shifts = shuffled[ranking[:SLOTS]]
    worker_rank_here = jax.vmap(permuted_slot_list)(jax.random.split(key_local, processor_units))
    relabel_blocks = jax.vmap(permuted_slot_list)(jax.random.split(slot_key_random, processor_units))
    sources = jnp.arange(processor_units, dtype=jnp.int32)[:, None]
    block_owner_list = (sources + shifts[worker_rank_here]) % processor_units
    slot_number = relabel_blocks[block_owner_list, worker_rank_here]
    target = block_owner_list * SLOTS + slot_number
    layout = target.reshape(N_ROW, N_COL, TR, TC // 128).transpose(0, 2, 1, 3)
    return layout.reshape(NR, NC // 128).astype(jnp.int32)


def place_ends(result, own_key, least, largest):
    shape = result.shape
    spot = [jax.random.randint(jax.random.fold_in(own_key, axis), (), 0, shape[axis]) for axis in range(len(shape))]
    result = result.at[tuple(spot)].set(least)
    longest = shape.index(max(shape))
    spot[longest] = (spot[longest] + 1) % shape[longest]
    return result.at[tuple(spot)].set(largest)


def block_scale(key, extent, shards, least, high):
    gain, own = 1.0, jax.random.fold_in(key, 6)
    for position, parts in shards:
        heights = jnp.exp(jax.random.uniform(jax.random.fold_in(own, position), (parts,), jnp.float32, least / len(shards), high / len(shards)))
        gain = gain * jnp.repeat(heights, extent[position] // parts).reshape([-1 if axis == position else 1 for axis in range(len(extent))])
    return gain


def gaussian(key, dims, deviation, most, cuts=(), kind=jnp.bfloat16):
    gain = block_scale(key, dims, cuts, -0.22, 0.18) if cuts else 1.0
    entries = jax.random.normal(key, dims, jnp.float32) * deviation * gain
    return jnp.minimum(jnp.maximum(entries, -most), most).astype(kind)


def setup_inputs(seed: int = 0) -> dict:
    key_of = jax.random.split(jax.random.key(seed), 8)
    precip = jnp.clip(jnp.exp(math.log(0.02) - 2.30258502 * jax.random.uniform(key_of[0], (NR, NC), jnp.float32) ** block_scale(key_of[0], (NR, NC), ((0, 4), (1, 8)), -0.2, 0.2)), 0.002, 0.02)
    head = gaussian(key_of[1], (NR, NC), 1.0, 4.0, ((0, 4), (1, 8)), jnp.float32)
    trans_coef = jnp.clip(jnp.exp(math.log(0.5) - 2.3025851 * jax.random.uniform(key_of[2], (NR, NC), jnp.float32) ** block_scale(key_of[2], (NR, NC), ((0, 4), (1, 8)), -0.2, 0.2)), 0.05, 0.5)
    land = place_ends((jax.random.randint(key_of[3], (NR, NC), 0, 4) < 3).astype(jnp.int32), jax.random.fold_in(key_of[3], 1), 0, 1)
    dest = draw_dest(jax.random.fold_in(key_of[7], 71), 0)
    moisture = jnp.clip(0.08 + 0.3399999886751175 * jax.random.uniform(key_of[5], (NBLK, L, 128), jnp.float32) ** block_scale(key_of[5], (NBLK, L, 128), ((0, 32),), -0.2, 0.2), 0.08, 0.42)
    ksat = jnp.clip(jnp.exp(math.log(0.01) - 1.6094378 * jax.random.uniform(key_of[6], (NBLK, 128), jnp.float32) ** block_scale(key_of[6], (NBLK, 128), ((0, 32),), -0.2, 0.2)), 0.002, 0.01)
    return {"precip": precip, "head": head, "trans_coef": trans_coef, "land": land, "dest": dest, "moisture": moisture, "ksat": ksat}


layer_depth = 0.1
step_ratio = 0.1
residual_water = 0.05
pore_range = 0.4
diff_length = 0.5
couple_rate = 0.05
recharge_gain = 20.0
store_rate = 0.2


def factor(moisture, ksat):
    layers = moisture.shape[1]
    depths = (jnp.arange(layers, dtype=jnp.float32) + 0.5) * layer_depth
    scaled_k = ksat[:, None, :] * jnp.exp(-depths)[None, :, None]
    wetness = (moisture - residual_water) / pore_range
    conduct = scaled_k * wetness * wetness * wetness
    slopes = 3.0 * scaled_k * wetness * wetness / pore_range
    diffusion = scaled_k * diff_length * (0.2 + wetness * wetness)
    coupling = (diffusion[:, :-1] + diffusion[:, 1:]) / (2.0 * layer_depth)
    subs, pivots, ratios = [], [], []
    for k in range(layers):
        diagonal = step_ratio + jnp.zeros_like(moisture[:, k])
        if k > 0:
            diagonal = diagonal + coupling[:, k - 1]
        if k < layers - 1:
            diagonal = diagonal + coupling[:, k]
        if k == 0:
            diagonal = diagonal + 0.5 * slopes[:, 0]
        if k == layers - 1:
            diagonal = diagonal + 0.5 * slopes[:, k] + couple_rate
        if k > 0:
            sub_term = -(0.5 * slopes[:, k - 1] + coupling[:, k - 1])
            pivot_k = diagonal - sub_term * ratios[k - 1]
        else:
            sub_term = jnp.zeros_like(diagonal)
            pivot_k = diagonal
        if k < layers - 1:
            ratio_k = (0.5 * slopes[:, k + 1] - coupling[:, k]) / pivot_k
        else:
            ratio_k = jnp.zeros_like(diagonal)
        subs.append(sub_term)
        pivots.append(pivot_k)
        ratios.append(ratio_k)
    return conduct, slopes, coupling, subs, pivots, ratios


def solve(moisture, factors, infiltration, owned_head):
    conduct, slopes, coupling, subs, pivots, ratios = factors
    layers = moisture.shape[1]
    face_flux = 0.5 * (conduct[:, :-1] + conduct[:, 1:]) - coupling * (moisture[:, 1:] - moisture[:, :-1])
    table = residual_water + pore_range * jax.nn.sigmoid(owned_head)
    bottom = conduct[:, -1] + couple_rate * (moisture[:, -1] - table)
    reduced = []
    for k in range(layers):
        above = infiltration if k == 0 else face_flux[:, k - 1]
        below = bottom if k == layers - 1 else face_flux[:, k]
        right_side = above - below
        if k > 0:
            right_side = right_side - subs[k] * reduced[k - 1]
        reduced.append(right_side / pivots[k])
    change = [None] * layers
    change[layers - 1] = reduced[layers - 1]
    for k in range(layers - 2, -1, -1):
        change[k] = reduced[k] - ratios[k] * change[k + 1]
    updated = moisture + jnp.stack(change, axis=1)
    saturation = (updated - residual_water) / pore_range
    recharge = bottom + (slopes[:, -1] + couple_rate) * change[layers - 1]
    return saturation, recharge


def relax(source_term, trans_pad, head_pad, land_share):
    center_t = trans_pad[1:-1, 1:-1]
    face_up = 0.5 * (center_t + trans_pad[:-2, 1:-1])
    face_down = 0.5 * (center_t + trans_pad[2:, 1:-1])
    face_left = 0.5 * (center_t + trans_pad[1:-1, :-2])
    face_right = 0.5 * (center_t + trans_pad[1:-1, 2:])
    total_t = face_up + face_down + face_left + face_right
    inflow = face_up * head_pad[:-2, 1:-1] + face_down * head_pad[2:, 1:-1]
    inflow = inflow + face_left * head_pad[1:-1, :-2] + face_right * head_pad[1:-1, 2:]
    return (source_term + inflow) / (store_rate + total_t) * land_share


def reference(precip, head, trans_coef, land, dest, moisture, ksat):
    grid_rows, grid_cols = precip.shape
    count = grid_rows * grid_cols // 128
    land_share = land.astype(jnp.float32)
    infiltration = (precip * land_share).reshape(count, 128)
    head_blocks = head.reshape(count, 128)
    target = dest.reshape(count)
    owned_infil = jnp.zeros_like(infiltration).at[target].set(infiltration)
    owned_head = jnp.zeros_like(head_blocks).at[target].set(head_blocks)
    factors = factor(moisture, ksat)
    saturation, recharge = solve(moisture, factors, owned_infil, owned_head)
    tile_recharge = recharge[target].reshape(grid_rows, grid_cols)
    initial = head * land_share
    transmit = trans_coef * (1.0 + 0.5 * jnp.tanh(head))
    source_term = store_rate * initial + recharge_gain * tile_recharge
    trans_pad = jnp.pad(transmit, 1)
    surface = initial
    for sweep_k in range(SWEEPS):
        surface = relax(source_term, trans_pad, jnp.pad(surface, 1), land_share)
    return saturation, surface
```

```python
import functools
import math

import jax
import jax.numpy as jnp
from jax import lax
from jax.experimental import pallas as pl
from jax.experimental.pallas import tpu as pltpu
from jax.sharding import PartitionSpec as P

SWEEPS = 4
LANES = 128

layer_depth = 0.1
step_ratio = 0.1
residual_water = 0.05
pore_range = 0.4
diff_length = 0.5
couple_rate = 0.05
recharge_gain = 20.0
store_rate = 0.2

VM = pl.BlockSpec(memory_space=pltpu.VMEM)
SM = pl.BlockSpec(memory_space=pltpu.SMEM)


def f32(*shape):
    return jax.ShapeDtypeStruct(shape, jnp.float32)


def pack_kernel(peers, per_peer, src, labels, precip, head, land, out, infil, heads):
    rows, cols = precip.shape
    for j in range(cols // LANES):
        part = pl.ds(j * LANES, LANES)
        infil[pl.ds(j * rows, rows), :] = precip[:, part] * land[:, part].astype(jnp.float32)
        heads[pl.ds(j * rows, rows), :] = head[:, part]

    def body(p, _):
        for r in range(per_peer):
            block = src[p * per_peer + r]
            out[p, pl.ds(r, 1), :] = infil[pl.ds(block, 1), :]
            out[p, pl.ds(per_peer + r, 1), :] = heads[pl.ds(block, 1), :]
        out[p, pl.ds(2 * per_peer, 8), :] = jnp.broadcast_to(labels[pl.ds(p, 1), :], (8, LANES))
        return 0

    lax.fori_loop(0, peers, body, 0)


def owner_kernel(
    peers, per_peer, slots, arrived, rec0, rec_x, rec_y, answer, infil, sig, own_i, own_h, rec
):
    owned = rec0.shape[0]

    def scatter(p, _):
        for r in range(per_peer):
            slot = slots[p * per_peer + r]
            own_i[pl.ds(slot, 1), :] = arrived[p, pl.ds(r, 1), :]
            own_h[pl.ds(slot, 1), :] = arrived[p, pl.ds(per_peer + r, 1), :]
        return 0

    lax.fori_loop(0, peers, scatter, 0)
    rec[pl.ds(owned, 8), :] = jnp.zeros((8, LANES), jnp.float32)

    def combine(g, _):
        part = pl.ds(g * 64, 64)
        inf = own_i[part, :]
        sg = jax.nn.sigmoid(own_h[part, :])
        infil[part, :] = inf
        sig[part, :] = sg
        rec[part, :] = rec0[part, :] + inf * rec_x[part, :] + sg * rec_y[part, :]
        return 0

    lax.fori_loop(0, owned // 64, combine, 0)

    def gather(p, _):
        for r in range(per_peer):
            slot = slots[p * per_peer + r]
            answer[p, pl.ds(r, 1), :] = rec[pl.ds(slot, 1), :]
        return 0

    lax.fori_loop(0, peers, gather, 0)


def factor_kernel(layers, group, moist, ksat, s0, sx, sy, rec0, rec_x, rec_y):
    count = ksat.shape[0]

    def body(step, _):
        base_row = step * group
        rows = pl.ds(pl.multiple_of(base_row, group), group)
        ks = ksat[rows, :]
        ratios, reds, xs = [], [], []
        before = None
        for k in range(layers):
            m = moist[pl.ds(base_row * layers + k, group, stride=layers), :]
            w = (m - residual_water) * (1.0 / pore_range)
            s = ks * math.exp(-(k + 0.5) * layer_depth)
            sw2 = s * (w * w)
            hs = sw2 * (1.5 / pore_range)
            d = s * (0.2 * diff_length / (2.0 * layer_depth)) + sw2 * (
                diff_length / (2.0 * layer_depth)
            )
            hc = 0.5 * (sw2 * w)
            cur = (m, hs, d, hc)
            if before is None:
                before = cur
                g_up = q_up = nsub = None
                continue
            m0, hs0, d0, hc0 = before
            g = d0 + d
            q = (hc0 + hc) - g * (m - m0)
            if g_up is None:
                pivot = step_ratio + g + hs0
                inv = 1.0 / pivot
                reds.append(-q * inv)
                xs.append(inv)
            else:
                pivot = step_ratio + g_up + g - nsub * ratios[-1]
                inv = 1.0 / pivot
                reds.append(((q_up - q) + nsub * reds[-1]) * inv)
                xs.append(nsub * inv * xs[-1])
            ratios.append((g - hs) * inv)
            nsub = hs0 + g
            g_up, q_up = g, q
            before = cur
        m, hs, d, hc = before
        bottom = 2.0 * hc + couple_rate * (m - residual_water)
        pivot = step_ratio + g_up + hs + couple_rate - nsub * ratios[-1]
        inv = 1.0 / pivot
        change = ((q_up - bottom) + nsub * reds[-1]) * inv
        cx = nsub * inv * xs[-1]
        cy = (couple_rate * pore_range) * inv
        gain = 2.0 * hs + couple_rate
        rec0[rows, :] = bottom + gain * change
        rec_x[rows, :] = gain * cx
        rec_y[rows, :] = gain * cy - couple_rate * pore_range
        unit = 1.0 / pore_range
        for k in range(layers - 1, -1, -1):
            if k < layers - 1:
                change = reds[k] + ratios[k] * change
                cx = xs[k] + ratios[k] * cx
                cy = ratios[k] * cy
            m = moist[pl.ds(base_row * layers + k, group, stride=layers), :]
            s0[k, rows, :] = (m + change - residual_water) * unit
            sx[k, rows, :] = cx * unit
            sy[k, rows, :] = cy * unit
        return 0

    lax.fori_loop(0, count // group, body, 0)


def saturation_kernel(layers, s0, sx, sy, infil, sig, out):
    count = infil.shape[0]
    group = 32

    def body(step, _):
        rows = pl.ds(pl.multiple_of(step * group, group), group)
        inf = infil[rows, :]
        sg = sig[rows, :]
        for k in range(layers):
            out[pl.ds(step * group * layers + k, group, stride=layers), :] = (
                s0[k, rows, :] + inf * sx[k, rows, :] + sg * sy[k, rows, :]
            )
        return 0

    lax.fori_loop(0, count // group, body, 0)


def relax_kernel(
    position, returned, head, land, mid, mid_r, mid_c, out,
    t_ref, s_ref, fu, fd, fl, fr, a, b, sorted_rows, strip_out, from_row, strip_in, corner, send_sem, recv_sem,
):
    rows, cols = head.shape
    high, wide = t_ref.shape
    row, col = lax.axis_index("row"), lax.axis_index("col")
    n_row, n_col = lax.axis_size("row"), lax.axis_size("col")
    up, down = row > 0, row < n_row - 1
    left, right = col > 0, col < n_col - 1
    east = cols - LANES
    south = rows - 8
    links = [
        (up, -1, 0, s_ref.at[pl.ds(0, 8), pl.ds(0, cols)], from_row.at[0]),
        (down, 1, 0, s_ref.at[pl.ds(south, 8), pl.ds(0, cols)], from_row.at[1]),
        (left, 0, -1, strip_out.at[0], strip_in.at[0]),
        (right, 0, 1, strip_out.at[1], strip_in.at[1]),
        (up & left, -1, -1, s_ref.at[pl.ds(0, 8), pl.ds(0, LANES)], corner.at[0]),
        (up & right, -1, 1, s_ref.at[pl.ds(0, 8), pl.ds(east, LANES)], corner.at[1]),
        (down & left, 1, -1, s_ref.at[pl.ds(south, 8), pl.ds(0, LANES)], corner.at[2]),
        (down & right, 1, 1, s_ref.at[pl.ds(south, 8), pl.ds(east, LANES)], corner.at[3]),
    ]
    come = [down, up, right, left, down & right, down & left, up & right, up & left]
    barrier = pltpu.get_barrier_semaphore()

    def each(flags, act):
        for k, flag in enumerate(flags):
            pl.when(flag)(functools.partial(act, k))

    def copy(k):
        _, dr, dc, src, dst = links[k]
        return pltpu.make_async_remote_copy(
            src_ref=src,
            dst_ref=dst,
            send_sem=send_sem.at[k],
            recv_sem=recv_sem.at[k],
            device_id=(row + dr, col + dc),
            device_id_type=pl.DeviceIdType.MESH,
        )

    def copy_in(k):
        _, _, _, src, dst = links[k]
        return pltpu.make_async_remote_copy(
            src_ref=src,
            dst_ref=dst,
            send_sem=send_sem.at[k],
            recv_sem=recv_sem.at[k],
            device_id=(row, col),
            device_id_type=pl.DeviceIdType.MESH,
        )

    go = [link[0] for link in links]

    def greet(k):
        pl.semaphore_signal(
            barrier,
            inc=1,
            device_id=(row + links[k][1], col + links[k][2]),
            device_id_type=pl.DeviceIdType.MESH,
        )

    each(go, greet)
    for k in range(8):
        ref = [from_row.at[0], from_row.at[1], strip_in.at[0], strip_in.at[1]] + [
            corner.at[c] for c in range(4)
        ]

        @pl.when(jnp.logical_not(come[k]))
        def _(ref=ref[k]):
            ref[...] = jnp.zeros(ref.shape, jnp.float32)

    for j in range(cols // LANES):
        part = slice(j * LANES, (j + 1) * LANES)

        def body(g, _, j=j, part=part):
            base = g * 32
            got = [returned[pl.ds(position[j * rows + base + u], 1), :] for u in range(32)]
            for u in range(32):
                sorted_rows[pl.ds(j * rows + base + u, 1), :] = got[u]
            return 0

        lax.fori_loop(0, rows // 32, body, 0)
        s_ref[0:rows, part] = (
            store_rate * (head[:, part] * land[:, part].astype(jnp.float32))
            + recharge_gain * sorted_rows[j * rows : (j + 1) * rows, :]
        )
    strip_out[0] = jnp.transpose(s_ref[0:rows, 0:LANES])[0:8]
    strip_out[1] = jnp.transpose(s_ref[0:rows, east:cols])[LANES - 8 : LANES]

    def count(flags):
        return functools.reduce(lambda x, y: x + y, [f.astype(jnp.int32) for f in flags])

    pl.semaphore_wait(barrier, count(go))
    each(go, lambda k: copy(k).start())

    def place(dst, centre, edge, side):
        dst[0:rows, 0:cols] = centre
        dst[rows:high, 0:cols] = edge
        dst[:, cols:wide] = side

    place(t_ref, mid[0], mid_r[0], mid_c[0])
    place(a, mid[1], mid_r[1], mid_c[1])
    place(b, mid[2], mid_r[2], mid_c[2])
    for g in range(wide // LANES):
        part = slice(g * LANES, (g + 1) * LANES)
        lo = slice((g - 1) % (wide // LANES) * LANES, (g - 1) % (wide // LANES) * LANES + LANES)
        hi = slice((g + 1) % (wide // LANES) * LANES, (g + 1) % (wide // LANES) * LANES + LANES)
        lane = lax.broadcasted_iota(jnp.int32, (high, LANES), 1)
        t = t_ref[:, part]
        tu = 0.5 * (t + pltpu.roll(t, 1, 0))
        td = 0.5 * (t + pltpu.roll(t, high - 1, 0))
        tl = jnp.where(lane == 0, pltpu.roll(t_ref[:, lo], 1, 1), pltpu.roll(t, 1, 1))
        tr = jnp.where(
            lane == LANES - 1,
            pltpu.roll(t_ref[:, hi], LANES - 1, 1),
            pltpu.roll(t, LANES - 1, 1),
        )
        lf = 0.5 * (t + tl)
        rt = 0.5 * (t + tr)
        inv = b[:, part] / (store_rate + (tu + td + lf + rt))
        fu[:, part] = tu * inv
        fd[:, part] = td * inv
        fl[:, part] = lf * inv
        fr[:, part] = rt * inv
        b[:, part] = inv

    each(go, lambda k: copy(k).wait_send())
    each(come, lambda k: copy_in(k).wait_recv())

    first = lax.broadcasted_iota(jnp.int32, (8, LANES), 0) < 4
    near = lax.broadcasted_iota(jnp.int32, (8, LANES), 1) < LANES // 2
    for j in range(cols // LANES):
        part = slice(j * LANES, (j + 1) * LANES)
        s_ref[rows:high, part] = jnp.where(first, from_row[0, :, part], from_row[1, :, part])
    s_ref[rows:high, cols:wide] = jnp.where(
        first,
        jnp.where(near, corner[0], corner[1]),
        jnp.where(near, corner[2], corner[3]),
    )
    s_ref[0:rows, cols:wide] = jnp.transpose(
        jnp.concatenate(
            [strip_in[0], jnp.zeros((LANES - 16, rows), jnp.float32), strip_in[1]], axis=0
        )
    )
    for g in range(wide // LANES):
        part = slice(g * LANES, (g + 1) * LANES)
        s_ref[:, part] = s_ref[:, part] * b[:, part]
    now, later = a, b
    for sweep in range(SWEEPS):
        last = sweep == SWEEPS - 1
        for g in range(wide // LANES):
            if last and g * LANES >= cols:
                continue
            part = slice(g * LANES, (g + 1) * LANES)
            lo = (g - 1) % (wide // LANES) * LANES
            hi = (g + 1) % (wide // LANES) * LANES
            lane = lax.broadcasted_iota(jnp.int32, (high, LANES), 1)
            x = now[:, part]
            xl = jnp.where(
                lane == 0, pltpu.roll(now[:, lo : lo + LANES], 1, 1), pltpu.roll(x, 1, 1)
            )
            xr = jnp.where(
                lane == LANES - 1,
                pltpu.roll(now[:, hi : hi + LANES], LANES - 1, 1),
                pltpu.roll(x, LANES - 1, 1),
            )
            y = s_ref[:, part] + fu[:, part] * pltpu.roll(x, 1, 0)
            y = y + fd[:, part] * pltpu.roll(x, high - 1, 0)
            y = y + (fl[:, part] * xl + fr[:, part] * xr)
            if last:
                out[:, part] = y[0:rows]
            else:
                later[:, part] = y
        now, later = later, now


def halos(block):
    rows, cols = block.shape[-2:]

    def shift(x, axis, step):
        count = lax.axis_size(axis)
        if step > 0:
            pairs = [(i, i + 1) for i in range(count - 1)]
        else:
            pairs = [(i + 1, i) for i in range(count - 1)]
        return lax.ppermute(x, axis, pairs)

    above = shift(block[..., rows - SWEEPS :, :], "row", 1)
    below = shift(block[..., :SWEEPS, :], "row", -1)
    edge = jnp.concatenate([below, above], axis=-2)
    first = jnp.concatenate([block[..., :SWEEPS], edge[..., :SWEEPS]], axis=-2)
    final = jnp.concatenate([block[..., cols - SWEEPS :], edge[..., cols - SWEEPS :]], axis=-2)
    right = shift(first, "col", -1)
    left = shift(final, "col", 1)
    gap = jnp.zeros(right.shape[:-1] + (LANES - 2 * SWEEPS,), jnp.float32)
    side = jnp.concatenate([right, gap, left], axis=-1)
    return edge, side


def on_device(precip, head, trans_coef, land, dest, moisture, ksat):
    tile_rows, tile_cols = precip.shape
    peers = lax.axis_size("row") * lax.axis_size("col")
    owned, layers, _ = moisture.shape
    blocks = tile_rows * tile_cols // LANES
    per_peer = (2 * blocks + peers - 1) // peers
    places = peers * per_peer

    target = dest.T.reshape(blocks)
    owner = target // owned
    slot = target - owner * owned
    one_hot = owner[:, None] == jnp.arange(peers, dtype=jnp.int32)[None, :]
    order = jnp.arange(blocks, dtype=jnp.int32)
    earlier = (order[None, :] < order[:, None]).astype(jnp.bfloat16)
    counts = jnp.dot(earlier, one_hot.astype(jnp.bfloat16), preferred_element_type=jnp.float32)
    rank = jnp.sum(jnp.where(one_hot, counts, 0.0), axis=1).astype(jnp.int32)
    position = owner * per_peer + rank
    at_rank = rank[:, None] == jnp.arange(per_peer, dtype=jnp.int32)[None, :]
    values = jnp.concatenate(
        [
            jnp.where(at_rank, order.astype(jnp.float32)[:, None], 0.0),
            jnp.where(at_rank, (slot - owned).astype(jnp.float32)[:, None], 0.0),
        ],
        axis=1,
    )
    table = lax.dot_general(
        one_hot.astype(jnp.float32),
        values,
        (((0,), (0,)), ((), ())),
        precision=lax.Precision.HIGHEST,
        preferred_element_type=jnp.float32,
    )
    slot_source = table[:, :per_peer].astype(jnp.int32).reshape(places)
    labels = jnp.pad(table[:, per_peer:] + float(owned), ((0, 0), (0, LANES - per_peer)))

    depth = 2 * per_peer + 8
    outgoing = pl.pallas_call(
        functools.partial(pack_kernel, peers, per_peer),
        out_shape=f32(peers, depth, LANES),
        in_specs=[SM, VM, VM, VM, VM],
        out_specs=VM,
        scratch_shapes=[pltpu.VMEM((blocks, LANES), jnp.float32)] * 2,
    )(slot_source, labels, precip, head, land)
    arrived = lax.all_to_all(outgoing, ("row", "col"), split_axis=0, concat_axis=0, tiled=True)

    land_share = land.astype(jnp.float32)
    transmit = trans_coef * (1.0 + 0.5 * jnp.tanh(head))
    fixed = jnp.stack([transmit, head * land_share, land_share])
    fixed_r, fixed_c = halos(fixed)

    step = 128
    flat = moisture.reshape(owned * layers, LANES)
    layered = pl.BlockSpec((layers, step, LANES), lambda i: (0, i, 0))
    single = pl.BlockSpec((step, LANES), lambda i: (i, 0))
    natural = pl.BlockSpec((step * layers, LANES), lambda i: (i, 0))
    s0, sx, sy, rec0, rec_x, rec_y = pl.pallas_call(
        functools.partial(factor_kernel, layers, 32),
        grid=(owned // step,),
        out_shape=[f32(layers, owned, LANES)] * 3 + [f32(owned, LANES)] * 3,
        in_specs=[natural, single],
        out_specs=[layered] * 3 + [single] * 3,
        cost_estimate=pl.CostEstimate(
            flops=50 * owned * layers * LANES,
            bytes_accessed=16 * owned * layers * LANES,
            transcendentals=owned * layers * LANES,
        ),
    )(flat, ksat)

    arrived, fixed_r, fixed_c = lax.optimization_barrier((arrived, fixed_r, fixed_c))
    slots = arrived[:, 2 * per_peer, :per_peer].astype(jnp.int32).reshape(places)
    answer, infil, sig = pl.pallas_call(
        functools.partial(owner_kernel, peers, per_peer),
        out_shape=[f32(peers, per_peer, LANES), f32(owned, LANES), f32(owned, LANES)],
        in_specs=[SM, VM, VM, VM, VM],
        out_specs=[VM] * 3,
        scratch_shapes=[pltpu.VMEM((owned + 8, LANES), jnp.float32)] * 3,
    )(slots, arrived, rec0, rec_x, rec_y)
    returned = lax.all_to_all(answer, ("row", "col"), split_axis=0, concat_axis=0, tiled=True)

    saturation = pl.pallas_call(
        functools.partial(saturation_kernel, layers),
        grid=(owned // step,),
        out_shape=f32(owned * layers, LANES),
        in_specs=[layered] * 3 + [single] * 2,
        out_specs=natural,
        cost_estimate=pl.CostEstimate(
            flops=4 * owned * layers * LANES,
            bytes_accessed=16 * owned * layers * LANES,
            transcendentals=0,
        ),
    )(s0, sx, sy, infil, sig).reshape(owned, layers, LANES)

    high, wide = tile_rows + 2 * SWEEPS, tile_cols + LANES
    surface = pl.pallas_call(
        relax_kernel,
        out_shape=f32(tile_rows, tile_cols),
        in_specs=[SM] + [VM] * 6,
        out_specs=VM,
        scratch_shapes=[pltpu.VMEM((high, wide), jnp.float32)] * 8
        + [
            pltpu.VMEM((blocks, LANES), jnp.float32),
            pltpu.VMEM((2, 8, tile_rows), jnp.float32),
            pltpu.VMEM((2, 8, tile_cols), jnp.float32),
            pltpu.VMEM((2, 8, tile_rows), jnp.float32),
            pltpu.VMEM((4, 8, LANES), jnp.float32),
            pltpu.SemaphoreType.DMA((8,)),
            pltpu.SemaphoreType.DMA((8,)),
        ],
        compiler_params=pltpu.CompilerParams(collective_id=1, has_side_effects=True),
    )(position, returned.reshape(places, LANES), head, land, fixed, fixed_r, fixed_c)
    return (saturation, surface)


def solution(mesh):
    tile = P("row", "col")
    placed = (
        tile,
        tile,
        tile,
        tile,
        tile,
        P(("row", "col"), None, None),
        P(("row", "col"), None),
    )
    return jax.shard_map(
        on_device,
        mesh=mesh,
        in_specs=placed,
        out_specs=(P(("row", "col"), None, None), P("row", "col")),
        check_vma=False,
    )
```

```python
import functools
import math

import jax
import jax.numpy as jnp
from jax import lax
from jax.experimental import pallas as pl
from jax.experimental.pallas import tpu as pltpu
from jax.sharding import PartitionSpec as P

SWEEPS = 4
LANES = 128

layer_depth = 0.1
step_ratio = 0.1
residual_water = 0.05
pore_range = 0.4
diff_length = 0.5
couple_rate = 0.05
recharge_gain = 20.0
store_rate = 0.2

VM = pl.BlockSpec(memory_space=pltpu.VMEM)
SM = pl.BlockSpec(memory_space=pltpu.SMEM)


def f32(*shape):
    return jax.ShapeDtypeStruct(shape, jnp.float32)


def pack_spread_kernel(depth, extra, src, labels, precip, head, land, out, infil, heads):
    rows, cols = precip.shape
    peers = out.shape[0]
    for j in range(cols // LANES):
        part = pl.ds(j * LANES, LANES)
        infil[pl.ds(j * rows, rows), :] = precip[:, part] * land[:, part].astype(jnp.float32)
        heads[pl.ds(j * rows, rows), :] = head[:, part]

    def body(p, _):
        for r in range(depth - 1):
            block = src[p * depth + r]
            out[p, pl.ds(r, 1), :] = infil[pl.ds(block, 1), :]
            out[p, pl.ds(depth + r, 1), :] = heads[pl.ds(block, 1), :]
        out[p, pl.ds(depth - 1, 1), :] = labels[0, pl.ds(p, 1), :]
        out[p, pl.ds(2 * depth - 1, 1), :] = labels[1, pl.ds(p, 1), :]
        return 0

    lax.fori_loop(0, peers, body, 0)


def exchange_kernel(
    cap, extra, hop, arrived, rec0, rec_x, rec_y, returned, slots, slot2, arr2, fits,
    mid_out, ans, ans2, arr4, out5, arr5, g0, gx, gy, src_v, ret_v,
    slots_s, slot2_s, src_s, ret_s, move, send2, recv2, send3, recv3, send4, recv4, send5, recv5, own,
):
    peers = arrived.shape[0]
    depth = arrived.shape[1] // 2
    direct = depth - 1 - extra
    owned = rec0.shape[0]
    n_col = lax.axis_size("col")
    me = lax.axis_index("row") * n_col + lax.axis_index("col")
    barrier = pltpu.get_barrier_semaphore()

    def where_is(k):
        p = lax.rem(me + k, peers)
        return p, (p // n_col, lax.rem(p, n_col))

    def greet(k, _):
        pl.semaphore_signal(
            barrier, inc=1, device_id=where_is(k)[1], device_id_type=pl.DeviceIdType.MESH
        )
        return 0

    lax.fori_loop(1, peers, greet, 0)

    shape = (peers, LANES)
    lane = lax.broadcasted_iota(jnp.int32, shape, 1)
    sub = lax.broadcasted_iota(jnp.int32, shape, 0)
    lab = arrived[:, depth - 1, :]
    count = arrived[:, 2 * depth - 1, :]
    over = jnp.maximum(count - direct, 0.0)
    tri = lax.broadcasted_iota(jnp.int32, (LANES, LANES), 0) < lax.broadcasted_iota(
        jnp.int32, (LANES, LANES), 1
    )
    base = jnp.dot(
        over, tri.astype(jnp.float32), precision=lax.Precision.HIGHEST,
        preferred_element_type=jnp.float32,
    )
    total = extra * peers
    before = (
        lax.broadcasted_iota(jnp.int32, (total, total), 1)
        < lax.broadcasted_iota(jnp.int32, (total, total), 0)
    ).astype(jnp.float32)

    def number(m):
        gap = m - sub
        return jnp.where(gap < 0, gap + peers, gap).astype(jnp.float32)

    def holds(j, first, many, t):
        j = j + float(t * peers)
        return jnp.where((first <= j) & (j < first + many), 1.0, 0.0)

    def prefix(v):
        return jnp.dot(before, v, preferred_element_type=jnp.float32)

    flane = lane.astype(jnp.float32)
    code = sub.astype(jnp.float32) * 8.0
    via = jnp.concatenate([holds(number(me), base, over, t) for t in range(extra)], axis=0)
    rank = prefix(via)
    codes = jnp.concatenate([code + float(t) for t in range(extra)], axis=0)
    lanes = jnp.concatenate([flane] * extra, axis=0)
    back = jnp.sum(via * (lanes * hop + rank), axis=1, keepdims=True)
    ret_v[...] = jnp.broadcast_to(back, (total, LANES)).astype(jnp.int32)
    picks = [
        jnp.sum(jnp.where(rank == float(e), via * codes, 0.0), axis=0, keepdims=True)
        for e in range(hop)
    ]
    src_v[...] = jnp.concatenate(picks + [jnp.zeros((8 - hop, LANES), jnp.float32)], axis=0).astype(
        jnp.int32
    )
    mine = jnp.where(lane == me, 1.0, 0.0)
    first = jnp.sum(base * mine, axis=1, keepdims=True)
    many = jnp.sum(over * mine, axis=1, keepdims=True)
    inside = jnp.where(lane < peers, 1.0, 0.0)
    step = number(lane)
    took = [holds(step, first, many, t) * inside for t in range(extra)]
    value = []
    for t in range(extra):
        at = step + float(t * peers) - first
        v = jnp.zeros(shape, jnp.float32)
        for r in range(cap - direct):
            v = jnp.where(at == float(r), lab[:, direct + r : direct + r + 1] - float(owned), v)
        value.append(v)
    took = jnp.concatenate(took, axis=0)
    rank = prefix(took)
    value = jnp.concatenate(value, axis=0)
    picks = [
        jnp.sum(jnp.where(rank == float(e), took * value, 0.0), axis=0, keepdims=True)
        for e in range(hop)
    ]
    slot2[...] = (
        jnp.concatenate(picks + [jnp.zeros((8 - hop, LANES), jnp.float32)], axis=0) + float(owned)
    ).astype(jnp.int32)
    slots[...] = lab.astype(jnp.int32)
    g0[...] = jnp.zeros(g0.shape, jnp.float32)
    gx[...] = jnp.zeros(gx.shape, jnp.float32)
    gy[...] = jnp.zeros(gy.shape, jnp.float32)
    moves = [
        pltpu.make_async_copy(src_v, src_s, move.at[0]),
        pltpu.make_async_copy(slots, slots_s, move.at[1]),
        pltpu.make_async_copy(slot2, slot2_s, move.at[2]),
        pltpu.make_async_copy(ret_v, ret_s, move.at[3]),
    ]
    for m in moves:
        m.start()
    for m in moves:
        m.wait()

    def exchange(src, dst, send, recv, self_sem):
        def copy(k):
            p, place = where_is(k)
            return pltpu.make_async_remote_copy(
                src_ref=src.at[p],
                dst_ref=dst.at[me],
                send_sem=send.at[k],
                recv_sem=recv.at[k],
                device_id=place,
                device_id_type=pl.DeviceIdType.MESH,
            )

        here = pltpu.make_async_copy(src.at[me], dst.at[me], self_sem)

        def start(low, high):
            def body(k, _):
                copy(k).start()
                return 0

            lax.fori_loop(low, high, body, 0)

        def wait():
            def body(k, _):
                copy(k).wait()
                return 0

            lax.fori_loop(1, peers, body, 0)
            here.wait()

        return here, start, wait

    def pass_on(d, _):
        for e in range(hop):
            q = src_s[e, d]
            s = jnp.clip(q // 8, 0, peers - 1)
            t = jnp.clip(q - s * 8, 0, extra - 1)
            mid_out[d, pl.ds(e, 1), :] = arrived[s, pl.ds(direct + t, 1), :]
            mid_out[d, pl.ds(hop + e, 1), :] = arrived[s, pl.ds(depth + direct + t, 1), :]
        return 0

    lax.fori_loop(0, peers, pass_on, 0)
    pl.semaphore_wait(barrier, peers - 1)
    here2, start2, wait2 = exchange(mid_out, arr2, send2, recv2, own.at[0])
    here2.start()
    start2(1, peers)

    def answer(p, _):
        for r in range(direct):
            slot = jnp.clip(slots_s[p, r], 0, owned - 1)
            g0[pl.ds(r, 1), :] = rec0[pl.ds(slot, 1), :]
            gx[pl.ds(r, 1), :] = rec_x[pl.ds(slot, 1), :]
            gy[pl.ds(r, 1), :] = rec_y[pl.ds(slot, 1), :]
        ans[p] = (
            g0[...]
            + arrived[p, 0:depth, :] * gx[...]
            + jax.nn.sigmoid(arrived[p, depth : 2 * depth, :]) * gy[...]
        )
        return 0

    lax.fori_loop(0, peers, answer, 0)
    here3, start3, wait3 = exchange(ans, returned.at[pl.ds(0, peers)], send3, recv3, own.at[1])
    here4, start4, wait4 = exchange(ans2, arr4, send4, recv4, own.at[2])
    here5, start5, wait5 = exchange(out5, arr5, send5, recv5, own.at[3])
    wait2()

    def answer2(m, _):
        for e in range(hop):
            slot = jnp.clip(slot2_s[e, m], 0, owned - 1)
            ans2[m, pl.ds(e, 1), :] = (
                rec0[pl.ds(slot, 1), :]
                + arr2[m, pl.ds(e, 1), :] * rec_x[pl.ds(slot, 1), :]
                + jax.nn.sigmoid(arr2[m, pl.ds(hop + e, 1), :]) * rec_y[pl.ds(slot, 1), :]
            )
        return 0

    lax.fori_loop(0, peers, answer2, 0)
    here4.start()
    start4(1, peers)
    early = peers // 4
    here3.start()
    start3(1, early)
    wait4()

    def hand_back(s, _):
        for t in range(extra):
            at = jnp.clip(ret_s[t * peers + s, 0], 0, peers * hop - 1)
            d = at // hop
            out5[s, pl.ds(t, 1), :] = arr4[d, pl.ds(at - d * hop, 1), :]
        return 0

    lax.fori_loop(0, peers, hand_back, 0)
    here5.start()
    start5(1, peers)
    start3(early, peers)

    def widest(m, most):
        n = number(m)
        seen = functools.reduce(lambda x, y: x + y, [holds(n, base, over, t) for t in range(extra)])
        return jnp.maximum(most, jnp.sum(seen, axis=0, keepdims=True))

    most = lax.fori_loop(0, peers, widest, jnp.zeros((1, LANES), jnp.float32))
    spread = jnp.max(jnp.sum(over, axis=1, keepdims=True), axis=0, keepdims=True)
    bad = jnp.maximum(
        jnp.where(jnp.max(most, axis=1, keepdims=True) > float(hop), 1.0, 0.0),
        jnp.where(spread > float(total), 1.0, 0.0),
    )
    fits[...] = jnp.broadcast_to(1.0 - bad, fits.shape)
    wait5()
    for i in range(total):
        returned[peers + i // depth, pl.ds(i % depth, 1), :] = arr5[
            i // extra, pl.ds(i % extra, 1), :
        ]
    wait3()


def pack_kernel(peers, per_peer, src, labels, precip, head, land, out, infil, heads):
    rows, cols = precip.shape
    for j in range(cols // LANES):
        part = pl.ds(j * LANES, LANES)
        infil[pl.ds(j * rows, rows), :] = precip[:, part] * land[:, part].astype(jnp.float32)
        heads[pl.ds(j * rows, rows), :] = head[:, part]

    def body(p, _):
        for r in range(per_peer):
            block = src[p * per_peer + r]
            out[p, pl.ds(r, 1), :] = infil[pl.ds(block, 1), :]
            out[p, pl.ds(per_peer + r, 1), :] = heads[pl.ds(block, 1), :]
        out[p, pl.ds(2 * per_peer, 8), :] = jnp.broadcast_to(labels[pl.ds(p, 1), :], (8, LANES))
        return 0

    lax.fori_loop(0, peers, body, 0)


def owner_kernel(
    peers, per_peer, slots, arrived, rec0, rec_x, rec_y, answer, infil, sig, own_i, own_h, rec
):
    owned = rec0.shape[0]

    def scatter(p, _):
        for r in range(per_peer):
            slot = slots[p * per_peer + r]
            own_i[pl.ds(slot, 1), :] = arrived[p, pl.ds(r, 1), :]
            own_h[pl.ds(slot, 1), :] = arrived[p, pl.ds(per_peer + r, 1), :]
        return 0

    lax.fori_loop(0, peers, scatter, 0)
    rec[pl.ds(owned, 8), :] = jnp.zeros((8, LANES), jnp.float32)

    def combine(g, _):
        part = pl.ds(g * 64, 64)
        inf = own_i[part, :]
        sg = jax.nn.sigmoid(own_h[part, :])
        infil[part, :] = inf
        sig[part, :] = sg
        rec[part, :] = rec0[part, :] + inf * rec_x[part, :] + sg * rec_y[part, :]
        return 0

    lax.fori_loop(0, owned // 64, combine, 0)

    def gather(p, _):
        for r in range(per_peer):
            slot = slots[p * per_peer + r]
            answer[p, pl.ds(r, 1), :] = rec[pl.ds(slot, 1), :]
        return 0

    lax.fori_loop(0, peers, gather, 0)


def factor_kernel(layers, group, moist, ksat, s0, sx, sy, rec0, rec_x, rec_y):
    count = ksat.shape[0]

    def body(step, _):
        base_row = step * group
        rows = pl.ds(pl.multiple_of(base_row, group), group)
        ks = ksat[rows, :]
        ratios, reds, xs = [], [], []
        before = None
        for k in range(layers):
            m = moist[pl.ds(base_row * layers + k, group, stride=layers), :]
            w = (m - residual_water) * (1.0 / pore_range)
            s = ks * math.exp(-(k + 0.5) * layer_depth)
            sw2 = s * (w * w)
            hs = sw2 * (1.5 / pore_range)
            d = s * (0.2 * diff_length / (2.0 * layer_depth)) + sw2 * (
                diff_length / (2.0 * layer_depth)
            )
            hc = 0.5 * (sw2 * w)
            cur = (m, hs, d, hc)
            if before is None:
                before = cur
                g_up = q_up = nsub = None
                continue
            m0, hs0, d0, hc0 = before
            g = d0 + d
            q = (hc0 + hc) - g * (m - m0)
            if g_up is None:
                pivot = step_ratio + g + hs0
                inv = 1.0 / pivot
                reds.append(-q * inv)
                xs.append(inv)
            else:
                pivot = step_ratio + g_up + g - nsub * ratios[-1]
                inv = 1.0 / pivot
                reds.append(((q_up - q) + nsub * reds[-1]) * inv)
                xs.append(nsub * inv * xs[-1])
            ratios.append((g - hs) * inv)
            nsub = hs0 + g
            g_up, q_up = g, q
            before = cur
        m, hs, d, hc = before
        bottom = 2.0 * hc + couple_rate * (m - residual_water)
        pivot = step_ratio + g_up + hs + couple_rate - nsub * ratios[-1]
        inv = 1.0 / pivot
        change = ((q_up - bottom) + nsub * reds[-1]) * inv
        cx = nsub * inv * xs[-1]
        cy = (couple_rate * pore_range) * inv
        gain = 2.0 * hs + couple_rate
        rec0[rows, :] = bottom + gain * change
        rec_x[rows, :] = gain * cx
        rec_y[rows, :] = gain * cy - couple_rate * pore_range
        unit = 1.0 / pore_range
        for k in range(layers - 1, -1, -1):
            if k < layers - 1:
                change = reds[k] + ratios[k] * change
                cx = xs[k] + ratios[k] * cx
                cy = ratios[k] * cy
            m = moist[pl.ds(base_row * layers + k, group, stride=layers), :]
            s0[k, rows, :] = (m + change - residual_water) * unit
            sx[k, rows, :] = cx * unit
            sy[k, rows, :] = cy * unit
        return 0

    lax.fori_loop(0, count // group, body, 0)


def saturation_kernel(layers, s0, sx, sy, infil, sig, out):
    count = infil.shape[0]
    group = 32

    def body(step, _):
        rows = pl.ds(pl.multiple_of(step * group, group), group)
        inf = infil[rows, :]
        sg = sig[rows, :]
        for k in range(layers):
            out[pl.ds(step * group * layers + k, group, stride=layers), :] = (
                s0[k, rows, :] + inf * sx[k, rows, :] + sg * sy[k, rows, :]
            )
        return 0

    lax.fori_loop(0, count // group, body, 0)


def spread_saturation_kernel(
    layers, extra, hop, slots, slot2, arrived, arr2, s0, sx, sy, out, own_i, own_h
):
    count = s0.shape[1]
    group = 32
    peers = arrived.shape[0]
    depth = arrived.shape[1] // 2
    direct = depth - 1 - extra
    start = pl.program_id(0) * count

    @pl.when(pl.program_id(0) == 0)
    def _():
        def scatter(p, _):
            for r in range(direct):
                slot = slots[p, r]
                own_i[pl.ds(slot, 1), :] = arrived[p, pl.ds(r, 1), :]
                own_h[pl.ds(slot, 1), :] = arrived[p, pl.ds(depth + r, 1), :]
            for e in range(hop):
                slot = slot2[e, p]
                own_i[pl.ds(slot, 1), :] = arr2[p, pl.ds(e, 1), :]
                own_h[pl.ds(slot, 1), :] = arr2[p, pl.ds(hop + e, 1), :]
            return 0

        lax.fori_loop(0, peers, scatter, 0)

    def body(step, _):
        base = pl.multiple_of(step * group, group)
        rows = pl.ds(base, group)
        from_all = pl.ds(pl.multiple_of(start + base, group), group)
        inf = own_i[from_all, :]
        sg = jax.nn.sigmoid(own_h[from_all, :])
        for k in range(layers):
            out[pl.ds(step * group * layers + k, group, stride=layers), :] = (
                s0[k, rows, :] + inf * sx[k, rows, :] + sg * sy[k, rows, :]
            )
        return 0

    lax.fori_loop(0, count // group, body, 0)


def relax_kernel(
    position, returned, head, land, mid, mid_r, mid_c, out,
    t_ref, s_ref, fu, fd, fl, fr, a, b, sorted_rows, strip_out, from_row, strip_in, corner, send_sem, recv_sem,
):
    rows, cols = head.shape
    high, wide = t_ref.shape
    row, col = lax.axis_index("row"), lax.axis_index("col")
    n_row, n_col = lax.axis_size("row"), lax.axis_size("col")
    up, down = row > 0, row < n_row - 1
    left, right = col > 0, col < n_col - 1
    east = cols - LANES
    south = rows - 8
    links = [
        (up, -1, 0, s_ref.at[pl.ds(0, 8), pl.ds(0, cols)], from_row.at[0]),
        (down, 1, 0, s_ref.at[pl.ds(south, 8), pl.ds(0, cols)], from_row.at[1]),
        (left, 0, -1, strip_out.at[0], strip_in.at[0]),
        (right, 0, 1, strip_out.at[1], strip_in.at[1]),
        (up & left, -1, -1, s_ref.at[pl.ds(0, 8), pl.ds(0, LANES)], corner.at[0]),
        (up & right, -1, 1, s_ref.at[pl.ds(0, 8), pl.ds(east, LANES)], corner.at[1]),
        (down & left, 1, -1, s_ref.at[pl.ds(south, 8), pl.ds(0, LANES)], corner.at[2]),
        (down & right, 1, 1, s_ref.at[pl.ds(south, 8), pl.ds(east, LANES)], corner.at[3]),
    ]
    come = [down, up, right, left, down & right, down & left, up & right, up & left]
    barrier = pltpu.get_barrier_semaphore()

    def each(flags, act):
        for k, flag in enumerate(flags):
            pl.when(flag)(functools.partial(act, k))

    def copy(k):
        _, dr, dc, src, dst = links[k]
        return pltpu.make_async_remote_copy(
            src_ref=src,
            dst_ref=dst,
            send_sem=send_sem.at[k],
            recv_sem=recv_sem.at[k],
            device_id=(row + dr, col + dc),
            device_id_type=pl.DeviceIdType.MESH,
        )

    def copy_in(k):
        _, _, _, src, dst = links[k]
        return pltpu.make_async_remote_copy(
            src_ref=src,
            dst_ref=dst,
            send_sem=send_sem.at[k],
            recv_sem=recv_sem.at[k],
            device_id=(row, col),
            device_id_type=pl.DeviceIdType.MESH,
        )

    go = [link[0] for link in links]

    def greet(k):
        pl.semaphore_signal(
            barrier,
            inc=1,
            device_id=(row + links[k][1], col + links[k][2]),
            device_id_type=pl.DeviceIdType.MESH,
        )

    each(go, greet)
    for k in range(8):
        ref = [from_row.at[0], from_row.at[1], strip_in.at[0], strip_in.at[1]] + [
            corner.at[c] for c in range(4)
        ]

        @pl.when(jnp.logical_not(come[k]))
        def _(ref=ref[k]):
            ref[...] = jnp.zeros(ref.shape, jnp.float32)

    for j in range(cols // LANES):
        part = slice(j * LANES, (j + 1) * LANES)

        def body(g, _, j=j, part=part):
            base = g * 32
            got = [returned[pl.ds(position[j * rows + base + u], 1), :] for u in range(32)]
            for u in range(32):
                sorted_rows[pl.ds(j * rows + base + u, 1), :] = got[u]
            return 0

        lax.fori_loop(0, rows // 32, body, 0)
        s_ref[0:rows, part] = (
            store_rate * (head[:, part] * land[:, part].astype(jnp.float32))
            + recharge_gain * sorted_rows[j * rows : (j + 1) * rows, :]
        )
    strip_out[0] = jnp.transpose(s_ref[0:rows, 0:LANES])[0:8]
    strip_out[1] = jnp.transpose(s_ref[0:rows, east:cols])[LANES - 8 : LANES]

    def count(flags):
        return functools.reduce(lambda x, y: x + y, [f.astype(jnp.int32) for f in flags])

    pl.semaphore_wait(barrier, count(go))
    each(go, lambda k: copy(k).start())

    def place(dst, centre, edge, side):
        dst[0:rows, 0:cols] = centre
        dst[rows:high, 0:cols] = edge
        dst[:, cols:wide] = side

    place(t_ref, mid[0], mid_r[0], mid_c[0])
    place(a, mid[1], mid_r[1], mid_c[1])
    place(b, mid[2], mid_r[2], mid_c[2])
    for g in range(wide // LANES):
        part = slice(g * LANES, (g + 1) * LANES)
        lo = slice((g - 1) % (wide // LANES) * LANES, (g - 1) % (wide // LANES) * LANES + LANES)
        hi = slice((g + 1) % (wide // LANES) * LANES, (g + 1) % (wide // LANES) * LANES + LANES)
        lane = lax.broadcasted_iota(jnp.int32, (high, LANES), 1)
        t = t_ref[:, part]
        tu = 0.5 * (t + pltpu.roll(t, 1, 0))
        td = 0.5 * (t + pltpu.roll(t, high - 1, 0))
        tl = jnp.where(lane == 0, pltpu.roll(t_ref[:, lo], 1, 1), pltpu.roll(t, 1, 1))
        tr = jnp.where(
            lane == LANES - 1,
            pltpu.roll(t_ref[:, hi], LANES - 1, 1),
            pltpu.roll(t, LANES - 1, 1),
        )
        lf = 0.5 * (t + tl)
        rt = 0.5 * (t + tr)
        inv = b[:, part] / (store_rate + (tu + td + lf + rt))
        fu[:, part] = tu * inv
        fd[:, part] = td * inv
        fl[:, part] = lf * inv
        fr[:, part] = rt * inv
        b[:, part] = inv

    each(go, lambda k: copy(k).wait_send())
    each(come, lambda k: copy_in(k).wait_recv())

    first = lax.broadcasted_iota(jnp.int32, (8, LANES), 0) < 4
    near = lax.broadcasted_iota(jnp.int32, (8, LANES), 1) < LANES // 2
    for j in range(cols // LANES):
        part = slice(j * LANES, (j + 1) * LANES)
        s_ref[rows:high, part] = jnp.where(first, from_row[0, :, part], from_row[1, :, part])
    s_ref[rows:high, cols:wide] = jnp.where(
        first,
        jnp.where(near, corner[0], corner[1]),
        jnp.where(near, corner[2], corner[3]),
    )
    s_ref[0:rows, cols:wide] = jnp.transpose(
        jnp.concatenate(
            [strip_in[0], jnp.zeros((LANES - 16, rows), jnp.float32), strip_in[1]], axis=0
        )
    )
    for g in range(wide // LANES):
        part = slice(g * LANES, (g + 1) * LANES)
        s_ref[:, part] = s_ref[:, part] * b[:, part]
    now, later = a, b
    for sweep in range(SWEEPS):
        last = sweep == SWEEPS - 1
        for g in range(wide // LANES):
            if last and g * LANES >= cols:
                continue
            part = slice(g * LANES, (g + 1) * LANES)
            lo = (g - 1) % (wide // LANES) * LANES
            hi = (g + 1) % (wide // LANES) * LANES
            lane = lax.broadcasted_iota(jnp.int32, (high, LANES), 1)
            x = now[:, part]
            xl = jnp.where(
                lane == 0, pltpu.roll(now[:, lo : lo + LANES], 1, 1), pltpu.roll(x, 1, 1)
            )
            xr = jnp.where(
                lane == LANES - 1,
                pltpu.roll(now[:, hi : hi + LANES], LANES - 1, 1),
                pltpu.roll(x, LANES - 1, 1),
            )
            y = s_ref[:, part] + fu[:, part] * pltpu.roll(x, 1, 0)
            y = y + fd[:, part] * pltpu.roll(x, high - 1, 0)
            y = y + (fl[:, part] * xl + fr[:, part] * xr)
            if last:
                out[:, part] = y[0:rows]
            else:
                later[:, part] = y
        now, later = later, now


def halos(block):
    rows, cols = block.shape[-2:]

    def shift(x, axis, step):
        count = lax.axis_size(axis)
        if step > 0:
            pairs = [(i, i + 1) for i in range(count - 1)]
        else:
            pairs = [(i + 1, i) for i in range(count - 1)]
        return lax.ppermute(x, axis, pairs)

    above = shift(block[..., rows - SWEEPS :, :], "row", 1)
    below = shift(block[..., :SWEEPS, :], "row", -1)
    edge = jnp.concatenate([below, above], axis=-2)
    first = jnp.concatenate([block[..., :SWEEPS], edge[..., :SWEEPS]], axis=-2)
    final = jnp.concatenate([block[..., cols - SWEEPS :], edge[..., cols - SWEEPS :]], axis=-2)
    right = shift(first, "col", -1)
    left = shift(final, "col", 1)
    gap = jnp.zeros(right.shape[:-1] + (LANES - 2 * SWEEPS,), jnp.float32)
    side = jnp.concatenate([right, gap, left], axis=-1)
    return edge, side


def on_device(precip, head, trans_coef, land, dest, moisture, ksat):
    tile_rows, tile_cols = precip.shape
    n_col = lax.axis_size("col")
    peers = lax.axis_size("row") * n_col
    me = lax.axis_index("row") * n_col + lax.axis_index("col")
    owned, layers, _ = moisture.shape
    blocks = tile_rows * tile_cols // LANES
    cap = (2 * blocks + peers - 1) // peers
    extra, hop = 2, 4
    depth = (19 * blocks // (16 * peers) + 1 + 7) // 8 * 8
    direct = depth - 1 - extra

    target = dest.T.reshape(blocks)
    owner = target // owned
    slot = target - owner * owned
    all_peers = jnp.arange(peers, dtype=jnp.int32)
    one_hot = owner[:, None] == all_peers[None, :]
    order = jnp.arange(blocks, dtype=jnp.int32)
    earlier = (order[None, :] < order[:, None]).astype(jnp.bfloat16)
    counts = jnp.dot(earlier, one_hot.astype(jnp.bfloat16), preferred_element_type=jnp.float32)
    sums = jnp.sum(one_hot.astype(jnp.float32), axis=0)
    over = jnp.maximum(sums - direct, 0.0)
    base = jnp.sum(jnp.where(all_peers[:, None] < all_peers[None, :], over[:, None], 0.0), axis=0)
    rank = jnp.sum(jnp.where(one_hot, counts, 0.0), axis=1).astype(jnp.int32)
    number = jnp.sum(jnp.where(one_hot, counts + base[None, :] - direct, 0.0), axis=1).astype(
        jnp.int32
    )
    spread = rank >= direct
    via = (jnp.maximum(number, 0) + me) % peers
    turn = jnp.clip(number // peers, 0, extra - 1)
    position = jnp.where(
        spread, peers * depth + via * extra + turn, owner * depth + rank
    )
    place = jnp.where(spread, via, owner)
    row_of = jnp.where(spread, direct + turn, rank)

    def table(where, row, width, value):
        hot = (where[:, None] == all_peers[None, :]).astype(jnp.float32)
        at = row[:, None] == jnp.arange(width, dtype=jnp.int32)[None, :]
        return lax.dot_general(
            hot,
            jnp.where(at, value.astype(jnp.float32)[:, None], 0.0),
            (((0,), (0,)), ((), ())),
            precision=lax.Precision.HIGHEST,
            preferred_element_type=jnp.float32,
        )

    source_of = jnp.minimum(table(place, row_of, depth, order).astype(jnp.int32), blocks - 1)
    label = table(owner, rank, LANES, slot - owned) + float(owned)
    sent = jnp.broadcast_to(jnp.pad(sums, (0, LANES - peers))[None, :], (peers, LANES))

    outgoing = pl.pallas_call(
        functools.partial(pack_spread_kernel, depth, extra),
        out_shape=f32(peers, 2 * depth, LANES),
        in_specs=[SM, VM, VM, VM, VM],
        out_specs=VM,
        scratch_shapes=[pltpu.VMEM((blocks, LANES), jnp.float32)] * 2,
    )(source_of.reshape(peers * depth), jnp.stack([label, sent]), precip, head, land)
    arrived = lax.all_to_all(outgoing, ("row", "col"), split_axis=0, concat_axis=0, tiled=True)

    land_share = land.astype(jnp.float32)
    transmit = trans_coef * (1.0 + 0.5 * jnp.tanh(head))
    fixed = jnp.stack([transmit, head * land_share, land_share])
    fixed_r, fixed_c = halos(fixed)

    step = 128
    flat = moisture.reshape(owned * layers, LANES)
    layered = pl.BlockSpec((layers, step, LANES), lambda i: (0, i, 0))
    single = pl.BlockSpec((step, LANES), lambda i: (i, 0))
    natural = pl.BlockSpec((step * layers, LANES), lambda i: (i, 0))
    s0, sx, sy, rec0, rec_x, rec_y = pl.pallas_call(
        functools.partial(factor_kernel, layers, 32),
        grid=(owned // step,),
        out_shape=[f32(layers, owned, LANES)] * 3 + [f32(owned, LANES)] * 3,
        in_specs=[natural, single],
        out_specs=[layered] * 3 + [single] * 3,
        cost_estimate=pl.CostEstimate(
            flops=50 * owned * layers * LANES,
            bytes_accessed=16 * owned * layers * LANES,
            transcendentals=owned * layers * LANES,
        ),
    )(flat, ksat)

    arrived, fixed_r, fixed_c = lax.optimization_barrier((arrived, fixed_r, fixed_c))
    vm, i32 = pltpu.VMEM, jnp.int32
    dma = pltpu.SemaphoreType.DMA
    tail = (peers * extra + depth - 1) // depth
    returned, slots, slot2, arr2, fits = pl.pallas_call(
        functools.partial(exchange_kernel, cap, extra, hop),
        out_shape=[
            f32(peers + tail, depth, LANES),
            jax.ShapeDtypeStruct((peers, LANES), i32),
            jax.ShapeDtypeStruct((8, LANES), i32),
            f32(peers, 2 * hop, LANES),
            f32(8, LANES),
        ],
        in_specs=[VM] * 4,
        out_specs=[VM] * 5,
        scratch_shapes=[
            vm((peers, 2 * hop, LANES), jnp.float32),
            vm((peers, depth, LANES), jnp.float32),
            vm((peers, hop, LANES), jnp.float32),
            vm((peers, hop, LANES), jnp.float32),
            vm((peers, extra, LANES), jnp.float32),
            vm((peers, extra, LANES), jnp.float32),
            vm((depth, LANES), jnp.float32),
            vm((depth, LANES), jnp.float32),
            vm((depth, LANES), jnp.float32),
            vm((8, LANES), i32),
            vm((extra * peers, LANES), i32),
            pltpu.SMEM((peers, LANES), i32),
            pltpu.SMEM((8, LANES), i32),
            pltpu.SMEM((8, LANES), i32),
            pltpu.SMEM((extra * peers, LANES), i32),
            dma((4,)),
        ]
        + [dma((peers,))] * 8
        + [dma((4,))],
        compiler_params=pltpu.CompilerParams(collective_id=4, has_side_effects=True),
    )(arrived, rec0, rec_x, rec_y)

    high, wide = tile_rows + 2 * SWEEPS, tile_cols + LANES

    def relax(identity, at, rows):
        return pl.pallas_call(
            relax_kernel,
            out_shape=f32(tile_rows, tile_cols),
            in_specs=[SM] + [VM] * 6,
            out_specs=VM,
            scratch_shapes=[pltpu.VMEM((high, wide), jnp.float32)] * 8
            + [
                pltpu.VMEM((blocks, LANES), jnp.float32),
                pltpu.VMEM((2, 8, tile_rows), jnp.float32),
                pltpu.VMEM((2, 8, tile_cols), jnp.float32),
                pltpu.VMEM((2, 8, tile_rows), jnp.float32),
                pltpu.VMEM((4, 8, LANES), jnp.float32),
                pltpu.SemaphoreType.DMA((8,)),
                pltpu.SemaphoreType.DMA((8,)),
            ],
            compiler_params=pltpu.CompilerParams(collective_id=identity, has_side_effects=True),
        )(at, rows.reshape(-1, LANES), head, land, fixed, fixed_r, fixed_c)

    def hopped():
        saturation = pl.pallas_call(
            functools.partial(spread_saturation_kernel, layers, extra, hop),
            grid=(owned // step,),
            out_shape=f32(owned * layers, LANES),
            in_specs=[
                SM,
                SM,
                pl.BlockSpec((peers, 2 * depth, LANES), lambda i: (0, 0, 0)),
                pl.BlockSpec((peers, 2 * hop, LANES), lambda i: (0, 0, 0)),
            ]
            + [layered] * 3,
            out_specs=natural,
            scratch_shapes=[pltpu.VMEM((owned + 8, LANES), jnp.float32)] * 2,
        )(slots, slot2, arrived, arr2, s0, sx, sy)
        return saturation.reshape(owned, layers, LANES), relax(1, position, returned)

    def whole():
        sources = table(owner, rank, cap, order).astype(jnp.int32).reshape(peers * cap)
        outgoing = pl.pallas_call(
            functools.partial(pack_kernel, peers, cap),
            out_shape=f32(peers, 2 * cap + 8, LANES),
            in_specs=[SM, VM, VM, VM, VM],
            out_specs=VM,
            scratch_shapes=[pltpu.VMEM((blocks, LANES), jnp.float32)] * 2,
        )(sources, label, precip, head, land)
        arrived = lax.all_to_all(outgoing, ("row", "col"), split_axis=0, concat_axis=0, tiled=True)
        places = arrived[:, 2 * cap, :cap].astype(jnp.int32).reshape(peers * cap)
        answer, infil, sig = pl.pallas_call(
            functools.partial(owner_kernel, peers, cap),
            out_shape=[f32(peers, cap, LANES), f32(owned, LANES), f32(owned, LANES)],
            in_specs=[SM, VM, VM, VM, VM],
            out_specs=[VM] * 3,
            scratch_shapes=[pltpu.VMEM((owned + 8, LANES), jnp.float32)] * 3,
        )(places, arrived, rec0, rec_x, rec_y)
        back = lax.all_to_all(answer, ("row", "col"), split_axis=0, concat_axis=0, tiled=True)
        saturation = pl.pallas_call(
            functools.partial(saturation_kernel, layers),
            grid=(owned // step,),
            out_shape=f32(owned * layers, LANES),
            in_specs=[layered] * 3 + [single] * 2,
            out_specs=natural,
        )(s0, sx, sy, infil, sig)
        return saturation.reshape(owned, layers, LANES), relax(2, owner * cap + rank, back)

    return lax.cond(fits[0, 0] > 0.5, hopped, whole)


def solution(mesh):
    tile = P("row", "col")
    placed = (
        tile,
        tile,
        tile,
        tile,
        tile,
        P(("row", "col"), None, None),
        P(("row", "col"), None),
    )
    return jax.shard_map(
        on_device,
        mesh=mesh,
        in_specs=placed,
        out_specs=(P(("row", "col"), None, None), P("row", "col")),
        check_vma=False,
    )
```

```python
import functools
import math

import jax
import jax.numpy as jnp
from jax import lax
from jax.experimental import pallas as pl
from jax.experimental.pallas import tpu as pltpu
from jax.sharding import PartitionSpec as P

SWEEPS = 4
LANES = 128

layer_depth = 0.1
step_ratio = 0.1
residual_water = 0.05
pore_range = 0.4
diff_length = 0.5
couple_rate = 0.05
recharge_gain = 20.0
store_rate = 0.2

VM = pl.BlockSpec(memory_space=pltpu.VMEM)
SM = pl.BlockSpec(memory_space=pltpu.SMEM)


def f32(*shape):
    return jax.ShapeDtypeStruct(shape, jnp.float32)


def factor_rows(layers, moist, ksat, base_row, group):
    rows = pl.ds(pl.multiple_of(base_row, group), group)
    ks = ksat[rows, :]
    ratios, reds, xs = [], [], []
    before = None
    for k in range(layers):
        m = moist[pl.ds(base_row * layers + k, group, stride=layers), :]
        w = (m - residual_water) * (1.0 / pore_range)
        s = ks * math.exp(-(k + 0.5) * layer_depth)
        sw2 = s * (w * w)
        hs = sw2 * (1.5 / pore_range)
        d = s * (0.2 * diff_length / (2.0 * layer_depth)) + sw2 * (
            diff_length / (2.0 * layer_depth)
        )
        hc = 0.5 * (sw2 * w)
        cur = (m, hs, d, hc)
        if before is None:
            before = cur
            g_up = q_up = nsub = None
            continue
        m0, hs0, d0, hc0 = before
        g = d0 + d
        q = (hc0 + hc) - g * (m - m0)
        if g_up is None:
            pivot = step_ratio + g + hs0
            inv = 1.0 / pivot
            reds.append(-q * inv)
            xs.append(inv)
        else:
            pivot = step_ratio + g_up + g - nsub * ratios[-1]
            inv = 1.0 / pivot
            reds.append(((q_up - q) + nsub * reds[-1]) * inv)
            xs.append(nsub * inv * xs[-1])
        ratios.append((g - hs) * inv)
        nsub = hs0 + g
        g_up, q_up = g, q
        before = cur
    m, hs, d, hc = before
    bottom = 2.0 * hc + couple_rate * (m - residual_water)
    pivot = step_ratio + g_up + hs + couple_rate - nsub * ratios[-1]
    inv = 1.0 / pivot
    change = ((q_up - bottom) + nsub * reds[-1]) * inv
    cx = nsub * inv * xs[-1]
    cy = (couple_rate * pore_range) * inv
    gain = 2.0 * hs + couple_rate
    recharge = (
        bottom + gain * change,
        gain * cx,
        gain * cy - couple_rate * pore_range,
    )
    unit = 1.0 / pore_range
    terms = [None] * layers
    for k in range(layers - 1, -1, -1):
        if k < layers - 1:
            change = reds[k] + ratios[k] * change
            cx = xs[k] + ratios[k] * cx
            cy = ratios[k] * cy
        m = moist[pl.ds(base_row * layers + k, group, stride=layers), :]
        terms[k] = ((m + change - residual_water) * unit, cx * unit, cy * unit)
    return recharge, terms


def fixed_fields(head, trans_coef, land):
    share = land.astype(jnp.float32)
    return trans_coef * (1.0 + 0.5 * jnp.tanh(head)), head * share, share


def neighbours(row, col):
    n_row, n_col = lax.axis_size("row"), lax.axis_size("col")
    up, down = row > 0, row < n_row - 1
    left, right = col > 0, col < n_col - 1
    steps = [(-1, 0), (1, 0), (0, -1), (0, 1), (-1, -1), (-1, 1), (1, -1), (1, 1)]
    go = [up, down, left, right, up & left, up & right, down & left, down & right]
    come = [down, up, right, left, down & right, down & left, up & right, up & left]
    return steps, go, come


def each(flags, act):
    for k, flag in enumerate(flags):
        pl.when(flag)(functools.partial(act, k))


def halo_copy(k, steps, row, col, src, dst, send_sem, recv_sem):
    return pltpu.make_async_remote_copy(
        src_ref=src[k],
        dst_ref=dst[k],
        send_sem=send_sem.at[k],
        recv_sem=recv_sem.at[k],
        device_id=(row + steps[k][0], col + steps[k][1]),
        device_id_type=pl.DeviceIdType.MESH,
    )


def column_kernel(
    cap, extra, hop, chunks, src, labels, precip, head, trans_coef, land, moisture, ksat,
    returned, saturation, fits, mid_r, mid_c,
    infil, heads, out, allbuf, moist, s0, sx, sy, rec0, rec_x, rec_y, own_i, own_h,
    mid_out, arr2, ans, ans2, arr4, out5, arr5, g0, gx, gy, src_v, ret_v, slots_v, slot2_v, inv_v,
    row_out, strip_out, from_row, strip_in, corner,
    slots_s, slot2_s, src_s, ret_s, inv_s,
    move, read, write, send1, recv1, send2, recv2, send3, recv3, send4, recv4, send5, recv5, own,
    send_h, recv_h,
):
    rows, cols = precip.shape
    peers, width, _ = allbuf.shape
    depth = out.shape[1] // 2
    direct = depth - 1 - extra
    layers, owned, _ = s0.shape
    n_col = lax.axis_size("col")
    row, col = lax.axis_index("row"), lax.axis_index("col")
    me = row * n_col + col
    barrier = pltpu.get_barrier_semaphore()
    part_rows = owned // chunks

    def fetch(c):
        part = pl.ds(c * part_rows * layers, part_rows * layers)
        return pltpu.make_async_copy(moisture.at[part], moist.at[part], read.at[c])

    def flush(c):
        part = pl.ds(c * part_rows * layers, part_rows * layers)
        return pltpu.make_async_copy(moist.at[part], saturation.at[part], write.at[c])

    def where_is(k):
        p = lax.rem(me + k, peers)
        return p, (p // n_col, lax.rem(p, n_col))

    def greet(k, _):
        pl.semaphore_signal(
            barrier, inc=1, device_id=where_is(k)[1], device_id_type=pl.DeviceIdType.MESH
        )
        return 0

    lax.fori_loop(1, peers, greet, 0)
    for c in range(chunks):
        fetch(c).start()

    def exchange(src, dst, send, recv, self_sem):
        def copy(k):
            p, place = where_is(k)
            return pltpu.make_async_remote_copy(
                src_ref=src(p),
                dst_ref=dst(me),
                send_sem=send.at[k],
                recv_sem=recv.at[k],
                device_id=place,
                device_id_type=pl.DeviceIdType.MESH,
            )

        here = pltpu.make_async_copy(src(me), dst(me), self_sem)

        def start(low, high):
            def body(k, _):
                copy(k).start()
                return 0

            lax.fori_loop(low, high, body, 0)

        def wait():
            def body(k, _):
                copy(k).wait()
                return 0

            lax.fori_loop(1, peers, body, 0)
            here.wait()

        return copy, here, start, wait

    for j in range(cols // LANES):
        part = pl.ds(j * LANES, LANES)
        infil[pl.ds(j * rows, rows), :] = precip[:, part] * land[:, part].astype(jnp.float32)
        heads[pl.ds(j * rows, rows), :] = head[:, part]

    def pack(p):
        for r in range(depth - 1):
            block = jnp.clip(src[p * depth + r], 0, infil.shape[0] - 1)
            out[p, pl.ds(r, 1), :] = infil[pl.ds(block, 1), :]
            out[p, pl.ds(depth + r, 1), :] = heads[pl.ds(block, 1), :]
        out[p, pl.ds(depth - 1, 1), :] = labels[0, pl.ds(p, 1), :]
        out[p, pl.ds(2 * depth - 1, 1), :] = labels[1, pl.ds(p, 1), :]

    copy1, here1, _, wait1 = exchange(
        lambda p: out.at[p], lambda p: allbuf.at[p, pl.ds(0, 2 * depth)], send1, recv1, own.at[0]
    )
    pl.semaphore_wait(barrier, peers - 1)

    def ship(k, _):
        pack(where_is(k)[0])
        copy1(k).start()
        return 0

    lax.fori_loop(1, peers, ship, 0)
    pack(me)
    here1.start()

    steps, go, come = neighbours(row, col)
    east, south = cols - LANES, rows - 8
    for side, at in enumerate((0, south)):
        edge = pl.ds(at, 8)
        for f, field in enumerate(fixed_fields(head[edge, :], trans_coef[edge, :], land[edge, :])):
            row_out[side, pl.ds(8 * f, 8), :] = field
    for side, at in enumerate((0, east)):
        edge = pl.ds(at, LANES)
        keep = slice(0, 8) if side == 0 else slice(LANES - 8, LANES)
        for f, field in enumerate(fixed_fields(head[:, edge], trans_coef[:, edge], land[:, edge])):
            strip_out[side, pl.ds(8 * f, 8), :] = jnp.transpose(field)[keep]
    halo_dst = [from_row.at[0], from_row.at[1], strip_in.at[0], strip_in.at[1]] + [
        corner.at[c] for c in range(4)
    ]
    halo_src = [row_out.at[0], row_out.at[1], strip_out.at[0], strip_out.at[1]] + [
        row_out.at[c // 2, :, pl.ds((c % 2) * east, LANES)] for c in range(4)
    ]
    for k in range(8):

        @pl.when(jnp.logical_not(come[k]))
        def _(ref=halo_dst[k]):
            ref[...] = jnp.zeros(ref.shape, jnp.float32)

    def halo(k):
        return halo_copy(k, steps, row, col, halo_src, halo_dst, send_h, recv_h)

    each(go, lambda k: halo(k).start())

    group = 32

    def factor(c, _):
        fetch(c).wait()

        def body(i, _):
            base_row = pl.multiple_of(c * part_rows + i * group, group)
            at = pl.ds(base_row, group)
            recharge, terms = factor_rows(layers, moist, ksat, base_row, group)
            for ref, value in zip((rec0, rec_x, rec_y), recharge):
                ref[at, :] = value
            for k in range(layers):
                for ref, value in zip((s0, sx, sy), terms[k]):
                    ref[k, at, :] = value
            return 0

        lax.fori_loop(0, part_rows // group, body, 0)
        return 0

    lax.fori_loop(0, chunks, factor, 0)
    wait1()

    shape = (peers, LANES)
    lane = lax.broadcasted_iota(jnp.int32, shape, 1)
    sub = lax.broadcasted_iota(jnp.int32, shape, 0)
    lab = allbuf[:, depth - 1, :]
    count = allbuf[:, 2 * depth - 1, :]
    over = jnp.maximum(count - direct, 0.0)
    tri = lax.broadcasted_iota(jnp.int32, (LANES, LANES), 0) < lax.broadcasted_iota(
        jnp.int32, (LANES, LANES), 1
    )
    base = jnp.dot(
        over, tri.astype(jnp.float32), precision=lax.Precision.HIGHEST,
        preferred_element_type=jnp.float32,
    )
    total = extra * peers
    before = (
        lax.broadcasted_iota(jnp.int32, (total, total), 1)
        < lax.broadcasted_iota(jnp.int32, (total, total), 0)
    ).astype(jnp.float32)

    def number(m):
        gap = m - sub
        return jnp.where(gap < 0, gap + peers, gap).astype(jnp.float32)

    def holds(j, first, many, t):
        j = j + float(t * peers)
        return jnp.where((first <= j) & (j < first + many), 1.0, 0.0)

    def prefix(v):
        return jnp.dot(before, v, preferred_element_type=jnp.float32)

    flane = lane.astype(jnp.float32)
    code = sub.astype(jnp.float32) * 8.0
    via = jnp.concatenate([holds(number(me), base, over, t) for t in range(extra)], axis=0)
    rank = prefix(via)
    codes = jnp.concatenate([code + float(t) for t in range(extra)], axis=0)
    lanes = jnp.concatenate([flane] * extra, axis=0)
    back = jnp.sum(via * (lanes * hop + rank), axis=1, keepdims=True)
    ret_v[...] = jnp.broadcast_to(back, (total, LANES)).astype(jnp.int32)
    pad = jnp.zeros((8 - hop, LANES), jnp.float32)
    picks = [
        jnp.sum(jnp.where(rank == float(e), via * codes, 0.0), axis=0, keepdims=True)
        for e in range(hop)
    ]
    src_v[...] = jnp.concatenate(picks + [pad], axis=0).astype(jnp.int32)
    mine = jnp.where(lane == me, 1.0, 0.0)
    first = jnp.sum(base * mine, axis=1, keepdims=True)
    many = jnp.sum(over * mine, axis=1, keepdims=True)
    inside = jnp.where(lane < peers, 1.0, 0.0)
    step = number(lane)
    took = [holds(step, first, many, t) * inside for t in range(extra)]
    value = []
    for t in range(extra):
        at = step + float(t * peers) - first
        v = jnp.zeros(shape, jnp.float32)
        for r in range(cap - direct):
            v = jnp.where(at == float(r), lab[:, direct + r : direct + r + 1] - float(owned), v)
        value.append(v)
    took = jnp.concatenate(took, axis=0)
    rank = prefix(took)
    value = jnp.concatenate(value, axis=0)
    picks = [
        jnp.sum(jnp.where(rank == float(e), took * value, 0.0), axis=0, keepdims=True)
        for e in range(hop)
    ]
    hopped = jnp.concatenate(picks + [pad], axis=0) + float(owned)
    slot2_v[...] = hopped.astype(jnp.int32)
    slots_v[...] = lab.astype(jnp.int32)
    moves = [
        pltpu.make_async_copy(src_v, src_s, move.at[0]),
        pltpu.make_async_copy(slots_v, slots_s, move.at[1]),
        pltpu.make_async_copy(slot2_v, slot2_s, move.at[2]),
        pltpu.make_async_copy(ret_v, ret_s, move.at[3]),
    ]
    for m in moves:
        m.start()
    g0[...] = jnp.zeros(g0.shape, jnp.float32)
    gx[...] = jnp.zeros(gx.shape, jnp.float32)
    gy[...] = jnp.zeros(gy.shape, jnp.float32)
    for m in moves:
        m.wait()

    def pass_on(d, _):
        for e in range(hop):
            q = src_s[e, d]
            s = jnp.clip(q // 8, 0, peers - 1)
            t = jnp.clip(q - s * 8, 0, extra - 1)
            mid_out[d, pl.ds(e, 1), :] = allbuf[s, pl.ds(direct + t, 1), :]
            mid_out[d, pl.ds(hop + e, 1), :] = allbuf[s, pl.ds(depth + direct + t, 1), :]
        return 0

    lax.fori_loop(0, peers, pass_on, 0)
    _, here2, start2, wait2 = exchange(
        lambda p: mid_out.at[p], lambda p: arr2.at[p], send2, recv2, own.at[1]
    )
    here2.start()
    start2(1, peers)

    def answer(p, _):
        for r in range(direct):
            slot = jnp.clip(slots_s[p, r], 0, owned - 1)
            g0[pl.ds(r, 1), :] = rec0[pl.ds(slot, 1), :]
            gx[pl.ds(r, 1), :] = rec_x[pl.ds(slot, 1), :]
            gy[pl.ds(r, 1), :] = rec_y[pl.ds(slot, 1), :]
        ans[p] = (
            g0[...]
            + allbuf[p, pl.ds(0, depth), :] * gx[...]
            + jax.nn.sigmoid(allbuf[p, pl.ds(depth, depth), :]) * gy[...]
        )
        return 0

    lax.fori_loop(0, peers, answer, 0)
    _, here3, start3, wait3 = exchange(
        lambda p: ans.at[p], lambda p: returned.at[p], send3, recv3, own.at[2]
    )
    _, here4, start4, wait4 = exchange(
        lambda p: ans2.at[p], lambda p: arr4.at[p], send4, recv4, own.at[3]
    )
    _, here5, start5, wait5 = exchange(
        lambda p: out5.at[p], lambda p: arr5.at[p], send5, recv5, own.at[4]
    )
    wait2()

    def answer2(m, _):
        for e in range(hop):
            slot = jnp.clip(slot2_s[e, m], 0, owned - 1)
            ans2[m, pl.ds(e, 1), :] = (
                rec0[pl.ds(slot, 1), :]
                + arr2[m, pl.ds(e, 1), :] * rec_x[pl.ds(slot, 1), :]
                + jax.nn.sigmoid(arr2[m, pl.ds(hop + e, 1), :]) * rec_y[pl.ds(slot, 1), :]
            )
        allbuf[m, pl.ds(2 * depth, 2 * hop), :] = arr2[m]
        return 0

    lax.fori_loop(0, peers, answer2, 0)
    here4.start()
    start4(1, peers)
    early = peers // 4
    here3.start()
    start3(1, early)

    columns = jnp.transpose(
        jnp.concatenate([hopped, jnp.zeros((LANES - 8, LANES), jnp.float32)], axis=0)
    )
    place = sub.astype(jnp.float32) * 65536.0
    for g in range(owned // LANES):
        want = flane + float(g * LANES)
        found = jnp.zeros(shape, jnp.float32)
        for r in range(direct):
            found = jnp.where(lab[:, r : r + 1] == want, place + float(256 * r + depth + r), found)
        for e in range(hop):
            at = 2 * depth + e
            found = jnp.where(
                columns[0:peers, e : e + 1] == want, place + float(256 * at + at + hop), found
            )
        inv_v[pl.ds(g, 1), :] = jnp.sum(found, axis=0, keepdims=True).astype(jnp.int32)
    turn = pltpu.make_async_copy(inv_v, inv_s, move.at[4])
    turn.start()
    wait4()

    def hand_back(s, _):
        for t in range(extra):
            at = jnp.clip(ret_s[t * peers + s, 0], 0, peers * hop - 1)
            d = at // hop
            out5[s, pl.ds(t, 1), :] = arr4[d, pl.ds(at - d * hop, 1), :]
        return 0

    lax.fori_loop(0, peers, hand_back, 0)
    here5.start()
    start5(1, peers)
    start3(early, peers)
    turn.wait()

    def sort(g, _):
        for u in range(16):
            v = inv_s[g // (LANES // 16), lax.rem(g, LANES // 16) * 16 + u]
            p = jnp.clip(v // 65536, 0, peers - 1)
            rest = v - p * 65536
            i = jnp.clip(rest // 256, 0, width - 1)
            h = jnp.clip(rest - i * 256, 0, width - 1)
            own_i[pl.ds(g * 16 + u, 1), :] = allbuf[p, pl.ds(i, 1), :]
            own_h[pl.ds(g * 16 + u, 1), :] = allbuf[p, pl.ds(h, 1), :]
        return 0

    lax.fori_loop(0, owned // 16, sort, 0)

    def finish(c, _):
        def body(i, _):
            base_row = pl.multiple_of(c * part_rows + i * group, group)
            at = pl.ds(base_row, group)
            inf = own_i[at, :]
            sg = jax.nn.sigmoid(own_h[at, :])
            for k in range(layers):
                moist[pl.ds(base_row * layers + k, group, stride=layers), :] = (
                    s0[k, at, :] + inf * sx[k, at, :] + sg * sy[k, at, :]
                )
            return 0

        lax.fori_loop(0, part_rows // group, body, 0)
        flush(c).start()
        return 0

    lax.fori_loop(0, chunks, finish, 0)

    def widest(m, most):
        n = number(m)
        seen = functools.reduce(lambda x, y: x + y, [holds(n, base, over, t) for t in range(extra)])
        return jnp.maximum(most, jnp.sum(seen, axis=0, keepdims=True))

    most = lax.fori_loop(0, peers, widest, jnp.zeros((1, LANES), jnp.float32))
    spread = jnp.max(jnp.sum(over, axis=1, keepdims=True), axis=0, keepdims=True)
    bad = jnp.maximum(
        jnp.where(jnp.max(most, axis=1, keepdims=True) > float(hop), 1.0, 0.0),
        jnp.where(spread > float(total), 1.0, 0.0),
    )
    fits[...] = jnp.broadcast_to(1.0 - bad, fits.shape)

    def landed(k):
        return pltpu.make_async_remote_copy(
            src_ref=halo_src[k],
            dst_ref=halo_dst[k],
            send_sem=send_h.at[k],
            recv_sem=recv_h.at[k],
            device_id=(row, col),
            device_id_type=pl.DeviceIdType.MESH,
        )

    each(go, lambda k: halo(k).wait_send())
    each(come, lambda k: landed(k).wait_recv())
    upper = lax.broadcasted_iota(jnp.int32, (8, LANES), 0) < 4
    near = lax.broadcasted_iota(jnp.int32, (8, LANES), 1) < LANES // 2
    for f in range(3):
        eight = pl.ds(8 * f, 8)
        for j in range(cols // LANES):
            part = pl.ds(j * LANES, LANES)
            mid_r[f, :, part] = jnp.where(upper, from_row[0, eight, part], from_row[1, eight, part])
        mid_c[f, pl.ds(rows, 8), :] = jnp.where(
            upper,
            jnp.where(near, corner[0, eight, :], corner[1, eight, :]),
            jnp.where(near, corner[2, eight, :], corner[3, eight, :]),
        )
        mid_c[f, pl.ds(0, rows), :] = jnp.transpose(
            jnp.concatenate(
                [
                    strip_in[0, eight, :],
                    jnp.zeros((LANES - 16, rows), jnp.float32),
                    strip_in[1, eight, :],
                ],
                axis=0,
            )
        )
    wait5()
    for i in range(total):
        returned[peers + i // depth, pl.ds(i % depth, 1), :] = arr5[
            i // extra, pl.ds(i % extra, 1), :
        ]
    wait3()
    for c in range(chunks):
        flush(c).wait()


def pack_kernel(peers, per_peer, src, labels, precip, head, land, out, infil, heads):
    rows, cols = precip.shape
    for j in range(cols // LANES):
        part = pl.ds(j * LANES, LANES)
        infil[pl.ds(j * rows, rows), :] = precip[:, part] * land[:, part].astype(jnp.float32)
        heads[pl.ds(j * rows, rows), :] = head[:, part]

    def body(p, _):
        for r in range(per_peer):
            block = src[p * per_peer + r]
            out[p, pl.ds(r, 1), :] = infil[pl.ds(block, 1), :]
            out[p, pl.ds(per_peer + r, 1), :] = heads[pl.ds(block, 1), :]
        out[p, pl.ds(2 * per_peer, 8), :] = jnp.broadcast_to(labels[pl.ds(p, 1), :], (8, LANES))
        return 0

    lax.fori_loop(0, peers, body, 0)


def owner_kernel(
    peers, per_peer, slots, arrived, rec0, rec_x, rec_y, answer, infil, sig, own_i, own_h, rec
):
    owned = rec0.shape[0]

    def scatter(p, _):
        for r in range(per_peer):
            slot = slots[p * per_peer + r]
            own_i[pl.ds(slot, 1), :] = arrived[p, pl.ds(r, 1), :]
            own_h[pl.ds(slot, 1), :] = arrived[p, pl.ds(per_peer + r, 1), :]
        return 0

    lax.fori_loop(0, peers, scatter, 0)
    rec[pl.ds(owned, 8), :] = jnp.zeros((8, LANES), jnp.float32)

    def combine(g, _):
        part = pl.ds(g * 64, 64)
        inf = own_i[part, :]
        sg = jax.nn.sigmoid(own_h[part, :])
        infil[part, :] = inf
        sig[part, :] = sg
        rec[part, :] = rec0[part, :] + inf * rec_x[part, :] + sg * rec_y[part, :]
        return 0

    lax.fori_loop(0, owned // 64, combine, 0)

    def gather(p, _):
        for r in range(per_peer):
            slot = slots[p * per_peer + r]
            answer[p, pl.ds(r, 1), :] = rec[pl.ds(slot, 1), :]
        return 0

    lax.fori_loop(0, peers, gather, 0)


def factor_kernel(layers, group, moist, ksat, s0, sx, sy, rec0, rec_x, rec_y):
    def body(step, _):
        base_row = step * group
        rows = pl.ds(pl.multiple_of(base_row, group), group)
        recharge, terms = factor_rows(layers, moist, ksat, base_row, group)
        for ref, value in zip((rec0, rec_x, rec_y), recharge):
            ref[rows, :] = value
        for k in range(layers):
            for ref, value in zip((s0, sx, sy), terms[k]):
                ref[k, rows, :] = value
        return 0

    lax.fori_loop(0, ksat.shape[0] // group, body, 0)


def saturation_kernel(layers, s0, sx, sy, infil, sig, out):
    count = infil.shape[0]
    group = 32

    def body(step, _):
        rows = pl.ds(pl.multiple_of(step * group, group), group)
        inf = infil[rows, :]
        sg = sig[rows, :]
        for k in range(layers):
            out[pl.ds(step * group * layers + k, group, stride=layers), :] = (
                s0[k, rows, :] + inf * sx[k, rows, :] + sg * sy[k, rows, :]
            )
        return 0

    lax.fori_loop(0, count // group, body, 0)


def relax_kernel(
    position, returned, head, trans_coef, land, mid_r, mid_c, out,
    t_ref, s_ref, fu, fd, fl, fr, a, b, sorted_rows, strip_out, from_row, strip_in, corner, send_sem, recv_sem,
):
    rows, cols = head.shape
    high, wide = t_ref.shape
    row, col = lax.axis_index("row"), lax.axis_index("col")
    n_row, n_col = lax.axis_size("row"), lax.axis_size("col")
    up, down = row > 0, row < n_row - 1
    left, right = col > 0, col < n_col - 1
    east = cols - LANES
    south = rows - 8
    links = [
        (up, -1, 0, s_ref.at[pl.ds(0, 8), pl.ds(0, cols)], from_row.at[0]),
        (down, 1, 0, s_ref.at[pl.ds(south, 8), pl.ds(0, cols)], from_row.at[1]),
        (left, 0, -1, strip_out.at[0], strip_in.at[0]),
        (right, 0, 1, strip_out.at[1], strip_in.at[1]),
        (up & left, -1, -1, s_ref.at[pl.ds(0, 8), pl.ds(0, LANES)], corner.at[0]),
        (up & right, -1, 1, s_ref.at[pl.ds(0, 8), pl.ds(east, LANES)], corner.at[1]),
        (down & left, 1, -1, s_ref.at[pl.ds(south, 8), pl.ds(0, LANES)], corner.at[2]),
        (down & right, 1, 1, s_ref.at[pl.ds(south, 8), pl.ds(east, LANES)], corner.at[3]),
    ]
    come = [down, up, right, left, down & right, down & left, up & right, up & left]
    barrier = pltpu.get_barrier_semaphore()

    def each(flags, act):
        for k, flag in enumerate(flags):
            pl.when(flag)(functools.partial(act, k))

    def copy(k):
        _, dr, dc, src, dst = links[k]
        return pltpu.make_async_remote_copy(
            src_ref=src,
            dst_ref=dst,
            send_sem=send_sem.at[k],
            recv_sem=recv_sem.at[k],
            device_id=(row + dr, col + dc),
            device_id_type=pl.DeviceIdType.MESH,
        )

    def copy_in(k):
        _, _, _, src, dst = links[k]
        return pltpu.make_async_remote_copy(
            src_ref=src,
            dst_ref=dst,
            send_sem=send_sem.at[k],
            recv_sem=recv_sem.at[k],
            device_id=(row, col),
            device_id_type=pl.DeviceIdType.MESH,
        )

    go = [link[0] for link in links]

    def greet(k):
        pl.semaphore_signal(
            barrier,
            inc=1,
            device_id=(row + links[k][1], col + links[k][2]),
            device_id_type=pl.DeviceIdType.MESH,
        )

    each(go, greet)
    for k in range(8):
        ref = [from_row.at[0], from_row.at[1], strip_in.at[0], strip_in.at[1]] + [
            corner.at[c] for c in range(4)
        ]

        @pl.when(jnp.logical_not(come[k]))
        def _(ref=ref[k]):
            ref[...] = jnp.zeros(ref.shape, jnp.float32)

    for j in range(cols // LANES):
        part = slice(j * LANES, (j + 1) * LANES)

        def body(g, _, j=j, part=part):
            base = g * 32
            got = [returned[pl.ds(position[j * rows + base + u], 1), :] for u in range(32)]
            for u in range(32):
                sorted_rows[pl.ds(j * rows + base + u, 1), :] = got[u]
            return 0

        lax.fori_loop(0, rows // 32, body, 0)
        s_ref[0:rows, part] = (
            store_rate * (head[:, part] * land[:, part].astype(jnp.float32))
            + recharge_gain * sorted_rows[j * rows : (j + 1) * rows, :]
        )
    strip_out[0] = jnp.transpose(s_ref[0:rows, 0:LANES])[0:8]
    strip_out[1] = jnp.transpose(s_ref[0:rows, east:cols])[LANES - 8 : LANES]

    def count(flags):
        return functools.reduce(lambda x, y: x + y, [f.astype(jnp.int32) for f in flags])

    pl.semaphore_wait(barrier, count(go))
    each(go, lambda k: copy(k).start())

    for f, (ref, centre) in enumerate(
        zip((t_ref, a, b), fixed_fields(head[...], trans_coef[...], land[...]))
    ):
        ref[0:rows, 0:cols] = centre
        ref[rows:high, 0:cols] = mid_r[f]
        ref[:, cols:wide] = mid_c[f]
    for g in range(wide // LANES):
        part = slice(g * LANES, (g + 1) * LANES)
        lo = slice((g - 1) % (wide // LANES) * LANES, (g - 1) % (wide // LANES) * LANES + LANES)
        hi = slice((g + 1) % (wide // LANES) * LANES, (g + 1) % (wide // LANES) * LANES + LANES)
        lane = lax.broadcasted_iota(jnp.int32, (high, LANES), 1)
        t = t_ref[:, part]
        tu = 0.5 * (t + pltpu.roll(t, 1, 0))
        td = 0.5 * (t + pltpu.roll(t, high - 1, 0))
        tl = jnp.where(lane == 0, pltpu.roll(t_ref[:, lo], 1, 1), pltpu.roll(t, 1, 1))
        tr = jnp.where(
            lane == LANES - 1,
            pltpu.roll(t_ref[:, hi], LANES - 1, 1),
            pltpu.roll(t, LANES - 1, 1),
        )
        lf = 0.5 * (t + tl)
        rt = 0.5 * (t + tr)
        inv = b[:, part] / (store_rate + (tu + td + lf + rt))
        fu[:, part] = tu * inv
        fd[:, part] = td * inv
        fl[:, part] = lf * inv
        fr[:, part] = rt * inv
        b[:, part] = inv

    each(go, lambda k: copy(k).wait_send())
    each(come, lambda k: copy_in(k).wait_recv())

    first = lax.broadcasted_iota(jnp.int32, (8, LANES), 0) < 4
    near = lax.broadcasted_iota(jnp.int32, (8, LANES), 1) < LANES // 2
    for j in range(cols // LANES):
        part = slice(j * LANES, (j + 1) * LANES)
        s_ref[rows:high, part] = jnp.where(first, from_row[0, :, part], from_row[1, :, part])
    s_ref[rows:high, cols:wide] = jnp.where(
        first,
        jnp.where(near, corner[0], corner[1]),
        jnp.where(near, corner[2], corner[3]),
    )
    s_ref[0:rows, cols:wide] = jnp.transpose(
        jnp.concatenate(
            [strip_in[0], jnp.zeros((LANES - 16, rows), jnp.float32), strip_in[1]], axis=0
        )
    )
    for g in range(wide // LANES):
        part = slice(g * LANES, (g + 1) * LANES)
        s_ref[:, part] = s_ref[:, part] * b[:, part]
    now, later = a, b
    for sweep in range(SWEEPS):
        last = sweep == SWEEPS - 1
        for g in range(wide // LANES):
            if last and g * LANES >= cols:
                continue
            part = slice(g * LANES, (g + 1) * LANES)
            lo = (g - 1) % (wide // LANES) * LANES
            hi = (g + 1) % (wide // LANES) * LANES
            lane = lax.broadcasted_iota(jnp.int32, (high, LANES), 1)
            x = now[:, part]
            xl = jnp.where(
                lane == 0, pltpu.roll(now[:, lo : lo + LANES], 1, 1), pltpu.roll(x, 1, 1)
            )
            xr = jnp.where(
                lane == LANES - 1,
                pltpu.roll(now[:, hi : hi + LANES], LANES - 1, 1),
                pltpu.roll(x, LANES - 1, 1),
            )
            y = s_ref[:, part] + fu[:, part] * pltpu.roll(x, 1, 0)
            y = y + fd[:, part] * pltpu.roll(x, high - 1, 0)
            y = y + (fl[:, part] * xl + fr[:, part] * xr)
            if last:
                out[:, part] = y[0:rows]
            else:
                later[:, part] = y
        now, later = later, now


def on_device(precip, head, trans_coef, land, dest, moisture, ksat):
    tile_rows, tile_cols = precip.shape
    n_col = lax.axis_size("col")
    peers = lax.axis_size("row") * n_col
    me = lax.axis_index("row") * n_col + lax.axis_index("col")
    owned, layers, _ = moisture.shape
    blocks = tile_rows * tile_cols // LANES
    cap = (2 * blocks + peers - 1) // peers
    extra, hop = 2, 4
    depth = (19 * blocks // (16 * peers) + 1 + 7) // 8 * 8
    direct = depth - 1 - extra

    target = dest.T.reshape(blocks)
    owner = target // owned
    slot = target - owner * owned
    all_peers = jnp.arange(peers, dtype=jnp.int32)
    one_hot = owner[:, None] == all_peers[None, :]
    order = jnp.arange(blocks, dtype=jnp.int32)
    earlier = (order[None, :] < order[:, None]).astype(jnp.bfloat16)
    counts = jnp.dot(earlier, one_hot.astype(jnp.bfloat16), preferred_element_type=jnp.float32)
    sums = jnp.sum(one_hot.astype(jnp.float32), axis=0)
    over = jnp.maximum(sums - direct, 0.0)
    base = jnp.sum(jnp.where(all_peers[:, None] < all_peers[None, :], over[:, None], 0.0), axis=0)
    rank = jnp.sum(jnp.where(one_hot, counts, 0.0), axis=1).astype(jnp.int32)
    number = jnp.sum(jnp.where(one_hot, counts + base[None, :] - direct, 0.0), axis=1).astype(
        jnp.int32
    )
    spread = rank >= direct
    via = (jnp.maximum(number, 0) + me) % peers
    turn = jnp.clip(number // peers, 0, extra - 1)
    position = jnp.where(
        spread, peers * depth + via * extra + turn, owner * depth + rank
    )
    place = jnp.where(spread, via, owner)
    row_of = jnp.where(spread, direct + turn, rank)

    def table(where, row, width, value):
        hot = (where[:, None] == all_peers[None, :]).astype(jnp.float32)
        at = row[:, None] == jnp.arange(width, dtype=jnp.int32)[None, :]
        return lax.dot_general(
            hot,
            jnp.where(at, value.astype(jnp.float32)[:, None], 0.0),
            (((0,), (0,)), ((), ())),
            precision=lax.Precision.HIGHEST,
            preferred_element_type=jnp.float32,
        )

    source_of = jnp.minimum(table(place, row_of, depth, order).astype(jnp.int32), blocks - 1)
    label = table(owner, rank, LANES, slot - owned) + float(owned)
    sent = jnp.broadcast_to(jnp.pad(sums, (0, LANES - peers))[None, :], (peers, LANES))

    sources, labels, position, owner, rank = lax.optimization_barrier(
        (source_of.reshape(peers * depth), jnp.stack([label, sent]), position, owner, rank)
    )
    flat = moisture.reshape(owned * layers, LANES)
    vm = lambda *shape: pltpu.VMEM(shape, jnp.float32)
    iv = lambda *shape: pltpu.VMEM(shape, jnp.int32)
    sm = lambda *shape: pltpu.SMEM(shape, jnp.int32)
    dma = lambda n: pltpu.SemaphoreType.DMA((n,))
    chunks = 8
    tail = (peers * extra + depth - 1) // depth
    high, wide = tile_rows + 2 * SWEEPS, tile_cols + LANES
    returned, stepped, fits, mid_r, mid_c = pl.pallas_call(
        functools.partial(column_kernel, cap, extra, hop, chunks),
        out_shape=[
            f32(peers + tail, depth, LANES),
            f32(owned * layers, LANES),
            f32(8, LANES),
            f32(3, 2 * SWEEPS, tile_cols),
            f32(3, high, LANES),
        ],
        in_specs=[SM] + [VM] * 5 + [pl.BlockSpec(memory_space=pl.ANY), VM],
        out_specs=[VM, pl.BlockSpec(memory_space=pl.ANY), VM, VM, VM],
        scratch_shapes=[
            vm(blocks, LANES),
            vm(blocks, LANES),
            vm(peers, 2 * depth, LANES),
            vm(peers, 2 * (depth + hop), LANES),
            vm(owned * layers, LANES),
        ]
        + [vm(layers, owned, LANES)] * 3
        + [vm(owned, LANES)] * 5
        + [
            vm(peers, 2 * hop, LANES),
            vm(peers, 2 * hop, LANES),
            vm(peers, depth, LANES),
            vm(peers, hop, LANES),
            vm(peers, hop, LANES),
            vm(peers, extra, LANES),
            vm(peers, extra, LANES),
            vm(depth, LANES),
            vm(depth, LANES),
            vm(depth, LANES),
            iv(8, LANES),
            iv(extra * peers, LANES),
            iv(peers, LANES),
            iv(8, LANES),
            iv(owned // LANES, LANES),
            vm(2, 24, tile_cols),
            vm(2, 24, tile_rows),
            vm(2, 24, tile_cols),
            vm(2, 24, tile_rows),
            vm(4, 24, LANES),
            sm(peers, LANES),
            sm(8, LANES),
            sm(8, LANES),
            sm(extra * peers, LANES),
            sm(owned // LANES, LANES),
            dma(5),
            dma(chunks),
            dma(chunks),
        ]
        + [dma(peers)] * 10
        + [dma(5), dma(8), dma(8)],
        compiler_params=pltpu.CompilerParams(
            collective_id=4, has_side_effects=True, vmem_limit_bytes=58 * 2**20
        ),
    )(sources, labels, precip, head, trans_coef, land, flat, ksat)


    def relax(identity, at, rows):
        return pl.pallas_call(
            relax_kernel,
            out_shape=f32(tile_rows, tile_cols),
            in_specs=[SM] + [VM] * 6,
            out_specs=VM,
            scratch_shapes=[pltpu.VMEM((high, wide), jnp.float32)] * 8
            + [
                pltpu.VMEM((blocks, LANES), jnp.float32),
                pltpu.VMEM((2, 8, tile_rows), jnp.float32),
                pltpu.VMEM((2, 8, tile_cols), jnp.float32),
                pltpu.VMEM((2, 8, tile_rows), jnp.float32),
                pltpu.VMEM((4, 8, LANES), jnp.float32),
                pltpu.SemaphoreType.DMA((8,)),
                pltpu.SemaphoreType.DMA((8,)),
            ],
            compiler_params=pltpu.CompilerParams(collective_id=identity, has_side_effects=True),
        )(at, rows.reshape(-1, LANES), head, trans_coef, land, mid_r, mid_c)

    def hopped():
        return stepped.reshape(owned, layers, LANES), relax(1, position, returned)

    def whole():
        step = 128
        layered = pl.BlockSpec((layers, step, LANES), lambda i: (0, i, 0))
        single = pl.BlockSpec((step, LANES), lambda i: (i, 0))
        natural = pl.BlockSpec((step * layers, LANES), lambda i: (i, 0))
        s0, sx, sy, rec0, rec_x, rec_y = pl.pallas_call(
            functools.partial(factor_kernel, layers, 32),
            grid=(owned // step,),
            out_shape=[f32(layers, owned, LANES)] * 3 + [f32(owned, LANES)] * 3,
            in_specs=[natural, single],
            out_specs=[layered] * 3 + [single] * 3,
        )(flat, ksat)
        slots_of = table(owner, rank, cap, order).astype(jnp.int32).reshape(peers * cap)
        outgoing = pl.pallas_call(
            functools.partial(pack_kernel, peers, cap),
            out_shape=f32(peers, 2 * cap + 8, LANES),
            in_specs=[SM, VM, VM, VM, VM],
            out_specs=VM,
            scratch_shapes=[pltpu.VMEM((blocks, LANES), jnp.float32)] * 2,
        )(slots_of, labels[0], precip, head, land)
        arrived = lax.all_to_all(outgoing, ("row", "col"), split_axis=0, concat_axis=0, tiled=True)
        places = arrived[:, 2 * cap, :cap].astype(jnp.int32).reshape(peers * cap)
        answer, infil, sig = pl.pallas_call(
            functools.partial(owner_kernel, peers, cap),
            out_shape=[f32(peers, cap, LANES), f32(owned, LANES), f32(owned, LANES)],
            in_specs=[SM, VM, VM, VM, VM],
            out_specs=[VM] * 3,
            scratch_shapes=[pltpu.VMEM((owned + 8, LANES), jnp.float32)] * 3,
        )(places, arrived, rec0, rec_x, rec_y)
        back = lax.all_to_all(answer, ("row", "col"), split_axis=0, concat_axis=0, tiled=True)
        saturation = pl.pallas_call(
            functools.partial(saturation_kernel, layers),
            grid=(owned // step,),
            out_shape=f32(owned * layers, LANES),
            in_specs=[layered] * 3 + [single] * 2,
            out_specs=natural,
        )(s0, sx, sy, infil, sig)
        return saturation.reshape(owned, layers, LANES), relax(2, owner * cap + rank, back)

    return lax.cond(fits[0, 0] > 0.5, hopped, whole)


def solution(mesh):
    tile = P("row", "col")
    placed = (
        tile,
        tile,
        tile,
        tile,
        tile,
        P(("row", "col"), None, None),
        P(("row", "col"), None),
    )
    return jax.shard_map(
        on_device,
        mesh=mesh,
        in_specs=placed,
        out_specs=(P(("row", "col"), None, None), P("row", "col")),
        check_vma=False,
    )
```

```python
import functools
import math

import jax
import jax.numpy as jnp
from jax import lax
from jax.experimental import pallas as pl
from jax.experimental.pallas import tpu as pltpu
from jax.sharding import PartitionSpec as P

SWEEPS = 4
LANES = 128

layer_depth = 0.1
step_ratio = 0.1
residual_water = 0.05
pore_range = 0.4
diff_length = 0.5
couple_rate = 0.05
recharge_gain = 20.0
store_rate = 0.2

VM = pl.BlockSpec(memory_space=pltpu.VMEM)
SM = pl.BlockSpec(memory_space=pltpu.SMEM)


def f32(*shape):
    return jax.ShapeDtypeStruct(shape, jnp.float32)


def factor_rows(layers, moist, ksat, base_row, group):
    rows = pl.ds(pl.multiple_of(base_row, group), group)
    ks = ksat[rows, :]
    ratios, reds, xs = [], [], []
    before = None
    for k in range(layers):
        m = moist[pl.ds(base_row * layers + k, group, stride=layers), :]
        w = (m - residual_water) * (1.0 / pore_range)
        s = ks * math.exp(-(k + 0.5) * layer_depth)
        sw2 = s * (w * w)
        hs = sw2 * (1.5 / pore_range)
        d = s * (0.2 * diff_length / (2.0 * layer_depth)) + sw2 * (
            diff_length / (2.0 * layer_depth)
        )
        hc = 0.5 * (sw2 * w)
        cur = (m, hs, d, hc)
        if before is None:
            before = cur
            g_up = q_up = nsub = None
            continue
        m0, hs0, d0, hc0 = before
        g = d0 + d
        q = (hc0 + hc) - g * (m - m0)
        if g_up is None:
            pivot = step_ratio + g + hs0
            inv = 1.0 / pivot
            reds.append(-q * inv)
            xs.append(inv)
        else:
            pivot = step_ratio + g_up + g - nsub * ratios[-1]
            inv = 1.0 / pivot
            reds.append(((q_up - q) + nsub * reds[-1]) * inv)
            xs.append(nsub * inv * xs[-1])
        ratios.append((g - hs) * inv)
        nsub = hs0 + g
        g_up, q_up = g, q
        before = cur
    m, hs, d, hc = before
    bottom = 2.0 * hc + couple_rate * (m - residual_water)
    pivot = step_ratio + g_up + hs + couple_rate - nsub * ratios[-1]
    inv = 1.0 / pivot
    change = ((q_up - bottom) + nsub * reds[-1]) * inv
    cx = nsub * inv * xs[-1]
    cy = (couple_rate * pore_range) * inv
    gain = 2.0 * hs + couple_rate
    recharge = (
        bottom + gain * change,
        gain * cx,
        gain * cy - couple_rate * pore_range,
    )
    unit = 1.0 / pore_range
    terms = [None] * layers
    for k in range(layers - 1, -1, -1):
        if k < layers - 1:
            change = reds[k] + ratios[k] * change
            cx = xs[k] + ratios[k] * cx
            cy = ratios[k] * cy
        m = moist[pl.ds(base_row * layers + k, group, stride=layers), :]
        terms[k] = ((m + change - residual_water) * unit, cx * unit, cy * unit)
    return recharge, terms


def fixed_fields(head, trans_coef, land):
    share = land.astype(jnp.float32)
    return trans_coef * (1.0 + 0.5 * jnp.tanh(head)), head * share, share


def neighbours(row, col):
    n_row, n_col = lax.axis_size("row"), lax.axis_size("col")
    up, down = row > 0, row < n_row - 1
    left, right = col > 0, col < n_col - 1
    steps = [(-1, 0), (1, 0), (0, -1), (0, 1), (-1, -1), (-1, 1), (1, -1), (1, 1)]
    go = [up, down, left, right, up & left, up & right, down & left, down & right]
    come = [down, up, right, left, down & right, down & left, up & right, up & left]
    return steps, go, come


def each(flags, act):
    for k, flag in enumerate(flags):
        pl.when(flag)(functools.partial(act, k))


def halo_copy(k, steps, row, col, src, dst, send_sem, recv_sem):
    return pltpu.make_async_remote_copy(
        src_ref=src[k],
        dst_ref=dst[k],
        send_sem=send_sem.at[k],
        recv_sem=recv_sem.at[k],
        device_id=(row + steps[k][0], col + steps[k][1]),
        device_id_type=pl.DeviceIdType.MESH,
    )


def column_kernel(
    cap, extra, hop, chunks, src, labels, precip, head, trans_coef, land, moisture, ksat,
    returned, saturation, fits, mid_r, mid_c,
    infil, sigs, out, allbuf, labs, moist, sx, sy, rec0, rec_x, rec_y,
    mid_out, arr2, ans, ans2, arr4, out5, arr5, g0, gx, gy, src_v, ret_v, slots_v, slot2_v, inv_v,
    row_out, strip_out, from_row, strip_in, corner,
    slots_s, slot2_s, src_s, ret_s, inv_s,
    move, read, write, send0, recv0, send1, recv1, send2, recv2, send3, recv3, send4, recv4, send5, recv5, own,
    send_h, recv_h,
):
    rows, cols = precip.shape
    peers, _, lines, _ = allbuf.shape
    depth = out.shape[2]
    direct = depth - extra
    owned = rec0.shape[0]
    layers = moist.shape[0] // owned
    n_col = lax.axis_size("col")
    row, col = lax.axis_index("row"), lax.axis_index("col")
    me = row * n_col + col
    barrier = pltpu.get_barrier_semaphore()
    part_rows = owned // chunks

    def fetch(c):
        part = pl.ds(c * part_rows * layers, part_rows * layers)
        return pltpu.make_async_copy(moisture.at[part], moist.at[part], read.at[c])

    def flush(c):
        part = pl.ds(c * part_rows * layers, part_rows * layers)
        return pltpu.make_async_copy(moist.at[part], saturation.at[part], write.at[c])

    def where_is(k):
        p = lax.rem(me + k, peers)
        return p, (p // n_col, lax.rem(p, n_col))

    def greet(k, _):
        pl.semaphore_signal(
            barrier, inc=1, device_id=where_is(k)[1], device_id_type=pl.DeviceIdType.MESH
        )
        return 0

    lax.fori_loop(1, peers, greet, 0)
    for c in range(chunks):
        fetch(c).start()

    def exchange(src, dst, send, recv, self_sem):
        def copy(k):
            p, place = where_is(k)
            return pltpu.make_async_remote_copy(
                src_ref=src(p),
                dst_ref=dst(me),
                send_sem=send.at[k],
                recv_sem=recv.at[k],
                device_id=place,
                device_id_type=pl.DeviceIdType.MESH,
            )

        here = pltpu.make_async_copy(src(me), dst(me), self_sem)

        def start(low, high):
            def body(k, _):
                copy(k).start()
                return 0

            lax.fori_loop(low, high, body, 0)

        def wait():
            def body(k, _):
                copy(k).wait()
                return 0

            lax.fori_loop(1, peers, body, 0)
            here.wait()

        return copy, here, start, wait

    for j in range(cols // LANES):
        part = pl.ds(j * LANES, LANES)
        infil[pl.ds(j * rows, rows), :] = precip[:, part] * land[:, part].astype(jnp.float32)
        sigs[pl.ds(j * rows, rows), :] = jax.nn.sigmoid(head[:, part])

    def pack(p):
        for r in range(depth):
            block = jnp.clip(src[p * depth + r], 0, infil.shape[0] - 1)
            out[p, 0, pl.ds(r, 1), :] = infil[pl.ds(block, 1), :]
            out[p, 1, pl.ds(r, 1), :] = sigs[pl.ds(block, 1), :]

    _, here0, start0, wait0 = exchange(
        lambda p: labels.at[p], lambda p: labs.at[p], send0, recv0, own.at[5]
    )
    copy1, here1, _, _ = exchange(
        lambda p: out.at[p], lambda p: allbuf.at[p, :, pl.ds(0, depth)], send1, recv1, own.at[0]
    )
    pl.semaphore_wait(barrier, peers - 1)
    here0.start()
    start0(1, peers)

    def ship(k, _):
        pack(where_is(k)[0])
        copy1(k).start()
        return 0

    lax.fori_loop(1, peers, ship, 0)
    pack(me)
    here1.start()

    steps, go, come = neighbours(row, col)
    east, south = cols - LANES, rows - 8
    for side, at in enumerate((0, south)):
        edge = pl.ds(at, 8)
        for f, field in enumerate(fixed_fields(head[edge, :], trans_coef[edge, :], land[edge, :])):
            row_out[side, pl.ds(8 * f, 8), :] = field
    for side, at in enumerate((0, east)):
        edge = pl.ds(at, LANES)
        keep = slice(0, 8) if side == 0 else slice(LANES - 8, LANES)
        for f, field in enumerate(fixed_fields(head[:, edge], trans_coef[:, edge], land[:, edge])):
            strip_out[side, pl.ds(8 * f, 8), :] = jnp.transpose(field)[keep]
    halo_dst = [from_row.at[0], from_row.at[1], strip_in.at[0], strip_in.at[1]] + [
        corner.at[c] for c in range(4)
    ]
    halo_src = [row_out.at[0], row_out.at[1], strip_out.at[0], strip_out.at[1]] + [
        row_out.at[c // 2, :, pl.ds((c % 2) * east, LANES)] for c in range(4)
    ]
    for k in range(8):

        @pl.when(jnp.logical_not(come[k]))
        def _(ref=halo_dst[k]):
            ref[...] = jnp.zeros(ref.shape, jnp.float32)

    def halo(k):
        return halo_copy(k, steps, row, col, halo_src, halo_dst, send_h, recv_h)

    each(go, lambda k: halo(k).start())

    group = 32

    def factor(c, _):
        fetch(c).wait()

        def body(i, _):
            base_row = pl.multiple_of(c * part_rows + i * group, group)
            at = pl.ds(base_row, group)
            recharge, terms = factor_rows(layers, moist, ksat, base_row, group)
            for ref, value in zip((rec0, rec_x, rec_y), recharge):
                ref[at, :] = value
            for k in range(layers):
                for ref, value in zip((moist, sx, sy), terms[k]):
                    ref[pl.ds(base_row * layers + k, group, stride=layers), :] = value
            return 0

        lax.fori_loop(0, part_rows // group, body, 0)
        return 0

    lax.fori_loop(0, chunks, factor, 0)
    wait0()

    shape = (peers, LANES)
    lane = lax.broadcasted_iota(jnp.int32, shape, 1)
    sub = lax.broadcasted_iota(jnp.int32, shape, 0)
    lab = labs[:, 0, :]
    count = labs[:, 1, :]
    over = jnp.maximum(count - direct, 0.0)
    tri = lax.broadcasted_iota(jnp.int32, (LANES, LANES), 0) < lax.broadcasted_iota(
        jnp.int32, (LANES, LANES), 1
    )
    base = jnp.dot(
        over, tri.astype(jnp.float32), precision=lax.Precision.HIGHEST,
        preferred_element_type=jnp.float32,
    )
    total = extra * peers
    before = (
        lax.broadcasted_iota(jnp.int32, (total, total), 1)
        < lax.broadcasted_iota(jnp.int32, (total, total), 0)
    ).astype(jnp.float32)

    def number(m):
        gap = m - sub
        return jnp.where(gap < 0, gap + peers, gap).astype(jnp.float32)

    def holds(j, first, many, t):
        j = j + float(t * peers)
        return jnp.where((first <= j) & (j < first + many), 1.0, 0.0)

    def prefix(v):
        return jnp.dot(before, v, preferred_element_type=jnp.float32)

    flane = lane.astype(jnp.float32)
    code = sub.astype(jnp.float32) * 8.0
    via = jnp.concatenate([holds(number(me), base, over, t) for t in range(extra)], axis=0)
    rank = prefix(via)
    codes = jnp.concatenate([code + float(t) for t in range(extra)], axis=0)
    lanes = jnp.concatenate([flane] * extra, axis=0)
    back = jnp.sum(via * (lanes * hop + rank), axis=1, keepdims=True)
    ret_v[...] = jnp.broadcast_to(back, (total, LANES)).astype(jnp.int32)
    pad = jnp.zeros((8 - hop, LANES), jnp.float32)
    picks = [
        jnp.sum(jnp.where(rank == float(e), via * codes, 0.0), axis=0, keepdims=True)
        for e in range(hop)
    ]
    src_v[...] = jnp.concatenate(picks + [pad], axis=0).astype(jnp.int32)
    mine = jnp.where(lane == me, 1.0, 0.0)
    first = jnp.sum(base * mine, axis=1, keepdims=True)
    many = jnp.sum(over * mine, axis=1, keepdims=True)
    inside = jnp.where(lane < peers, 1.0, 0.0)
    step = number(lane)
    took = [holds(step, first, many, t) * inside for t in range(extra)]
    value = []
    for t in range(extra):
        at = step + float(t * peers) - first
        v = jnp.zeros(shape, jnp.float32)
        for r in range(cap - direct):
            v = jnp.where(at == float(r), lab[:, direct + r : direct + r + 1] - float(owned), v)
        value.append(v)
    took = jnp.concatenate(took, axis=0)
    rank = prefix(took)
    value = jnp.concatenate(value, axis=0)
    picks = [
        jnp.sum(jnp.where(rank == float(e), took * value, 0.0), axis=0, keepdims=True)
        for e in range(hop)
    ]
    hopped = jnp.concatenate(picks + [pad], axis=0) + float(owned)
    slot2_v[...] = hopped.astype(jnp.int32)
    slots_v[...] = lab.astype(jnp.int32)
    columns = jnp.transpose(
        jnp.concatenate([hopped, jnp.zeros((LANES - 8, LANES), jnp.float32)], axis=0)
    )
    place = sub.astype(jnp.float32) * float(lines)
    for g in range(owned // LANES):
        want = flane + float(g * LANES)
        found = jnp.zeros(shape, jnp.float32)
        for r in range(direct):
            found = jnp.where(lab[:, r : r + 1] == want, place + float(r), found)
        for e in range(hop):
            found = jnp.where(
                columns[0:peers, e : e + 1] == want, place + float(depth + e), found
            )
        inv_v[pl.ds(g, 1), :] = jnp.sum(found, axis=0, keepdims=True).astype(jnp.int32)
    moves = [
        pltpu.make_async_copy(inv_v, inv_s, move.at[4]),
        pltpu.make_async_copy(src_v, src_s, move.at[0]),
        pltpu.make_async_copy(slots_v, slots_s, move.at[1]),
        pltpu.make_async_copy(slot2_v, slot2_s, move.at[2]),
        pltpu.make_async_copy(ret_v, ret_s, move.at[3]),
    ]
    for m in moves:
        m.start()
    g0[...] = jnp.zeros(g0.shape, jnp.float32)
    gx[...] = jnp.zeros(gx.shape, jnp.float32)
    gy[...] = jnp.zeros(gy.shape, jnp.float32)
    for m in moves:
        m.wait()

    def answer(q):
        for r in range(direct):
            slot = jnp.clip(slots_s[q, r], 0, owned - 1)
            g0[pl.ds(r, 1), :] = rec0[pl.ds(slot, 1), :]
            gx[pl.ds(r, 1), :] = rec_x[pl.ds(slot, 1), :]
            gy[pl.ds(r, 1), :] = rec_y[pl.ds(slot, 1), :]
        ans[q] = (
            g0[...]
            + allbuf[q, 0, pl.ds(0, depth), :] * gx[...]
            + allbuf[q, 1, pl.ds(0, depth), :] * gy[...]
        )

    here1.wait()
    answer(me)

    def receive(k, _):
        copy1(k).wait_recv()
        answer(lax.rem(me + peers - k, peers))
        return 0

    lax.fori_loop(1, peers, receive, 0)

    def pass_on(d, _):
        for e in range(hop):
            q = src_s[e, d]
            s = jnp.clip(q // 8, 0, peers - 1)
            t = jnp.clip(q - s * 8, 0, extra - 1)
            mid_out[d, pl.ds(e, 1), :] = allbuf[s, 0, pl.ds(direct + t, 1), :]
            mid_out[d, pl.ds(hop + e, 1), :] = allbuf[s, 1, pl.ds(direct + t, 1), :]
        return 0

    lax.fori_loop(0, peers, pass_on, 0)
    _, here2, start2, wait2 = exchange(
        lambda p: mid_out.at[p], lambda p: arr2.at[p], send2, recv2, own.at[1]
    )
    _, here3, start3, wait3 = exchange(
        lambda p: ans.at[p], lambda p: returned.at[p], send3, recv3, own.at[2]
    )
    _, here4, start4, wait4 = exchange(
        lambda p: ans2.at[p], lambda p: arr4.at[p], send4, recv4, own.at[3]
    )
    _, here5, start5, wait5 = exchange(
        lambda p: out5.at[p], lambda p: arr5.at[p], send5, recv5, own.at[4]
    )
    thirds = [1, peers // 3, 2 * peers // 3, peers]
    here2.start()
    start2(1, peers)
    here3.start()
    start3(thirds[0], thirds[1])
    wait2()

    def answer2(m, _):
        for e in range(hop):
            slot = jnp.clip(slot2_s[e, m], 0, owned - 1)
            inf, sg = arr2[m, pl.ds(e, 1), :], arr2[m, pl.ds(hop + e, 1), :]
            ans2[m, pl.ds(e, 1), :] = (
                rec0[pl.ds(slot, 1), :]
                + inf * rec_x[pl.ds(slot, 1), :]
                + sg * rec_y[pl.ds(slot, 1), :]
            )
            allbuf[m, 0, pl.ds(depth + e, 1), :] = inf
            allbuf[m, 1, pl.ds(depth + e, 1), :] = sg
        return 0

    lax.fori_loop(0, peers, answer2, 0)
    here4.start()
    start4(1, peers)
    start3(thirds[1], thirds[2])

    def finish(c, _):
        def body(i, _):
            for u in range(8):
                n = c * part_rows + i * 8 + u
                v = inv_s[n // LANES, lax.rem(n, LANES)]
                p = jnp.minimum(lax.shift_right_logical(v, bits), peers - 1)
                r = jnp.bitwise_and(v, lines - 1)
                inf = allbuf[p, 0, pl.ds(r, 1), :]
                sg = allbuf[p, 1, pl.ds(r, 1), :]
                at = pl.ds(pl.multiple_of(n * layers, layers), layers)
                moist[at, :] = moist[at, :] + inf * sx[at, :] + sg * sy[at, :]
            return 0

        lax.fori_loop(0, part_rows // 8, body, 0)
        flush(c).start()
        return 0

    bits = lines.bit_length() - 1
    lax.fori_loop(0, chunks // 2, finish, 0)
    wait4()

    def hand_back(s, _):
        for t in range(extra):
            at = jnp.clip(ret_s[t * peers + s, 0], 0, peers * hop - 1)
            d = at // hop
            out5[s, pl.ds(t, 1), :] = arr4[d, pl.ds(at - d * hop, 1), :]
        return 0

    lax.fori_loop(0, peers, hand_back, 0)
    here5.start()
    start5(1, peers)
    start3(thirds[2], thirds[3])
    lax.fori_loop(chunks // 2, chunks, finish, 0)

    def widest(m, most):
        n = number(m)
        seen = functools.reduce(lambda x, y: x + y, [holds(n, base, over, t) for t in range(extra)])
        return jnp.maximum(most, jnp.sum(seen, axis=0, keepdims=True))

    most = lax.fori_loop(0, peers, widest, jnp.zeros((1, LANES), jnp.float32))
    spread = jnp.max(jnp.sum(over, axis=1, keepdims=True), axis=0, keepdims=True)
    bad = jnp.maximum(
        jnp.where(jnp.max(most, axis=1, keepdims=True) > float(hop), 1.0, 0.0),
        jnp.where(spread > float(total), 1.0, 0.0),
    )
    fits[...] = jnp.broadcast_to(1.0 - bad, fits.shape)

    def landed(k):
        return pltpu.make_async_remote_copy(
            src_ref=halo_src[k],
            dst_ref=halo_dst[k],
            send_sem=send_h.at[k],
            recv_sem=recv_h.at[k],
            device_id=(row, col),
            device_id_type=pl.DeviceIdType.MESH,
        )

    each(go, lambda k: halo(k).wait_send())
    each(come, lambda k: landed(k).wait_recv())
    upper = lax.broadcasted_iota(jnp.int32, (8, LANES), 0) < 4
    near = lax.broadcasted_iota(jnp.int32, (8, LANES), 1) < LANES // 2
    for f in range(3):
        eight = pl.ds(8 * f, 8)
        for j in range(cols // LANES):
            part = pl.ds(j * LANES, LANES)
            mid_r[f, :, part] = jnp.where(upper, from_row[0, eight, part], from_row[1, eight, part])
        mid_c[f, pl.ds(rows, 8), :] = jnp.where(
            upper,
            jnp.where(near, corner[0, eight, :], corner[1, eight, :]),
            jnp.where(near, corner[2, eight, :], corner[3, eight, :]),
        )
        mid_c[f, pl.ds(0, rows), :] = jnp.transpose(
            jnp.concatenate(
                [
                    strip_in[0, eight, :],
                    jnp.zeros((LANES - 16, rows), jnp.float32),
                    strip_in[1, eight, :],
                ],
                axis=0,
            )
        )
    wait5()
    for i in range(total):
        returned[peers + i // depth, pl.ds(i % depth, 1), :] = arr5[
            i // extra, pl.ds(i % extra, 1), :
        ]
    wait3()

    def sent(k, _):
        copy1(k).wait_send()
        return 0

    lax.fori_loop(1, peers, sent, 0)
    for c in range(chunks):
        flush(c).wait()


def pack_kernel(peers, per_peer, src, labels, precip, head, land, out, infil, heads):
    rows, cols = precip.shape
    for j in range(cols // LANES):
        part = pl.ds(j * LANES, LANES)
        infil[pl.ds(j * rows, rows), :] = precip[:, part] * land[:, part].astype(jnp.float32)
        heads[pl.ds(j * rows, rows), :] = head[:, part]

    def body(p, _):
        for r in range(per_peer):
            block = src[p * per_peer + r]
            out[p, pl.ds(r, 1), :] = infil[pl.ds(block, 1), :]
            out[p, pl.ds(per_peer + r, 1), :] = heads[pl.ds(block, 1), :]
        out[p, pl.ds(2 * per_peer, 8), :] = jnp.broadcast_to(labels[pl.ds(p, 1), :], (8, LANES))
        return 0

    lax.fori_loop(0, peers, body, 0)


def owner_kernel(
    peers, per_peer, slots, arrived, rec0, rec_x, rec_y, answer, infil, sig, own_i, own_h, rec
):
    owned = rec0.shape[0]

    def scatter(p, _):
        for r in range(per_peer):
            slot = slots[p * per_peer + r]
            own_i[pl.ds(slot, 1), :] = arrived[p, pl.ds(r, 1), :]
            own_h[pl.ds(slot, 1), :] = arrived[p, pl.ds(per_peer + r, 1), :]
        return 0

    lax.fori_loop(0, peers, scatter, 0)
    rec[pl.ds(owned, 8), :] = jnp.zeros((8, LANES), jnp.float32)

    def combine(g, _):
        part = pl.ds(g * 64, 64)
        inf = own_i[part, :]
        sg = jax.nn.sigmoid(own_h[part, :])
        infil[part, :] = inf
        sig[part, :] = sg
        rec[part, :] = rec0[part, :] + inf * rec_x[part, :] + sg * rec_y[part, :]
        return 0

    lax.fori_loop(0, owned // 64, combine, 0)

    def gather(p, _):
        for r in range(per_peer):
            slot = slots[p * per_peer + r]
            answer[p, pl.ds(r, 1), :] = rec[pl.ds(slot, 1), :]
        return 0

    lax.fori_loop(0, peers, gather, 0)


def factor_kernel(layers, group, moist, ksat, s0, sx, sy, rec0, rec_x, rec_y):
    def body(step, _):
        base_row = step * group
        rows = pl.ds(pl.multiple_of(base_row, group), group)
        recharge, terms = factor_rows(layers, moist, ksat, base_row, group)
        for ref, value in zip((rec0, rec_x, rec_y), recharge):
            ref[rows, :] = value
        for k in range(layers):
            for ref, value in zip((s0, sx, sy), terms[k]):
                ref[k, rows, :] = value
        return 0

    lax.fori_loop(0, ksat.shape[0] // group, body, 0)


def saturation_kernel(layers, s0, sx, sy, infil, sig, out):
    count = infil.shape[0]
    group = 32

    def body(step, _):
        rows = pl.ds(pl.multiple_of(step * group, group), group)
        inf = infil[rows, :]
        sg = sig[rows, :]
        for k in range(layers):
            out[pl.ds(step * group * layers + k, group, stride=layers), :] = (
                s0[k, rows, :] + inf * sx[k, rows, :] + sg * sy[k, rows, :]
            )
        return 0

    lax.fori_loop(0, count // group, body, 0)


def relax_kernel(
    position, returned, head, trans_coef, land, mid_r, mid_c, out,
    t_ref, s_ref, fu, fd, fl, fr, a, b, sorted_rows, strip_out, from_row, strip_in, corner, send_sem, recv_sem,
):
    rows, cols = head.shape
    high, wide = t_ref.shape
    row, col = lax.axis_index("row"), lax.axis_index("col")
    n_row, n_col = lax.axis_size("row"), lax.axis_size("col")
    up, down = row > 0, row < n_row - 1
    left, right = col > 0, col < n_col - 1
    east = cols - LANES
    south = rows - 8
    links = [
        (up, -1, 0, s_ref.at[pl.ds(0, 8), pl.ds(0, cols)], from_row.at[0]),
        (down, 1, 0, s_ref.at[pl.ds(south, 8), pl.ds(0, cols)], from_row.at[1]),
        (left, 0, -1, strip_out.at[0], strip_in.at[0]),
        (right, 0, 1, strip_out.at[1], strip_in.at[1]),
        (up & left, -1, -1, s_ref.at[pl.ds(0, 8), pl.ds(0, LANES)], corner.at[0]),
        (up & right, -1, 1, s_ref.at[pl.ds(0, 8), pl.ds(east, LANES)], corner.at[1]),
        (down & left, 1, -1, s_ref.at[pl.ds(south, 8), pl.ds(0, LANES)], corner.at[2]),
        (down & right, 1, 1, s_ref.at[pl.ds(south, 8), pl.ds(east, LANES)], corner.at[3]),
    ]
    come = [down, up, right, left, down & right, down & left, up & right, up & left]
    barrier = pltpu.get_barrier_semaphore()

    def each(flags, act):
        for k, flag in enumerate(flags):
            pl.when(flag)(functools.partial(act, k))

    def copy(k):
        _, dr, dc, src, dst = links[k]
        return pltpu.make_async_remote_copy(
            src_ref=src,
            dst_ref=dst,
            send_sem=send_sem.at[k],
            recv_sem=recv_sem.at[k],
            device_id=(row + dr, col + dc),
            device_id_type=pl.DeviceIdType.MESH,
        )

    def copy_in(k):
        _, _, _, src, dst = links[k]
        return pltpu.make_async_remote_copy(
            src_ref=src,
            dst_ref=dst,
            send_sem=send_sem.at[k],
            recv_sem=recv_sem.at[k],
            device_id=(row, col),
            device_id_type=pl.DeviceIdType.MESH,
        )

    go = [link[0] for link in links]

    def greet(k):
        pl.semaphore_signal(
            barrier,
            inc=1,
            device_id=(row + links[k][1], col + links[k][2]),
            device_id_type=pl.DeviceIdType.MESH,
        )

    each(go, greet)
    for k in range(8):
        ref = [from_row.at[0], from_row.at[1], strip_in.at[0], strip_in.at[1]] + [
            corner.at[c] for c in range(4)
        ]

        @pl.when(jnp.logical_not(come[k]))
        def _(ref=ref[k]):
            ref[...] = jnp.zeros(ref.shape, jnp.float32)

    for j in range(cols // LANES):
        part = slice(j * LANES, (j + 1) * LANES)

        def body(g, _, j=j, part=part):
            base = g * 32
            got = [returned[pl.ds(position[j * rows + base + u], 1), :] for u in range(32)]
            for u in range(32):
                sorted_rows[pl.ds(j * rows + base + u, 1), :] = got[u]
            return 0

        lax.fori_loop(0, rows // 32, body, 0)
        s_ref[0:rows, part] = (
            store_rate * (head[:, part] * land[:, part].astype(jnp.float32))
            + recharge_gain * sorted_rows[j * rows : (j + 1) * rows, :]
        )
    strip_out[0] = jnp.transpose(s_ref[0:rows, 0:LANES])[0:8]
    strip_out[1] = jnp.transpose(s_ref[0:rows, east:cols])[LANES - 8 : LANES]

    def count(flags):
        return functools.reduce(lambda x, y: x + y, [f.astype(jnp.int32) for f in flags])

    pl.semaphore_wait(barrier, count(go))
    each(go, lambda k: copy(k).start())

    for f, (ref, centre) in enumerate(
        zip((t_ref, a, b), fixed_fields(head[...], trans_coef[...], land[...]))
    ):
        ref[0:rows, 0:cols] = centre
        ref[rows:high, 0:cols] = mid_r[f]
        ref[:, cols:wide] = mid_c[f]
    for g in range(wide // LANES):
        part = slice(g * LANES, (g + 1) * LANES)
        lo = slice((g - 1) % (wide // LANES) * LANES, (g - 1) % (wide // LANES) * LANES + LANES)
        hi = slice((g + 1) % (wide // LANES) * LANES, (g + 1) % (wide // LANES) * LANES + LANES)
        lane = lax.broadcasted_iota(jnp.int32, (high, LANES), 1)
        t = t_ref[:, part]
        tu = 0.5 * (t + pltpu.roll(t, 1, 0))
        td = 0.5 * (t + pltpu.roll(t, high - 1, 0))
        tl = jnp.where(lane == 0, pltpu.roll(t_ref[:, lo], 1, 1), pltpu.roll(t, 1, 1))
        tr = jnp.where(
            lane == LANES - 1,
            pltpu.roll(t_ref[:, hi], LANES - 1, 1),
            pltpu.roll(t, LANES - 1, 1),
        )
        lf = 0.5 * (t + tl)
        rt = 0.5 * (t + tr)
        inv = b[:, part] / (store_rate + (tu + td + lf + rt))
        fu[:, part] = tu * inv
        fd[:, part] = td * inv
        fl[:, part] = lf * inv
        fr[:, part] = rt * inv
        b[:, part] = inv

    each(go, lambda k: copy(k).wait_send())
    each(come, lambda k: copy_in(k).wait_recv())

    first = lax.broadcasted_iota(jnp.int32, (8, LANES), 0) < 4
    near = lax.broadcasted_iota(jnp.int32, (8, LANES), 1) < LANES // 2
    for j in range(cols // LANES):
        part = slice(j * LANES, (j + 1) * LANES)
        s_ref[rows:high, part] = jnp.where(first, from_row[0, :, part], from_row[1, :, part])
    s_ref[rows:high, cols:wide] = jnp.where(
        first,
        jnp.where(near, corner[0], corner[1]),
        jnp.where(near, corner[2], corner[3]),
    )
    s_ref[0:rows, cols:wide] = jnp.transpose(
        jnp.concatenate(
            [strip_in[0], jnp.zeros((LANES - 16, rows), jnp.float32), strip_in[1]], axis=0
        )
    )
    for g in range(wide // LANES):
        part = slice(g * LANES, (g + 1) * LANES)
        s_ref[:, part] = s_ref[:, part] * b[:, part]
    now, later = a, b
    for sweep in range(SWEEPS):
        last = sweep == SWEEPS - 1
        for g in range(wide // LANES):
            if last and g * LANES >= cols:
                continue
            part = slice(g * LANES, (g + 1) * LANES)
            lo = (g - 1) % (wide // LANES) * LANES
            hi = (g + 1) % (wide // LANES) * LANES
            lane = lax.broadcasted_iota(jnp.int32, (high, LANES), 1)
            x = now[:, part]
            xl = jnp.where(
                lane == 0, pltpu.roll(now[:, lo : lo + LANES], 1, 1), pltpu.roll(x, 1, 1)
            )
            xr = jnp.where(
                lane == LANES - 1,
                pltpu.roll(now[:, hi : hi + LANES], LANES - 1, 1),
                pltpu.roll(x, LANES - 1, 1),
            )
            y = s_ref[:, part] + fu[:, part] * pltpu.roll(x, 1, 0)
            y = y + fd[:, part] * pltpu.roll(x, high - 1, 0)
            y = y + (fl[:, part] * xl + fr[:, part] * xr)
            if last:
                out[:, part] = y[0:rows]
            else:
                later[:, part] = y
        now, later = later, now


def on_device(precip, head, trans_coef, land, dest, moisture, ksat):
    tile_rows, tile_cols = precip.shape
    n_col = lax.axis_size("col")
    peers = lax.axis_size("row") * n_col
    me = lax.axis_index("row") * n_col + lax.axis_index("col")
    owned, layers, _ = moisture.shape
    blocks = tile_rows * tile_cols // LANES
    cap = (2 * blocks + peers - 1) // peers
    extra, hop = 2, 4
    depth = (19 * blocks // (16 * peers) + 1 + 7) // 8 * 8
    direct = depth - extra
    lines = 1 << (depth + hop - 1).bit_length()

    target = dest.T.reshape(blocks)
    owner = target // owned
    slot = target - owner * owned
    all_peers = jnp.arange(peers, dtype=jnp.int32)
    one_hot = owner[:, None] == all_peers[None, :]
    order = jnp.arange(blocks, dtype=jnp.int32)
    earlier = (order[None, :] < order[:, None]).astype(jnp.bfloat16)
    counts = jnp.dot(earlier, one_hot.astype(jnp.bfloat16), preferred_element_type=jnp.float32)
    sums = jnp.sum(one_hot.astype(jnp.float32), axis=0)
    over = jnp.maximum(sums - direct, 0.0)
    base = jnp.sum(jnp.where(all_peers[:, None] < all_peers[None, :], over[:, None], 0.0), axis=0)
    rank = jnp.sum(jnp.where(one_hot, counts, 0.0), axis=1).astype(jnp.int32)
    number = jnp.sum(jnp.where(one_hot, counts + base[None, :] - direct, 0.0), axis=1).astype(
        jnp.int32
    )
    spread = rank >= direct
    via = (jnp.maximum(number, 0) + me) % peers
    turn = jnp.clip(number // peers, 0, extra - 1)
    position = jnp.where(
        spread, peers * depth + via * extra + turn, owner * depth + rank
    )
    place = jnp.where(spread, via, owner)
    row_of = jnp.where(spread, direct + turn, rank)

    def table(where, row, width, value):
        hot = (where[:, None] == all_peers[None, :]).astype(jnp.float32)
        at = row[:, None] == jnp.arange(width, dtype=jnp.int32)[None, :]
        return lax.dot_general(
            hot,
            jnp.where(at, value.astype(jnp.float32)[:, None], 0.0),
            (((0,), (0,)), ((), ())),
            precision=lax.Precision.HIGHEST,
            preferred_element_type=jnp.float32,
        )

    source_of = jnp.minimum(table(place, row_of, depth, order).astype(jnp.int32), blocks - 1)
    label = table(owner, rank, LANES, slot - owned) + float(owned)
    sent = jnp.broadcast_to(jnp.pad(sums, (0, LANES - peers))[None, :], (peers, LANES))

    sources, labels, position, owner, rank = lax.optimization_barrier(
        (source_of.reshape(peers * depth), jnp.stack([label, sent], axis=1), position, owner, rank)
    )
    flat = moisture.reshape(owned * layers, LANES)
    vm = lambda *shape: pltpu.VMEM(shape, jnp.float32)
    iv = lambda *shape: pltpu.VMEM(shape, jnp.int32)
    sm = lambda *shape: pltpu.SMEM(shape, jnp.int32)
    dma = lambda n: pltpu.SemaphoreType.DMA((n,))
    chunks = 8
    tail = (peers * extra + depth - 1) // depth
    high, wide = tile_rows + 2 * SWEEPS, tile_cols + LANES
    returned, stepped, fits, mid_r, mid_c = pl.pallas_call(
        functools.partial(column_kernel, cap, extra, hop, chunks),
        out_shape=[
            f32(peers + tail, depth, LANES),
            f32(owned * layers, LANES),
            f32(1, 1),
            f32(3, 2 * SWEEPS, tile_cols),
            f32(3, high, LANES),
        ],
        in_specs=[SM] + [VM] * 5 + [pl.BlockSpec(memory_space=pl.ANY), VM],
        out_specs=[VM, pl.BlockSpec(memory_space=pl.ANY), VM, VM, VM],
        scratch_shapes=[
            vm(blocks, LANES),
            vm(blocks, LANES),
            vm(peers, 2, depth, LANES),
            vm(peers, 2, lines, LANES),
            vm(peers, 2, LANES),
        ]
        + [vm(owned * layers, LANES)] * 3
        + [vm(owned, LANES)] * 3
        + [
            vm(peers, 2 * hop, LANES),
            vm(peers, 2 * hop, LANES),
            vm(peers, depth, LANES),
            vm(peers, hop, LANES),
            vm(peers, hop, LANES),
            vm(peers, extra, LANES),
            vm(peers, extra, LANES),
            vm(depth, LANES),
            vm(depth, LANES),
            vm(depth, LANES),
            iv(8, LANES),
            iv(extra * peers, LANES),
            iv(peers, LANES),
            iv(8, LANES),
            iv(owned // LANES, LANES),
            vm(2, 24, tile_cols),
            vm(2, 24, tile_rows),
            vm(2, 24, tile_cols),
            vm(2, 24, tile_rows),
            vm(4, 24, LANES),
            sm(peers, LANES),
            sm(8, LANES),
            sm(8, LANES),
            sm(extra * peers, LANES),
            sm(owned // LANES, LANES),
            dma(5),
            dma(chunks),
            dma(chunks),
        ]
        + [dma(peers)] * 12
        + [dma(6), dma(8), dma(8)],
        compiler_params=pltpu.CompilerParams(
            collective_id=4, has_side_effects=True, vmem_limit_bytes=58 * 2**20
        ),
    )(sources, labels, precip, head, trans_coef, land, flat, ksat)


    def relax(identity, at, rows):
        return pl.pallas_call(
            relax_kernel,
            out_shape=f32(tile_rows, tile_cols),
            in_specs=[SM] + [VM] * 6,
            out_specs=VM,
            scratch_shapes=[pltpu.VMEM((high, wide), jnp.float32)] * 8
            + [
                pltpu.VMEM((blocks, LANES), jnp.float32),
                pltpu.VMEM((2, 8, tile_rows), jnp.float32),
                pltpu.VMEM((2, 8, tile_cols), jnp.float32),
                pltpu.VMEM((2, 8, tile_rows), jnp.float32),
                pltpu.VMEM((4, 8, LANES), jnp.float32),
                pltpu.SemaphoreType.DMA((8,)),
                pltpu.SemaphoreType.DMA((8,)),
            ],
            compiler_params=pltpu.CompilerParams(collective_id=identity, has_side_effects=True),
        )(at, rows.reshape(-1, LANES), head, trans_coef, land, mid_r, mid_c)

    def hopped():
        return stepped.reshape(owned, layers, LANES), relax(1, position, returned)

    def whole():
        step = 128
        layered = pl.BlockSpec((layers, step, LANES), lambda i: (0, i, 0))
        single = pl.BlockSpec((step, LANES), lambda i: (i, 0))
        natural = pl.BlockSpec((step * layers, LANES), lambda i: (i, 0))
        s0, sx, sy, rec0, rec_x, rec_y = pl.pallas_call(
            functools.partial(factor_kernel, layers, 32),
            grid=(owned // step,),
            out_shape=[f32(layers, owned, LANES)] * 3 + [f32(owned, LANES)] * 3,
            in_specs=[natural, single],
            out_specs=[layered] * 3 + [single] * 3,
        )(flat, ksat)
        slots_of = table(owner, rank, cap, order).astype(jnp.int32).reshape(peers * cap)
        outgoing = pl.pallas_call(
            functools.partial(pack_kernel, peers, cap),
            out_shape=f32(peers, 2 * cap + 8, LANES),
            in_specs=[SM, VM, VM, VM, VM],
            out_specs=VM,
            scratch_shapes=[pltpu.VMEM((blocks, LANES), jnp.float32)] * 2,
        )(slots_of, labels[:, 0], precip, head, land)
        arrived = lax.all_to_all(outgoing, ("row", "col"), split_axis=0, concat_axis=0, tiled=True)
        places = arrived[:, 2 * cap, :cap].astype(jnp.int32).reshape(peers * cap)
        answer, infil, sig = pl.pallas_call(
            functools.partial(owner_kernel, peers, cap),
            out_shape=[f32(peers, cap, LANES), f32(owned, LANES), f32(owned, LANES)],
            in_specs=[SM, VM, VM, VM, VM],
            out_specs=[VM] * 3,
            scratch_shapes=[pltpu.VMEM((owned + 8, LANES), jnp.float32)] * 3,
        )(places, arrived, rec0, rec_x, rec_y)
        back = lax.all_to_all(answer, ("row", "col"), split_axis=0, concat_axis=0, tiled=True)
        saturation = pl.pallas_call(
            functools.partial(saturation_kernel, layers),
            grid=(owned // step,),
            out_shape=f32(owned * layers, LANES),
            in_specs=[layered] * 3 + [single] * 2,
            out_specs=natural,
        )(s0, sx, sy, infil, sig)
        return saturation.reshape(owned, layers, LANES), relax(2, owner * cap + rank, back)

    return lax.cond(fits.reshape(()) > 0.5, hopped, whole)


def solution(mesh):
    tile = P("row", "col")
    placed = (
        tile,
        tile,
        tile,
        tile,
        tile,
        P(("row", "col"), None, None),
        P(("row", "col"), None),
    )
    return jax.shard_map(
        on_device,
        mesh=mesh,
        in_specs=placed,
        out_specs=(P(("row", "col"), None, None), P("row", "col")),
        check_vma=False,
    )
```

```python
import functools
import math

import jax
import jax.numpy as jnp
from jax import lax
from jax.experimental import pallas as pl
from jax.experimental.pallas import tpu as pltpu
from jax.sharding import PartitionSpec as P

SWEEPS = 4
LANES = 128

layer_depth = 0.1
step_ratio = 0.1
residual_water = 0.05
pore_range = 0.4
diff_length = 0.5
couple_rate = 0.05
recharge_gain = 20.0
store_rate = 0.2

VM = pl.BlockSpec(memory_space=pltpu.VMEM)
SM = pl.BlockSpec(memory_space=pltpu.SMEM)


def f32(*shape):
    return jax.ShapeDtypeStruct(shape, jnp.float32)


def factor_rows(layers, moist, ksat, base_row, group):
    rows = pl.ds(pl.multiple_of(base_row, group), group)
    ks = ksat[rows, :]
    ratios, reds, xs = [], [], []
    before = None
    for k in range(layers):
        m = moist[pl.ds(base_row * layers + k, group, stride=layers), :]
        w = (m - residual_water) * (1.0 / pore_range)
        s = ks * math.exp(-(k + 0.5) * layer_depth)
        sw2 = s * (w * w)
        hs = sw2 * (1.5 / pore_range)
        d = s * (0.2 * diff_length / (2.0 * layer_depth)) + sw2 * (
            diff_length / (2.0 * layer_depth)
        )
        hc = 0.5 * (sw2 * w)
        cur = (m, hs, d, hc)
        if before is None:
            before = cur
            g_up = q_up = nsub = None
            continue
        m0, hs0, d0, hc0 = before
        g = d0 + d
        q = (hc0 + hc) - g * (m - m0)
        if g_up is None:
            pivot = step_ratio + g + hs0
            inv = 1.0 / pivot
            reds.append(-q * inv)
            xs.append(inv)
        else:
            pivot = step_ratio + g_up + g - nsub * ratios[-1]
            inv = 1.0 / pivot
            reds.append(((q_up - q) + nsub * reds[-1]) * inv)
            xs.append(nsub * inv * xs[-1])
        ratios.append((g - hs) * inv)
        nsub = hs0 + g
        g_up, q_up = g, q
        before = cur
    m, hs, d, hc = before
    bottom = 2.0 * hc + couple_rate * (m - residual_water)
    pivot = step_ratio + g_up + hs + couple_rate - nsub * ratios[-1]
    inv = 1.0 / pivot
    change = ((q_up - bottom) + nsub * reds[-1]) * inv
    cx = nsub * inv * xs[-1]
    cy = (couple_rate * pore_range) * inv
    gain = 2.0 * hs + couple_rate
    recharge = (
        bottom + gain * change,
        gain * cx,
        gain * cy - couple_rate * pore_range,
    )
    unit = 1.0 / pore_range
    terms = [None] * layers
    for k in range(layers - 1, -1, -1):
        if k < layers - 1:
            change = reds[k] + ratios[k] * change
            cx = xs[k] + ratios[k] * cx
            cy = ratios[k] * cy
        m = moist[pl.ds(base_row * layers + k, group, stride=layers), :]
        terms[k] = ((m + change - residual_water) * unit, cx * unit, cy * unit)
    return recharge, terms


def fixed_fields(head, trans_coef, land):
    share = land.astype(jnp.float32)
    return trans_coef * (1.0 + 0.5 * jnp.tanh(head)), head * share, share


def neighbours(row, col):
    n_row, n_col = lax.axis_size("row"), lax.axis_size("col")
    up, down = row > 0, row < n_row - 1
    left, right = col > 0, col < n_col - 1
    steps = [(-1, 0), (1, 0), (0, -1), (0, 1), (-1, -1), (-1, 1), (1, -1), (1, 1)]
    go = [up, down, left, right, up & left, up & right, down & left, down & right]
    come = [down, up, right, left, down & right, down & left, up & right, up & left]
    return steps, go, come


def each(flags, act):
    for k, flag in enumerate(flags):
        pl.when(flag)(functools.partial(act, k))


def halo_copy(k, steps, row, col, src, dst, send_sem, recv_sem):
    return pltpu.make_async_remote_copy(
        src_ref=src[k],
        dst_ref=dst[k],
        send_sem=send_sem.at[k],
        recv_sem=recv_sem.at[k],
        device_id=(row + steps[k][0], col + steps[k][1]),
        device_id_type=pl.DeviceIdType.MESH,
    )


def column_kernel(
    cap, extra, hop, chunks, src, position, labels, precip, head, trans_coef, land, moisture, ksat,
    s_ref, saturation, fits, mid_r, mid_c, returned,
    infil, sigs, out, allbuf, labs, moist, sx, sy, rec0, rec_x, rec_y,
    mid_out, arr2, ans, ans2, arr4, out5, arr5, g0, gx, gy, src_v, ret_v, slots_v, slot2_v, inv_v,
    row_out, strip_out, from_row, strip_in, corner,
    slots_s, slot2_s, src_s, ret_s, inv_s,
    move, read, write, send0, recv0, send1, recv1, send2, recv2, send3, recv3, send4, recv4, send5, recv5, own,
    send_h, recv_h, *for_source,
):
    rows, cols = precip.shape
    peers, _, lines, _ = allbuf.shape
    depth = out.shape[2]
    direct = depth - extra
    owned = rec0.shape[0]
    layers = moist.shape[0] // owned
    n_col = lax.axis_size("col")
    row, col = lax.axis_index("row"), lax.axis_index("col")
    me = row * n_col + col
    barrier = pltpu.get_barrier_semaphore()
    part_rows = owned // chunks

    def fetch(c):
        part = pl.ds(c * part_rows * layers, part_rows * layers)
        return pltpu.make_async_copy(moisture.at[part], moist.at[part], read.at[c])

    def flush(c):
        part = pl.ds(c * part_rows * layers, part_rows * layers)
        return pltpu.make_async_copy(moist.at[part], saturation.at[part], write.at[c])

    def where_is(k):
        p = lax.rem(me + k, peers)
        return p, (p // n_col, lax.rem(p, n_col))

    def greet(k, _):
        pl.semaphore_signal(
            barrier, inc=1, device_id=where_is(k)[1], device_id_type=pl.DeviceIdType.MESH
        )
        return 0

    lax.fori_loop(1, peers, greet, 0)
    for c in range(chunks):
        fetch(c).start()

    def exchange(src, dst, send, recv, self_sem):
        def copy(k):
            p, place = where_is(k)
            return pltpu.make_async_remote_copy(
                src_ref=src(p),
                dst_ref=dst(me),
                send_sem=send.at[k],
                recv_sem=recv.at[k],
                device_id=place,
                device_id_type=pl.DeviceIdType.MESH,
            )

        here = pltpu.make_async_copy(src(me), dst(me), self_sem)

        def start(low, high):
            def body(k, _):
                copy(k).start()
                return 0

            lax.fori_loop(low, high, body, 0)

        def wait():
            def body(k, _):
                copy(k).wait()
                return 0

            lax.fori_loop(1, peers, body, 0)
            here.wait()

        return copy, here, start, wait

    for j in range(cols // LANES):
        part = pl.ds(j * LANES, LANES)
        infil[pl.ds(j * rows, rows), :] = precip[:, part] * land[:, part].astype(jnp.float32)
        sigs[pl.ds(j * rows, rows), :] = jax.nn.sigmoid(head[:, part])

    def pack(p):
        for r in range(depth):
            block = jnp.clip(src[p * depth + r], 0, infil.shape[0] - 1)
            out[p, 0, pl.ds(r, 1), :] = infil[pl.ds(block, 1), :]
            out[p, 1, pl.ds(r, 1), :] = sigs[pl.ds(block, 1), :]

    _, here0, start0, wait0 = exchange(
        lambda p: labels.at[p], lambda p: labs.at[p], send0, recv0, own.at[5]
    )
    copy1, here1, _, _ = exchange(
        lambda p: out.at[p], lambda p: allbuf.at[p, :, pl.ds(0, depth)], send1, recv1, own.at[0]
    )
    pl.semaphore_wait(barrier, peers - 1)
    here0.start()
    start0(1, peers)

    def ship(k, _):
        pack(where_is(k)[0])
        copy1(k).start()
        return 0

    lax.fori_loop(1, peers, ship, 0)
    pack(me)
    here1.start()

    steps, go, come = neighbours(row, col)
    east, south = cols - LANES, rows - 8
    for side, at in enumerate((0, south)):
        edge = pl.ds(at, 8)
        for f, field in enumerate(fixed_fields(head[edge, :], trans_coef[edge, :], land[edge, :])):
            row_out[side, pl.ds(8 * f, 8), :] = field
    for side, at in enumerate((0, east)):
        edge = pl.ds(at, LANES)
        keep = slice(0, 8) if side == 0 else slice(LANES - 8, LANES)
        for f, field in enumerate(fixed_fields(head[:, edge], trans_coef[:, edge], land[:, edge])):
            strip_out[side, pl.ds(8 * f, 8), :] = jnp.transpose(field)[keep]
    halo_dst = [from_row.at[0], from_row.at[1], strip_in.at[0], strip_in.at[1]] + [
        corner.at[c] for c in range(4)
    ]
    halo_src = [row_out.at[0], row_out.at[1], strip_out.at[0], strip_out.at[1]] + [
        row_out.at[c // 2, :, pl.ds((c % 2) * east, LANES)] for c in range(4)
    ]
    for k in range(8):

        @pl.when(jnp.logical_not(come[k]))
        def _(ref=halo_dst[k]):
            ref[...] = jnp.zeros(ref.shape, jnp.float32)

    def halo(k):
        return halo_copy(k, steps, row, col, halo_src, halo_dst, send_h, recv_h)

    each(go, lambda k: halo(k).start())

    group = 32

    def factor(c, _):
        fetch(c).wait()

        def body(i, _):
            base_row = pl.multiple_of(c * part_rows + i * group, group)
            at = pl.ds(base_row, group)
            recharge, terms = factor_rows(layers, moist, ksat, base_row, group)
            for ref, value in zip((rec0, rec_x, rec_y), recharge):
                ref[at, :] = value
            for k in range(layers):
                for ref, value in zip((moist, sx, sy), terms[k]):
                    ref[pl.ds(base_row * layers + k, group, stride=layers), :] = value
            return 0

        lax.fori_loop(0, part_rows // group, body, 0)
        return 0

    lax.fori_loop(0, chunks, factor, 0)
    wait0()

    shape = (peers, LANES)
    lane = lax.broadcasted_iota(jnp.int32, shape, 1)
    sub = lax.broadcasted_iota(jnp.int32, shape, 0)
    lab = labs[:, 0, :]
    count = labs[:, 1, :]
    over = jnp.maximum(count - direct, 0.0)
    tri = lax.broadcasted_iota(jnp.int32, (LANES, LANES), 0) < lax.broadcasted_iota(
        jnp.int32, (LANES, LANES), 1
    )
    base = jnp.dot(
        over, tri.astype(jnp.float32), precision=lax.Precision.HIGHEST,
        preferred_element_type=jnp.float32,
    )
    total = extra * peers
    before = (
        lax.broadcasted_iota(jnp.int32, (total, total), 1)
        < lax.broadcasted_iota(jnp.int32, (total, total), 0)
    ).astype(jnp.float32)

    def number(m):
        gap = m - sub
        return jnp.where(gap < 0, gap + peers, gap).astype(jnp.float32)

    def holds(j, first, many, t):
        j = j + float(t * peers)
        return jnp.where((first <= j) & (j < first + many), 1.0, 0.0)

    def prefix(v):
        return jnp.dot(before, v, preferred_element_type=jnp.float32)

    flane = lane.astype(jnp.float32)
    code = sub.astype(jnp.float32) * 8.0
    via = jnp.concatenate([holds(number(me), base, over, t) for t in range(extra)], axis=0)
    rank = prefix(via)
    codes = jnp.concatenate([code + float(t) for t in range(extra)], axis=0)
    lanes = jnp.concatenate([flane] * extra, axis=0)
    back = jnp.sum(via * (lanes * hop + rank), axis=1, keepdims=True)
    ret_v[...] = jnp.broadcast_to(back, (total, LANES)).astype(jnp.int32)
    pad = jnp.zeros((8 - hop, LANES), jnp.float32)
    picks = [
        jnp.sum(jnp.where(rank == float(e), via * codes, 0.0), axis=0, keepdims=True)
        for e in range(hop)
    ]
    src_v[...] = jnp.concatenate(picks + [pad], axis=0).astype(jnp.int32)
    mine = jnp.where(lane == me, 1.0, 0.0)
    first = jnp.sum(base * mine, axis=1, keepdims=True)
    many = jnp.sum(over * mine, axis=1, keepdims=True)
    inside = jnp.where(lane < peers, 1.0, 0.0)
    step = number(lane)
    took = [holds(step, first, many, t) * inside for t in range(extra)]
    value = []
    for t in range(extra):
        at = step + float(t * peers) - first
        v = jnp.zeros(shape, jnp.float32)
        for r in range(cap - direct):
            v = jnp.where(at == float(r), lab[:, direct + r : direct + r + 1] - float(owned), v)
        value.append(v)
    took = jnp.concatenate(took, axis=0)
    rank = prefix(took)
    value = jnp.concatenate(value, axis=0)
    picks = [
        jnp.sum(jnp.where(rank == float(e), took * value, 0.0), axis=0, keepdims=True)
        for e in range(hop)
    ]
    hopped = jnp.concatenate(picks + [pad], axis=0) + float(owned)
    slot2_v[...] = hopped.astype(jnp.int32)
    slots_v[...] = lab.astype(jnp.int32)
    columns = jnp.transpose(
        jnp.concatenate([hopped, jnp.zeros((LANES - 8, LANES), jnp.float32)], axis=0)
    )
    place = sub.astype(jnp.float32) * float(lines)
    for g in range(owned // LANES):
        want = flane + float(g * LANES)
        found = jnp.zeros(shape, jnp.float32)
        for r in range(direct):
            found = jnp.where(lab[:, r : r + 1] == want, place + float(r), found)
        for e in range(hop):
            found = jnp.where(
                columns[0:peers, e : e + 1] == want, place + float(depth + e), found
            )
        inv_v[pl.ds(g, 1), :] = jnp.sum(found, axis=0, keepdims=True).astype(jnp.int32)
    moves = [
        pltpu.make_async_copy(inv_v, inv_s, move.at[4]),
        pltpu.make_async_copy(src_v, src_s, move.at[0]),
        pltpu.make_async_copy(slots_v, slots_s, move.at[1]),
        pltpu.make_async_copy(slot2_v, slot2_s, move.at[2]),
        pltpu.make_async_copy(ret_v, ret_s, move.at[3]),
    ]
    for m in moves:
        m.start()
    g0[...] = jnp.zeros(g0.shape, jnp.float32)
    gx[...] = jnp.zeros(gx.shape, jnp.float32)
    gy[...] = jnp.zeros(gy.shape, jnp.float32)
    for m in moves:
        m.wait()

    def answer(q):
        for r in range(direct):
            slot = jnp.clip(slots_s[q, r], 0, owned - 1)
            g0[pl.ds(r, 1), :] = rec0[pl.ds(slot, 1), :]
            gx[pl.ds(r, 1), :] = rec_x[pl.ds(slot, 1), :]
            gy[pl.ds(r, 1), :] = rec_y[pl.ds(slot, 1), :]
        ans[q] = (
            g0[...]
            + allbuf[q, 0, pl.ds(0, depth), :] * gx[...]
            + allbuf[q, 1, pl.ds(0, depth), :] * gy[...]
        )

    here1.wait()
    answer(me)

    def receive(k, _):
        copy1(k).wait_recv()
        answer(lax.rem(me + peers - k, peers))
        return 0

    lax.fori_loop(1, peers, receive, 0)

    def pass_on(d, _):
        for e in range(hop):
            q = src_s[e, d]
            s = jnp.clip(q // 8, 0, peers - 1)
            t = jnp.clip(q - s * 8, 0, extra - 1)
            mid_out[d, pl.ds(e, 1), :] = allbuf[s, 0, pl.ds(direct + t, 1), :]
            mid_out[d, pl.ds(hop + e, 1), :] = allbuf[s, 1, pl.ds(direct + t, 1), :]
        return 0

    lax.fori_loop(0, peers, pass_on, 0)
    _, here2, start2, wait2 = exchange(
        lambda p: mid_out.at[p], lambda p: arr2.at[p], send2, recv2, own.at[1]
    )
    _, here3, start3, wait3 = exchange(
        lambda p: ans.at[p],
        lambda p: returned.at[pl.ds(pl.multiple_of(p * depth, 8), depth)],
        send3, recv3, own.at[2]
    )
    _, here4, start4, wait4 = exchange(
        lambda p: ans2.at[p], lambda p: arr4.at[p], send4, recv4, own.at[3]
    )
    _, here5, start5, wait5 = exchange(
        lambda p: out5.at[p], lambda p: arr5.at[p], send5, recv5, own.at[4]
    )
    thirds = [1, peers // 3, 2 * peers // 3, peers]
    here2.start()
    start2(1, peers)
    here3.start()
    start3(thirds[0], thirds[1])
    wait2()

    def answer2(m, _):
        for e in range(hop):
            slot = jnp.clip(slot2_s[e, m], 0, owned - 1)
            inf, sg = arr2[m, pl.ds(e, 1), :], arr2[m, pl.ds(hop + e, 1), :]
            ans2[m, pl.ds(e, 1), :] = (
                rec0[pl.ds(slot, 1), :]
                + inf * rec_x[pl.ds(slot, 1), :]
                + sg * rec_y[pl.ds(slot, 1), :]
            )
            allbuf[m, 0, pl.ds(depth + e, 1), :] = inf
            allbuf[m, 1, pl.ds(depth + e, 1), :] = sg
        return 0

    lax.fori_loop(0, peers, answer2, 0)
    here4.start()
    start4(1, peers)
    start3(thirds[1], thirds[2])

    def finish(c, _):
        def body(i, _):
            for u in range(8):
                n = c * part_rows + i * 8 + u
                v = inv_s[n // LANES, lax.rem(n, LANES)]
                p = jnp.minimum(lax.shift_right_logical(v, bits), peers - 1)
                r = jnp.bitwise_and(v, lines - 1)
                inf = allbuf[p, 0, pl.ds(r, 1), :]
                sg = allbuf[p, 1, pl.ds(r, 1), :]
                at = pl.ds(pl.multiple_of(n * layers, layers), layers)
                moist[at, :] = moist[at, :] + inf * sx[at, :] + sg * sy[at, :]
            return 0

        lax.fori_loop(0, part_rows // 8, body, 0)
        flush(c).start()
        return 0

    bits = lines.bit_length() - 1
    lax.fori_loop(0, chunks // 2, finish, 0)
    wait4()

    def hand_back(s, _):
        for t in range(extra):
            at = jnp.clip(ret_s[t * peers + s, 0], 0, peers * hop - 1)
            d = at // hop
            out5[s, pl.ds(t, 1), :] = arr4[d, pl.ds(at - d * hop, 1), :]
        return 0

    lax.fori_loop(0, peers, hand_back, 0)
    here5.start()
    start5(1, peers)
    start3(thirds[2], thirds[3])
    lax.fori_loop(chunks // 2, chunks, finish, 0)

    def widest(m, most):
        n = number(m)
        seen = functools.reduce(lambda x, y: x + y, [holds(n, base, over, t) for t in range(extra)])
        return jnp.maximum(most, jnp.sum(seen, axis=0, keepdims=True))

    most = lax.fori_loop(0, peers, widest, jnp.zeros((1, LANES), jnp.float32))
    spread = jnp.max(jnp.sum(over, axis=1, keepdims=True), axis=0, keepdims=True)
    bad = jnp.maximum(
        jnp.where(jnp.max(most, axis=1, keepdims=True) > float(hop), 1.0, 0.0),
        jnp.where(spread > float(total), 1.0, 0.0),
    )
    fits[...] = jnp.broadcast_to(1.0 - bad, fits.shape)

    def landed(k):
        return pltpu.make_async_remote_copy(
            src_ref=halo_src[k],
            dst_ref=halo_dst[k],
            send_sem=send_h.at[k],
            recv_sem=recv_h.at[k],
            device_id=(row, col),
            device_id_type=pl.DeviceIdType.MESH,
        )

    each(go, lambda k: halo(k).wait_send())
    each(come, lambda k: landed(k).wait_recv())
    upper = lax.broadcasted_iota(jnp.int32, (8, LANES), 0) < 4
    near = lax.broadcasted_iota(jnp.int32, (8, LANES), 1) < LANES // 2
    for f in range(3):
        eight = pl.ds(8 * f, 8)
        for j in range(cols // LANES):
            part = pl.ds(j * LANES, LANES)
            mid_r[f, :, part] = jnp.where(upper, from_row[0, eight, part], from_row[1, eight, part])
        mid_c[f, pl.ds(rows, 8), :] = jnp.where(
            upper,
            jnp.where(near, corner[0, eight, :], corner[1, eight, :]),
            jnp.where(near, corner[2, eight, :], corner[3, eight, :]),
        )
        mid_c[f, pl.ds(0, rows), :] = jnp.transpose(
            jnp.concatenate(
                [
                    strip_in[0, eight, :],
                    jnp.zeros((LANES - 16, rows), jnp.float32),
                    strip_in[1, eight, :],
                ],
                axis=0,
            )
        )
    wait5()
    for i in range(total):
        returned[pl.ds(peers * depth + i, 1), :] = arr5[i // extra, pl.ds(i % extra, 1), :]
    wait3()
    spread_source(
        position, returned, head, land, s_ref, *for_source, ready=lambda: None
    )

    def sent(k, _):
        copy1(k).wait_send()
        return 0

    lax.fori_loop(1, peers, sent, 0)
    for c in range(chunks):
        flush(c).wait()


def pack_kernel(peers, per_peer, src, labels, precip, head, land, out, infil, heads):
    rows, cols = precip.shape
    for j in range(cols // LANES):
        part = pl.ds(j * LANES, LANES)
        infil[pl.ds(j * rows, rows), :] = precip[:, part] * land[:, part].astype(jnp.float32)
        heads[pl.ds(j * rows, rows), :] = head[:, part]

    def body(p, _):
        for r in range(per_peer):
            block = src[p * per_peer + r]
            out[p, pl.ds(r, 1), :] = infil[pl.ds(block, 1), :]
            out[p, pl.ds(per_peer + r, 1), :] = heads[pl.ds(block, 1), :]
        out[p, pl.ds(2 * per_peer, 8), :] = jnp.broadcast_to(labels[pl.ds(p, 1), :], (8, LANES))
        return 0

    lax.fori_loop(0, peers, body, 0)


def owner_kernel(
    peers, per_peer, slots, arrived, rec0, rec_x, rec_y, answer, infil, sig, own_i, own_h, rec
):
    owned = rec0.shape[0]

    def scatter(p, _):
        for r in range(per_peer):
            slot = slots[p * per_peer + r]
            own_i[pl.ds(slot, 1), :] = arrived[p, pl.ds(r, 1), :]
            own_h[pl.ds(slot, 1), :] = arrived[p, pl.ds(per_peer + r, 1), :]
        return 0

    lax.fori_loop(0, peers, scatter, 0)
    rec[pl.ds(owned, 8), :] = jnp.zeros((8, LANES), jnp.float32)

    def combine(g, _):
        part = pl.ds(g * 64, 64)
        inf = own_i[part, :]
        sg = jax.nn.sigmoid(own_h[part, :])
        infil[part, :] = inf
        sig[part, :] = sg
        rec[part, :] = rec0[part, :] + inf * rec_x[part, :] + sg * rec_y[part, :]
        return 0

    lax.fori_loop(0, owned // 64, combine, 0)

    def gather(p, _):
        for r in range(per_peer):
            slot = slots[p * per_peer + r]
            answer[p, pl.ds(r, 1), :] = rec[pl.ds(slot, 1), :]
        return 0

    lax.fori_loop(0, peers, gather, 0)


def factor_kernel(layers, group, moist, ksat, s0, sx, sy, rec0, rec_x, rec_y):
    def body(step, _):
        base_row = step * group
        rows = pl.ds(pl.multiple_of(base_row, group), group)
        recharge, terms = factor_rows(layers, moist, ksat, base_row, group)
        for ref, value in zip((rec0, rec_x, rec_y), recharge):
            ref[rows, :] = value
        for k in range(layers):
            for ref, value in zip((s0, sx, sy), terms[k]):
                ref[k, rows, :] = value
        return 0

    lax.fori_loop(0, ksat.shape[0] // group, body, 0)


def saturation_kernel(layers, s0, sx, sy, infil, sig, out):
    count = infil.shape[0]
    group = 32

    def body(step, _):
        rows = pl.ds(pl.multiple_of(step * group, group), group)
        inf = infil[rows, :]
        sg = sig[rows, :]
        for k in range(layers):
            out[pl.ds(step * group * layers + k, group, stride=layers), :] = (
                s0[k, rows, :] + inf * sx[k, rows, :] + sg * sy[k, rows, :]
            )
        return 0

    lax.fori_loop(0, count // group, body, 0)


def spread_source(
    position, returned, head, land, s_ref,
    sorted_rows, strip_out, from_row, strip_in, corner, send_sem, recv_sem, ready,
):
    rows, cols = head.shape
    high, wide = s_ref.shape
    row, col = lax.axis_index("row"), lax.axis_index("col")
    steps, go, come = neighbours(row, col)
    east, south = cols - LANES, rows - 8
    src = [
        s_ref.at[pl.ds(0, 8), pl.ds(0, cols)],
        s_ref.at[pl.ds(south, 8), pl.ds(0, cols)],
        strip_out.at[0],
        strip_out.at[1],
    ] + [s_ref.at[pl.ds(y, 8), pl.ds(x, LANES)] for y in (0, south) for x in (0, east)]
    dst = [from_row.at[0], from_row.at[1], strip_in.at[0], strip_in.at[1]] + [
        corner.at[c] for c in range(4)
    ]
    for k in range(8):

        @pl.when(jnp.logical_not(come[k]))
        def _(ref=dst[k]):
            ref[...] = jnp.zeros(ref.shape, jnp.float32)

    def fill(j, g):
        base = pl.multiple_of(g * 32, 32)
        for u in range(32):
            at = j * rows + base + u
            place = jnp.clip(position[at], 0, returned.shape[0] - 1)
            sorted_rows[pl.ds(at, 1), :] = returned[pl.ds(place, 1), :]
        at, part = pl.ds(base, 32), pl.ds(j * LANES, LANES)
        s_ref[at, part] = (
            store_rate * (head[at, part] * land[at, part].astype(jnp.float32))
            + recharge_gain * sorted_rows[pl.ds(j * rows + base, 32), :]
        )

    def fill_range(j, low, high):
        def body(g, _):
            fill(j, g)
            return 0

        lax.fori_loop(low, high, body, 0)

    groups, strips = rows // 32, cols // LANES
    fill_range(0, 0, groups)
    fill_range(strips - 1, 0, groups)
    strip_out[0] = jnp.transpose(s_ref[0:rows, 0:LANES])[0:8]
    strip_out[1] = jnp.transpose(s_ref[0:rows, east:cols])[LANES - 8 : LANES]
    for j in range(1, strips - 1):
        fill(j, 0)
        fill(j, groups - 1)
    ready()

    def copy(k):
        return halo_copy(k, steps, row, col, src, dst, send_sem, recv_sem)

    def landed(k):
        return halo_copy(k, [(0, 0)] * 8, row, col, src, dst, send_sem, recv_sem)

    each(go, lambda k: copy(k).start())
    for j in range(1, strips - 1):
        fill_range(j, 1, groups - 1)
    each(go, lambda k: copy(k).wait_send())
    each(come, lambda k: landed(k).wait_recv())
    first = lax.broadcasted_iota(jnp.int32, (8, LANES), 0) < 4
    near = lax.broadcasted_iota(jnp.int32, (8, LANES), 1) < LANES // 2
    for j in range(strips):
        part = slice(j * LANES, (j + 1) * LANES)
        s_ref[rows:high, part] = jnp.where(first, from_row[0, :, part], from_row[1, :, part])
    s_ref[rows:high, cols:wide] = jnp.where(
        first,
        jnp.where(near, corner[0], corner[1]),
        jnp.where(near, corner[2], corner[3]),
    )
    s_ref[0:rows, cols:wide] = jnp.transpose(
        jnp.concatenate(
            [strip_in[0], jnp.zeros((LANES - 16, rows), jnp.float32), strip_in[1]], axis=0
        )
    )


def source_kernel(position, returned, head, land, s_ref, *scratch):
    row, col = lax.axis_index("row"), lax.axis_index("col")
    steps, go, _ = neighbours(row, col)
    barrier = pltpu.get_barrier_semaphore()

    def greet(k):
        pl.semaphore_signal(
            barrier,
            inc=1,
            device_id=(row + steps[k][0], col + steps[k][1]),
            device_id_type=pl.DeviceIdType.MESH,
        )

    each(go, greet)

    def ready():
        pl.semaphore_wait(
            barrier, functools.reduce(lambda x, y: x + y, [f.astype(jnp.int32) for f in go])
        )

    spread_source(position, returned, head, land, s_ref, *scratch, ready)


def relax_kernel(
    pieces, source, head, trans_coef, land, mid_r, mid_c, stepped, out, saturation,
    t_ref, s_ref, fu, fd, fl, fr, a, b, held, read, write,
):
    rows, cols = head.shape
    high, wide = t_ref.shape
    each_rows = stepped.shape[0] // pieces
    parts = [pl.ds(c * each_rows, each_rows) for c in range(pieces)]
    reads = [
        pltpu.make_async_copy(stepped.at[p], held.at[p], read.at[c]) for c, p in enumerate(parts)
    ]
    writes = [
        pltpu.make_async_copy(held.at[p], saturation.at[p], write.at[c])
        for c, p in enumerate(parts)
    ]
    for copy in reads:
        copy.start()
    left = list(range(pieces))

    def pass_piece():
        if left:
            c = left.pop(0)
            reads[c].wait()
            writes[c].start()

    for f, (ref, centre) in enumerate(
        zip((t_ref, a, b), fixed_fields(head[...], trans_coef[...], land[...]))
    ):
        ref[0:rows, 0:cols] = centre
        ref[rows:high, 0:cols] = mid_r[f]
        ref[:, cols:wide] = mid_c[f]
    for g in range(wide // LANES):
        part = slice(g * LANES, (g + 1) * LANES)
        lo = slice((g - 1) % (wide // LANES) * LANES, (g - 1) % (wide // LANES) * LANES + LANES)
        hi = slice((g + 1) % (wide // LANES) * LANES, (g + 1) % (wide // LANES) * LANES + LANES)
        lane = lax.broadcasted_iota(jnp.int32, (high, LANES), 1)
        t = t_ref[:, part]
        tu = 0.5 * (t + pltpu.roll(t, 1, 0))
        td = 0.5 * (t + pltpu.roll(t, high - 1, 0))
        tl = jnp.where(lane == 0, pltpu.roll(t_ref[:, lo], 1, 1), pltpu.roll(t, 1, 1))
        tr = jnp.where(
            lane == LANES - 1,
            pltpu.roll(t_ref[:, hi], LANES - 1, 1),
            pltpu.roll(t, LANES - 1, 1),
        )
        lf = 0.5 * (t + tl)
        rt = 0.5 * (t + tr)
        inv = b[:, part] / (store_rate + (tu + td + lf + rt))
        fu[:, part] = tu * inv
        fd[:, part] = td * inv
        fl[:, part] = lf * inv
        fr[:, part] = rt * inv
        s_ref[:, part] = source[:, part] * inv
        if g > 1:
            pass_piece()
    now, later = a, b
    for sweep in range(SWEEPS):
        last = sweep == SWEEPS - 1
        for g in range(wide // LANES):
            if last and g * LANES >= cols:
                continue
            pass_piece()
            part = slice(g * LANES, (g + 1) * LANES)
            lo = (g - 1) % (wide // LANES) * LANES
            hi = (g + 1) % (wide // LANES) * LANES
            lane = lax.broadcasted_iota(jnp.int32, (high, LANES), 1)
            x = now[:, part]
            xl = jnp.where(
                lane == 0, pltpu.roll(now[:, lo : lo + LANES], 1, 1), pltpu.roll(x, 1, 1)
            )
            xr = jnp.where(
                lane == LANES - 1,
                pltpu.roll(now[:, hi : hi + LANES], LANES - 1, 1),
                pltpu.roll(x, LANES - 1, 1),
            )
            y = s_ref[:, part] + fu[:, part] * pltpu.roll(x, 1, 0)
            y = y + fd[:, part] * pltpu.roll(x, high - 1, 0)
            y = y + (fl[:, part] * xl + fr[:, part] * xr)
            if last:
                out[:, part] = y[0:rows]
            else:
                later[:, part] = y
        now, later = later, now
    while left:
        pass_piece()
    for copy in writes:
        copy.wait()


def on_device(precip, head, trans_coef, land, dest, moisture, ksat):
    tile_rows, tile_cols = precip.shape
    n_col = lax.axis_size("col")
    peers = lax.axis_size("row") * n_col
    me = lax.axis_index("row") * n_col + lax.axis_index("col")
    owned, layers, _ = moisture.shape
    blocks = tile_rows * tile_cols // LANES
    cap = (2 * blocks + peers - 1) // peers
    extra, hop = 2, 4
    depth = (19 * blocks // (16 * peers) + 1 + 7) // 8 * 8
    direct = depth - extra
    lines = 1 << (depth + hop - 1).bit_length()

    target = dest.T.reshape(blocks)
    owner = target // owned
    slot = target - owner * owned
    all_peers = jnp.arange(peers, dtype=jnp.int32)
    one_hot = owner[:, None] == all_peers[None, :]
    order = jnp.arange(blocks, dtype=jnp.int32)
    earlier = (order[None, :] < order[:, None]).astype(jnp.bfloat16)
    counts = jnp.dot(earlier, one_hot.astype(jnp.bfloat16), preferred_element_type=jnp.float32)
    sums = jnp.sum(one_hot.astype(jnp.float32), axis=0)
    over = jnp.maximum(sums - direct, 0.0)
    base = jnp.sum(jnp.where(all_peers[:, None] < all_peers[None, :], over[:, None], 0.0), axis=0)
    rank = jnp.sum(jnp.where(one_hot, counts, 0.0), axis=1).astype(jnp.int32)
    number = jnp.sum(jnp.where(one_hot, counts + base[None, :] - direct, 0.0), axis=1).astype(
        jnp.int32
    )
    spread = rank >= direct
    via = (jnp.maximum(number, 0) + me) % peers
    turn = jnp.clip(number // peers, 0, extra - 1)
    position = jnp.where(
        spread, peers * depth + via * extra + turn, owner * depth + rank
    )
    place = jnp.where(spread, via, owner)
    row_of = jnp.where(spread, direct + turn, rank)

    def table(where, row, width, value):
        hot = (where[:, None] == all_peers[None, :]).astype(jnp.float32)
        at = row[:, None] == jnp.arange(width, dtype=jnp.int32)[None, :]
        return lax.dot_general(
            hot,
            jnp.where(at, value.astype(jnp.float32)[:, None], 0.0),
            (((0,), (0,)), ((), ())),
            precision=lax.Precision.HIGHEST,
            preferred_element_type=jnp.float32,
        )

    source_of = jnp.minimum(table(place, row_of, depth, order).astype(jnp.int32), blocks - 1)
    label = table(owner, rank, LANES, slot - owned) + float(owned)
    sent = jnp.broadcast_to(jnp.pad(sums, (0, LANES - peers))[None, :], (peers, LANES))

    sources, labels, position, owner, rank = lax.optimization_barrier(
        (source_of.reshape(peers * depth), jnp.stack([label, sent], axis=1), position, owner, rank)
    )
    flat = moisture.reshape(owned * layers, LANES)
    vm = lambda *shape: pltpu.VMEM(shape, jnp.float32)
    iv = lambda *shape: pltpu.VMEM(shape, jnp.int32)
    sm = lambda *shape: pltpu.SMEM(shape, jnp.int32)
    dma = lambda n: pltpu.SemaphoreType.DMA((n,))
    chunks = 8
    tail = (peers * extra + depth - 1) // depth
    high, wide = tile_rows + 2 * SWEEPS, tile_cols + LANES
    for_source = [
        vm(blocks, LANES),
        vm(2, 8, tile_rows),
        vm(2, 8, tile_cols),
        vm(2, 8, tile_rows),
        vm(4, 8, LANES),
        dma(8),
        dma(8),
    ]
    source, stepped, fits, mid_r, mid_c = pl.pallas_call(
        functools.partial(column_kernel, cap, extra, hop, chunks),
        out_shape=[
            f32(high, wide),
            f32(owned * layers, LANES),
            f32(1, 1),
            f32(3, 2 * SWEEPS, tile_cols),
            f32(3, high, LANES),
        ],
        in_specs=[SM, SM] + [VM] * 5 + [pl.BlockSpec(memory_space=pl.ANY), VM],
        out_specs=[VM, pl.BlockSpec(memory_space=pl.ANY), VM, VM, VM],
        scratch_shapes=[
            vm((peers + tail) * depth, LANES),
            vm(blocks, LANES),
            vm(blocks, LANES),
            vm(peers, 2, depth, LANES),
            vm(peers, 2, lines, LANES),
            vm(peers, 2, LANES),
        ]
        + [vm(owned * layers, LANES)] * 3
        + [vm(owned, LANES)] * 3
        + [
            vm(peers, 2 * hop, LANES),
            vm(peers, 2 * hop, LANES),
            vm(peers, depth, LANES),
            vm(peers, hop, LANES),
            vm(peers, hop, LANES),
            vm(peers, extra, LANES),
            vm(peers, extra, LANES),
            vm(depth, LANES),
            vm(depth, LANES),
            vm(depth, LANES),
            iv(8, LANES),
            iv(extra * peers, LANES),
            iv(peers, LANES),
            iv(8, LANES),
            iv(owned // LANES, LANES),
            vm(2, 24, tile_cols),
            vm(2, 24, tile_rows),
            vm(2, 24, tile_cols),
            vm(2, 24, tile_rows),
            vm(4, 24, LANES),
            sm(peers, LANES),
            sm(8, LANES),
            sm(8, LANES),
            sm(extra * peers, LANES),
            sm(owned // LANES, LANES),
            dma(5),
            dma(chunks),
            dma(chunks),
        ]
        + [dma(peers)] * 12
        + [dma(6), dma(8), dma(8)]
        + for_source,
        compiler_params=pltpu.CompilerParams(
            collective_id=4, has_side_effects=True, vmem_limit_bytes=58 * 2**20
        ),
    )(sources, position, labels, precip, head, trans_coef, land, flat, ksat)


    def relax(source, stepped):
        pieces = 16
        surface, saturation = pl.pallas_call(
            functools.partial(relax_kernel, pieces),
            out_shape=[f32(tile_rows, tile_cols), f32(owned * layers, LANES)],
            in_specs=[VM] * 6 + [pl.BlockSpec(memory_space=pl.ANY)],
            out_specs=[VM, pl.BlockSpec(memory_space=pl.ANY)],
            scratch_shapes=[vm(high, wide)] * 8
            + [vm(owned * layers, LANES), dma(pieces), dma(pieces)],
            compiler_params=pltpu.CompilerParams(vmem_limit_bytes=40 * 2**20),
        )(source, head, trans_coef, land, mid_r, mid_c, stepped)
        return saturation.reshape(owned, layers, LANES), surface

    def hopped():
        return relax(source, stepped)

    def whole():
        step = 128
        layered = pl.BlockSpec((layers, step, LANES), lambda i: (0, i, 0))
        single = pl.BlockSpec((step, LANES), lambda i: (i, 0))
        natural = pl.BlockSpec((step * layers, LANES), lambda i: (i, 0))
        s0, sx, sy, rec0, rec_x, rec_y = pl.pallas_call(
            functools.partial(factor_kernel, layers, 32),
            grid=(owned // step,),
            out_shape=[f32(layers, owned, LANES)] * 3 + [f32(owned, LANES)] * 3,
            in_specs=[natural, single],
            out_specs=[layered] * 3 + [single] * 3,
        )(flat, ksat)
        slots_of = table(owner, rank, cap, order).astype(jnp.int32).reshape(peers * cap)
        outgoing = pl.pallas_call(
            functools.partial(pack_kernel, peers, cap),
            out_shape=f32(peers, 2 * cap + 8, LANES),
            in_specs=[SM, VM, VM, VM, VM],
            out_specs=VM,
            scratch_shapes=[pltpu.VMEM((blocks, LANES), jnp.float32)] * 2,
        )(slots_of, labels[:, 0], precip, head, land)
        arrived = lax.all_to_all(outgoing, ("row", "col"), split_axis=0, concat_axis=0, tiled=True)
        places = arrived[:, 2 * cap, :cap].astype(jnp.int32).reshape(peers * cap)
        answer, infil, sig = pl.pallas_call(
            functools.partial(owner_kernel, peers, cap),
            out_shape=[f32(peers, cap, LANES), f32(owned, LANES), f32(owned, LANES)],
            in_specs=[SM, VM, VM, VM, VM],
            out_specs=[VM] * 3,
            scratch_shapes=[pltpu.VMEM((owned + 8, LANES), jnp.float32)] * 3,
        )(places, arrived, rec0, rec_x, rec_y)
        back = lax.all_to_all(answer, ("row", "col"), split_axis=0, concat_axis=0, tiled=True)
        saturation = pl.pallas_call(
            functools.partial(saturation_kernel, layers),
            grid=(owned // step,),
            out_shape=f32(owned * layers, LANES),
            in_specs=[layered] * 3 + [single] * 2,
            out_specs=natural,
        )(s0, sx, sy, infil, sig)
        source = pl.pallas_call(
            source_kernel,
            out_shape=f32(high, wide),
            in_specs=[SM] + [VM] * 3,
            out_specs=VM,
            scratch_shapes=for_source,
            compiler_params=pltpu.CompilerParams(collective_id=2, has_side_effects=True),
        )(owner * cap + rank, back.reshape(-1, LANES), head, land)
        return relax(source, saturation)

    return lax.cond(fits.reshape(()) > 0.5, hopped, whole)


def solution(mesh):
    tile = P("row", "col")
    placed = (
        tile,
        tile,
        tile,
        tile,
        tile,
        P(("row", "col"), None, None),
        P(("row", "col"), None),
    )
    return jax.shard_map(
        on_device,
        mesh=mesh,
        in_specs=placed,
        out_specs=(P(("row", "col"), None, None), P("row", "col")),
        check_vma=False,
    )
```

```python
import functools
import math

import jax
import jax.numpy as jnp
from jax import lax
from jax.experimental import pallas as pl
from jax.experimental.pallas import tpu as pltpu
from jax.sharding import PartitionSpec as P

SWEEPS = 4
LANES = 128

layer_depth = 0.1
step_ratio = 0.1
residual_water = 0.05
pore_range = 0.4
diff_length = 0.5
couple_rate = 0.05
recharge_gain = 20.0
store_rate = 0.2

VM = pl.BlockSpec(memory_space=pltpu.VMEM)
SM = pl.BlockSpec(memory_space=pltpu.SMEM)


def f32(*shape):
    return jax.ShapeDtypeStruct(shape, jnp.float32)


def factor_rows(layers, moist, ksat, base_row, group):
    rows = pl.ds(pl.multiple_of(base_row, group), group)
    ks = ksat[rows, :]
    ratios, reds, xs = [], [], []
    before = None
    for k in range(layers):
        m = moist[pl.ds(base_row * layers + k, group, stride=layers), :]
        w = (m - residual_water) * (1.0 / pore_range)
        s = ks * math.exp(-(k + 0.5) * layer_depth)
        sw2 = s * (w * w)
        hs = sw2 * (1.5 / pore_range)
        d = s * (0.2 * diff_length / (2.0 * layer_depth)) + sw2 * (
            diff_length / (2.0 * layer_depth)
        )
        hc = 0.5 * (sw2 * w)
        cur = (m, hs, d, hc)
        if before is None:
            before = cur
            g_up = q_up = nsub = None
            continue
        m0, hs0, d0, hc0 = before
        g = d0 + d
        q = (hc0 + hc) - g * (m - m0)
        if g_up is None:
            pivot = step_ratio + g + hs0
            inv = 1.0 / pivot
            reds.append(-q * inv)
            xs.append(inv)
        else:
            pivot = step_ratio + g_up + g - nsub * ratios[-1]
            inv = 1.0 / pivot
            reds.append(((q_up - q) + nsub * reds[-1]) * inv)
            xs.append(nsub * inv * xs[-1])
        ratios.append((g - hs) * inv)
        nsub = hs0 + g
        g_up, q_up = g, q
        before = cur
    m, hs, d, hc = before
    bottom = 2.0 * hc + couple_rate * (m - residual_water)
    pivot = step_ratio + g_up + hs + couple_rate - nsub * ratios[-1]
    inv = 1.0 / pivot
    change = ((q_up - bottom) + nsub * reds[-1]) * inv
    cx = nsub * inv * xs[-1]
    cy = (couple_rate * pore_range) * inv
    gain = 2.0 * hs + couple_rate
    recharge = (
        bottom + gain * change,
        gain * cx,
        gain * cy - couple_rate * pore_range,
    )
    unit = 1.0 / pore_range
    terms = [None] * layers
    for k in range(layers - 1, -1, -1):
        if k < layers - 1:
            change = reds[k] + ratios[k] * change
            cx = xs[k] + ratios[k] * cx
            cy = ratios[k] * cy
        m = moist[pl.ds(base_row * layers + k, group, stride=layers), :]
        terms[k] = ((m + change - residual_water) * unit, cx * unit, cy * unit)
    return recharge, terms


def within(index, size):
    if size & (size - 1) == 0:
        return jnp.bitwise_and(index, size - 1)
    return jnp.clip(index, 0, size - 1)


def fixed_fields(head, trans_coef, land):
    share = land.astype(jnp.float32)
    return trans_coef * (1.0 + 0.5 * jnp.tanh(head)), head * share, share


def neighbours(row, col):
    n_row, n_col = lax.axis_size("row"), lax.axis_size("col")
    up, down = row > 0, row < n_row - 1
    left, right = col > 0, col < n_col - 1
    steps = [(-1, 0), (1, 0), (0, -1), (0, 1), (-1, -1), (-1, 1), (1, -1), (1, 1)]
    go = [up, down, left, right, up & left, up & right, down & left, down & right]
    come = [down, up, right, left, down & right, down & left, up & right, up & left]
    return steps, go, come


def each(flags, act):
    for k, flag in enumerate(flags):
        pl.when(flag)(functools.partial(act, k))


def halo_copy(k, steps, row, col, src, dst, send_sem, recv_sem):
    return pltpu.make_async_remote_copy(
        src_ref=src[k],
        dst_ref=dst[k],
        send_sem=send_sem.at[k],
        recv_sem=recv_sem.at[k],
        device_id=(row + steps[k][0], col + steps[k][1]),
        device_id_type=pl.DeviceIdType.MESH,
    )


def column_kernel(
    cap, extra, hop, chunks, src, position, labels, precip, head, trans_coef, land, moisture, ksat,
    s_ref, saturation, fits, mid_r, mid_c, returned,
    infil, sigs, out, allbuf, labs, moist, sx, sy, rec0, rec_x, rec_y,
    mid_out, arr2, ans, ans2, arr4, out5, arr5, g0, gx, gy, src_v, ret_v, slots_v, slot2_v, inv_v,
    row_out, strip_out, from_row, strip_in, corner,
    slots_s, slot2_s, src_s, ret_s, inv_s,
    move, read, write, send0, recv0, send1, recv1, send2, recv2, send3, recv3, send4, recv4, send5, recv5, own,
    send_h, recv_h, *for_source,
):
    rows, cols = precip.shape
    peers, _, lines, _ = allbuf.shape
    depth = out.shape[2]
    direct = depth - extra
    owned = rec0.shape[0]
    layers = moist.shape[0] // owned
    n_col = lax.axis_size("col")
    row, col = lax.axis_index("row"), lax.axis_index("col")
    me = row * n_col + col
    barrier = pltpu.get_barrier_semaphore()
    part_rows = owned // chunks

    def fetch(c):
        part = pl.ds(c * part_rows * layers, part_rows * layers)
        return pltpu.make_async_copy(moisture.at[part], moist.at[part], read.at[c])

    def flush(c):
        part = pl.ds(c * part_rows * layers, part_rows * layers)
        return pltpu.make_async_copy(moist.at[part], saturation.at[part], write.at[c])

    def where_is(k):
        p = lax.rem(me + k, peers)
        return p, (p // n_col, lax.rem(p, n_col))

    def greet(k, _):
        pl.semaphore_signal(
            barrier, inc=1, device_id=where_is(k)[1], device_id_type=pl.DeviceIdType.MESH
        )
        return 0

    lax.fori_loop(1, peers, greet, 0)
    for c in range(chunks):
        fetch(c).start()

    def exchange(src, dst, send, recv, self_sem):
        def copy(k):
            p, place = where_is(k)
            return pltpu.make_async_remote_copy(
                src_ref=src(p),
                dst_ref=dst(me),
                send_sem=send.at[k],
                recv_sem=recv.at[k],
                device_id=place,
                device_id_type=pl.DeviceIdType.MESH,
            )

        here = pltpu.make_async_copy(src(me), dst(me), self_sem)

        def start(low, high):
            def body(k, _):
                copy(k).start()
                return 0

            lax.fori_loop(low, high, body, 0)

        def wait():
            def body(k, _):
                copy(k).wait()
                return 0

            lax.fori_loop(1, peers, body, 0)
            here.wait()

        return copy, here, start, wait

    for j in range(cols // LANES):
        part = pl.ds(j * LANES, LANES)
        infil[pl.ds(j * rows, rows), :] = precip[:, part] * land[:, part].astype(jnp.float32)
        sigs[pl.ds(j * rows, rows), :] = jax.nn.sigmoid(head[:, part])

    def pack(p):
        for r in range(depth):
            block = within(src[p * depth + r], infil.shape[0])
            out[p, 0, pl.ds(r, 1), :] = infil[pl.ds(block, 1), :]
            out[p, 1, pl.ds(r, 1), :] = sigs[pl.ds(block, 1), :]

    _, here0, start0, wait0 = exchange(
        lambda p: labels.at[p], lambda p: labs.at[p], send0, recv0, own.at[5]
    )
    copy1, here1, _, _ = exchange(
        lambda p: out.at[p], lambda p: allbuf.at[p, :, pl.ds(0, depth)], send1, recv1, own.at[0]
    )
    pl.semaphore_wait(barrier, peers - 1)
    here0.start()
    start0(1, peers)

    def ship(k, _):
        pack(where_is(k)[0])
        copy1(k).start()
        return 0

    lax.fori_loop(1, peers, ship, 0)
    pack(me)
    here1.start()

    steps, go, come = neighbours(row, col)
    east, south = cols - LANES, rows - 8
    for side, at in enumerate((0, south)):
        edge = pl.ds(at, 8)
        for f, field in enumerate(fixed_fields(head[edge, :], trans_coef[edge, :], land[edge, :])):
            row_out[side, pl.ds(8 * f, 8), :] = field
    for side, at in enumerate((0, east)):
        edge = pl.ds(at, LANES)
        keep = slice(0, 8) if side == 0 else slice(LANES - 8, LANES)
        for f, field in enumerate(fixed_fields(head[:, edge], trans_coef[:, edge], land[:, edge])):
            strip_out[side, pl.ds(8 * f, 8), :] = jnp.transpose(field)[keep]
    halo_dst = [from_row.at[0], from_row.at[1], strip_in.at[0], strip_in.at[1]] + [
        corner.at[c] for c in range(4)
    ]
    halo_src = [row_out.at[0], row_out.at[1], strip_out.at[0], strip_out.at[1]] + [
        row_out.at[c // 2, :, pl.ds((c % 2) * east, LANES)] for c in range(4)
    ]
    for k in range(8):

        @pl.when(jnp.logical_not(come[k]))
        def _(ref=halo_dst[k]):
            ref[...] = jnp.zeros(ref.shape, jnp.float32)

    def halo(k):
        return halo_copy(k, steps, row, col, halo_src, halo_dst, send_h, recv_h)

    each(go, lambda k: halo(k).start())

    group = 32

    def factor(c, _):
        fetch(c).wait()

        def body(i, _):
            base_row = pl.multiple_of(c * part_rows + i * group, group)
            at = pl.ds(base_row, group)
            recharge, terms = factor_rows(layers, moist, ksat, base_row, group)
            for ref, value in zip((rec0, rec_x, rec_y), recharge):
                ref[at, :] = value
            for k in range(layers):
                for ref, value in zip((moist, sx, sy), terms[k]):
                    ref[pl.ds(base_row * layers + k, group, stride=layers), :] = value
            return 0

        lax.fori_loop(0, part_rows // group, body, 0)
        return 0

    lax.fori_loop(0, chunks, factor, 0)
    wait0()

    shape = (peers, LANES)
    lane = lax.broadcasted_iota(jnp.int32, shape, 1)
    sub = lax.broadcasted_iota(jnp.int32, shape, 0)
    lab = labs[:, 0, :]
    count = labs[:, 1, :]
    over = jnp.maximum(count - direct, 0.0)
    tri = lax.broadcasted_iota(jnp.int32, (LANES, LANES), 0) < lax.broadcasted_iota(
        jnp.int32, (LANES, LANES), 1
    )
    base = jnp.dot(
        over, tri.astype(jnp.float32), precision=lax.Precision.HIGHEST,
        preferred_element_type=jnp.float32,
    )
    total = extra * peers
    before = (
        lax.broadcasted_iota(jnp.int32, (total, total), 1)
        < lax.broadcasted_iota(jnp.int32, (total, total), 0)
    ).astype(jnp.float32)

    def number(m):
        gap = m - sub
        return jnp.where(gap < 0, gap + peers, gap).astype(jnp.float32)

    def holds(j, first, many, t):
        j = j + float(t * peers)
        return jnp.where((first <= j) & (j < first + many), 1.0, 0.0)

    def prefix(v):
        return jnp.dot(before, v, preferred_element_type=jnp.float32)

    flane = lane.astype(jnp.float32)
    code = sub.astype(jnp.float32) * 8.0
    via = jnp.concatenate([holds(number(me), base, over, t) for t in range(extra)], axis=0)
    rank = prefix(via)
    codes = jnp.concatenate([code + float(t) for t in range(extra)], axis=0)
    lanes = jnp.concatenate([flane] * extra, axis=0)
    back = jnp.sum(via * (lanes * hop + rank), axis=1, keepdims=True)
    ret_v[...] = jnp.broadcast_to(back, (total, LANES)).astype(jnp.int32)
    pad = jnp.zeros((8 - hop, LANES), jnp.float32)
    picks = [
        jnp.sum(jnp.where(rank == float(e), via * codes, 0.0), axis=0, keepdims=True)
        for e in range(hop)
    ]
    src_v[...] = jnp.concatenate(picks + [pad], axis=0).astype(jnp.int32)
    mine = jnp.where(lane == me, 1.0, 0.0)
    first = jnp.sum(base * mine, axis=1, keepdims=True)
    many = jnp.sum(over * mine, axis=1, keepdims=True)
    inside = jnp.where(lane < peers, 1.0, 0.0)
    step = number(lane)
    took = [holds(step, first, many, t) * inside for t in range(extra)]
    value = []
    for t in range(extra):
        at = step + float(t * peers) - first
        v = jnp.zeros(shape, jnp.float32)
        for r in range(cap - direct):
            v = jnp.where(at == float(r), lab[:, direct + r : direct + r + 1] - float(owned), v)
        value.append(v)
    took = jnp.concatenate(took, axis=0)
    rank = prefix(took)
    value = jnp.concatenate(value, axis=0)
    picks = [
        jnp.sum(jnp.where(rank == float(e), took * value, 0.0), axis=0, keepdims=True)
        for e in range(hop)
    ]
    hopped = jnp.concatenate(picks + [pad], axis=0) + float(owned)
    slot2_v[...] = hopped.astype(jnp.int32)
    slots_v[...] = lab.astype(jnp.int32)
    moves = [
        pltpu.make_async_copy(src_v, src_s, move.at[0]),
        pltpu.make_async_copy(slots_v, slots_s, move.at[1]),
        pltpu.make_async_copy(slot2_v, slot2_s, move.at[2]),
        pltpu.make_async_copy(ret_v, ret_s, move.at[3]),
    ]
    for m in moves:
        m.start()
    g0[...] = jnp.zeros(g0.shape, jnp.float32)
    gx[...] = jnp.zeros(gx.shape, jnp.float32)
    gy[...] = jnp.zeros(gy.shape, jnp.float32)
    for m in moves:
        m.wait()

    def answer(q):
        for r in range(direct):
            slot = within(slots_s[q, r], owned)
            g0[pl.ds(r, 1), :] = rec0[pl.ds(slot, 1), :]
            gx[pl.ds(r, 1), :] = rec_x[pl.ds(slot, 1), :]
            gy[pl.ds(r, 1), :] = rec_y[pl.ds(slot, 1), :]
        ans[q] = (
            g0[...]
            + allbuf[q, 0, pl.ds(0, depth), :] * gx[...]
            + allbuf[q, 1, pl.ds(0, depth), :] * gy[...]
        )

    here1.wait()
    answer(me)

    def receive(k, _):
        copy1(k).wait_recv()
        answer(lax.rem(me + peers - k, peers))
        return 0

    lax.fori_loop(1, peers, receive, 0)

    def pass_on(d, _):
        for e in range(hop):
            q = src_s[e, d]
            s = jnp.clip(q // 8, 0, peers - 1)
            t = jnp.clip(q - s * 8, 0, extra - 1)
            mid_out[d, pl.ds(e, 1), :] = allbuf[s, 0, pl.ds(direct + t, 1), :]
            mid_out[d, pl.ds(hop + e, 1), :] = allbuf[s, 1, pl.ds(direct + t, 1), :]
        return 0

    lax.fori_loop(0, peers, pass_on, 0)
    _, here2, start2, wait2 = exchange(
        lambda p: mid_out.at[p], lambda p: arr2.at[p], send2, recv2, own.at[1]
    )
    _, here3, start3, wait3 = exchange(
        lambda p: ans.at[p],
        lambda p: returned.at[pl.ds(pl.multiple_of(p * depth, 8), depth)],
        send3, recv3, own.at[2]
    )
    _, here4, start4, wait4 = exchange(
        lambda p: ans2.at[p], lambda p: arr4.at[p], send4, recv4, own.at[3]
    )
    _, here5, start5, wait5 = exchange(
        lambda p: out5.at[p], lambda p: arr5.at[p], send5, recv5, own.at[4]
    )
    thirds = [1, peers // 3, 2 * peers // 3, peers]
    here2.start()
    start2(1, peers)
    here3.start()
    start3(thirds[0], thirds[1])

    columns = jnp.transpose(
        jnp.concatenate([hopped, jnp.zeros((LANES - 8, LANES), jnp.float32)], axis=0)
    )
    place = sub.astype(jnp.float32) * float(lines)
    for g in range(owned // LANES):
        want = flane + float(g * LANES)
        found = jnp.zeros(shape, jnp.float32)
        for r in range(direct):
            found = jnp.where(lab[:, r : r + 1] == want, place + float(r), found)
        for e in range(hop):
            found = jnp.where(
                columns[0:peers, e : e + 1] == want, place + float(depth + e), found
            )
        inv_v[pl.ds(g, 1), :] = jnp.sum(found, axis=0, keepdims=True).astype(jnp.int32)
    turn = pltpu.make_async_copy(inv_v, inv_s, move.at[4])
    turn.start()

    def widest(m, most):
        n = number(m)
        seen = functools.reduce(lambda x, y: x + y, [holds(n, base, over, t) for t in range(extra)])
        return jnp.maximum(most, jnp.sum(seen, axis=0, keepdims=True))

    most = lax.fori_loop(0, peers, widest, jnp.zeros((1, LANES), jnp.float32))
    spread = jnp.max(jnp.sum(over, axis=1, keepdims=True), axis=0, keepdims=True)
    bad = jnp.maximum(
        jnp.where(jnp.max(most, axis=1, keepdims=True) > float(hop), 1.0, 0.0),
        jnp.where(spread > float(total), 1.0, 0.0),
    )
    fits[...] = jnp.broadcast_to(1.0 - bad, fits.shape)

    def landed(k):
        return pltpu.make_async_remote_copy(
            src_ref=halo_src[k],
            dst_ref=halo_dst[k],
            send_sem=send_h.at[k],
            recv_sem=recv_h.at[k],
            device_id=(row, col),
            device_id_type=pl.DeviceIdType.MESH,
        )

    each(go, lambda k: halo(k).wait_send())
    each(come, lambda k: landed(k).wait_recv())
    upper = lax.broadcasted_iota(jnp.int32, (8, LANES), 0) < 4
    near = lax.broadcasted_iota(jnp.int32, (8, LANES), 1) < LANES // 2
    for f in range(3):
        eight = pl.ds(8 * f, 8)
        for j in range(cols // LANES):
            part = pl.ds(j * LANES, LANES)
            mid_r[f, :, part] = jnp.where(upper, from_row[0, eight, part], from_row[1, eight, part])
        mid_c[f, pl.ds(rows, 8), :] = jnp.where(
            upper,
            jnp.where(near, corner[0, eight, :], corner[1, eight, :]),
            jnp.where(near, corner[2, eight, :], corner[3, eight, :]),
        )
        mid_c[f, pl.ds(0, rows), :] = jnp.transpose(
            jnp.concatenate(
                [
                    strip_in[0, eight, :],
                    jnp.zeros((LANES - 16, rows), jnp.float32),
                    strip_in[1, eight, :],
                ],
                axis=0,
            )
        )
    turn.wait()
    wait2()

    def answer2(m, _):
        for e in range(hop):
            slot = within(slot2_s[e, m], owned)
            inf, sg = arr2[m, pl.ds(e, 1), :], arr2[m, pl.ds(hop + e, 1), :]
            ans2[m, pl.ds(e, 1), :] = (
                rec0[pl.ds(slot, 1), :]
                + inf * rec_x[pl.ds(slot, 1), :]
                + sg * rec_y[pl.ds(slot, 1), :]
            )
            allbuf[m, 0, pl.ds(depth + e, 1), :] = inf
            allbuf[m, 1, pl.ds(depth + e, 1), :] = sg
        return 0

    lax.fori_loop(0, peers, answer2, 0)
    here4.start()
    start4(1, peers)
    start3(thirds[1], thirds[2])

    def finish(c, _):
        def body(i, _):
            for u in range(8):
                n = c * part_rows + i * 8 + u
                v = inv_s[n // LANES, lax.rem(n, LANES)]
                p = jnp.minimum(lax.shift_right_logical(v, bits), peers - 1)
                r = jnp.bitwise_and(v, lines - 1)
                inf = allbuf[p, 0, pl.ds(r, 1), :]
                sg = allbuf[p, 1, pl.ds(r, 1), :]
                at = pl.ds(pl.multiple_of(n * layers, layers), layers)
                moist[at, :] = moist[at, :] + inf * sx[at, :] + sg * sy[at, :]
            return 0

        lax.fori_loop(0, part_rows // 8, body, 0)
        flush(c).start()
        return 0

    bits = lines.bit_length() - 1
    lax.fori_loop(0, chunks // 2, finish, 0)
    wait4()

    def hand_back(s, _):
        for t in range(extra):
            at = jnp.clip(ret_s[t * peers + s, 0], 0, peers * hop - 1)
            d = at // hop
            out5[s, pl.ds(t, 1), :] = arr4[d, pl.ds(at - d * hop, 1), :]
        return 0

    lax.fori_loop(0, peers, hand_back, 0)
    here5.start()
    start5(1, peers)
    start3(thirds[2], thirds[3])
    lax.fori_loop(chunks // 2, chunks, finish, 0)

    wait5()
    for i in range(total):
        returned[pl.ds(peers * depth + i, 1), :] = arr5[i // extra, pl.ds(i % extra, 1), :]
    wait3()
    spread_source(
        position, returned, head, land, s_ref, *for_source, ready=lambda: None
    )

    def sent(k, _):
        copy1(k).wait_send()
        return 0

    lax.fori_loop(1, peers, sent, 0)
    for c in range(chunks):
        flush(c).wait()


def pack_kernel(peers, per_peer, src, labels, precip, head, land, out, infil, heads):
    rows, cols = precip.shape
    for j in range(cols // LANES):
        part = pl.ds(j * LANES, LANES)
        infil[pl.ds(j * rows, rows), :] = precip[:, part] * land[:, part].astype(jnp.float32)
        heads[pl.ds(j * rows, rows), :] = head[:, part]

    def body(p, _):
        for r in range(per_peer):
            block = src[p * per_peer + r]
            out[p, pl.ds(r, 1), :] = infil[pl.ds(block, 1), :]
            out[p, pl.ds(per_peer + r, 1), :] = heads[pl.ds(block, 1), :]
        out[p, pl.ds(2 * per_peer, 8), :] = jnp.broadcast_to(labels[pl.ds(p, 1), :], (8, LANES))
        return 0

    lax.fori_loop(0, peers, body, 0)


def owner_kernel(
    peers, per_peer, slots, arrived, rec0, rec_x, rec_y, answer, infil, sig, own_i, own_h, rec
):
    owned = rec0.shape[0]

    def scatter(p, _):
        for r in range(per_peer):
            slot = slots[p * per_peer + r]
            own_i[pl.ds(slot, 1), :] = arrived[p, pl.ds(r, 1), :]
            own_h[pl.ds(slot, 1), :] = arrived[p, pl.ds(per_peer + r, 1), :]
        return 0

    lax.fori_loop(0, peers, scatter, 0)
    rec[pl.ds(owned, 8), :] = jnp.zeros((8, LANES), jnp.float32)

    def combine(g, _):
        part = pl.ds(g * 64, 64)
        inf = own_i[part, :]
        sg = jax.nn.sigmoid(own_h[part, :])
        infil[part, :] = inf
        sig[part, :] = sg
        rec[part, :] = rec0[part, :] + inf * rec_x[part, :] + sg * rec_y[part, :]
        return 0

    lax.fori_loop(0, owned // 64, combine, 0)

    def gather(p, _):
        for r in range(per_peer):
            slot = slots[p * per_peer + r]
            answer[p, pl.ds(r, 1), :] = rec[pl.ds(slot, 1), :]
        return 0

    lax.fori_loop(0, peers, gather, 0)


def factor_kernel(layers, group, moist, ksat, s0, sx, sy, rec0, rec_x, rec_y):
    def body(step, _):
        base_row = step * group
        rows = pl.ds(pl.multiple_of(base_row, group), group)
        recharge, terms = factor_rows(layers, moist, ksat, base_row, group)
        for ref, value in zip((rec0, rec_x, rec_y), recharge):
            ref[rows, :] = value
        for k in range(layers):
            for ref, value in zip((s0, sx, sy), terms[k]):
                ref[k, rows, :] = value
        return 0

    lax.fori_loop(0, ksat.shape[0] // group, body, 0)


def saturation_kernel(layers, s0, sx, sy, infil, sig, out):
    count = infil.shape[0]
    group = 32

    def body(step, _):
        rows = pl.ds(pl.multiple_of(step * group, group), group)
        inf = infil[rows, :]
        sg = sig[rows, :]
        for k in range(layers):
            out[pl.ds(step * group * layers + k, group, stride=layers), :] = (
                s0[k, rows, :] + inf * sx[k, rows, :] + sg * sy[k, rows, :]
            )
        return 0

    lax.fori_loop(0, count // group, body, 0)


def spread_source(
    position, returned, head, land, s_ref,
    sorted_rows, strip_out, from_row, strip_in, corner, send_sem, recv_sem, ready,
):
    rows, cols = head.shape
    high, wide = s_ref.shape
    row, col = lax.axis_index("row"), lax.axis_index("col")
    steps, go, come = neighbours(row, col)
    east, south = cols - LANES, rows - 8
    src = [
        s_ref.at[pl.ds(0, 8), pl.ds(0, cols)],
        s_ref.at[pl.ds(south, 8), pl.ds(0, cols)],
        strip_out.at[0],
        strip_out.at[1],
    ] + [s_ref.at[pl.ds(y, 8), pl.ds(x, LANES)] for y in (0, south) for x in (0, east)]
    dst = [from_row.at[0], from_row.at[1], strip_in.at[0], strip_in.at[1]] + [
        corner.at[c] for c in range(4)
    ]
    for k in range(8):

        @pl.when(jnp.logical_not(come[k]))
        def _(ref=dst[k]):
            ref[...] = jnp.zeros(ref.shape, jnp.float32)

    def fill(j, g):
        base = pl.multiple_of(g * 32, 32)
        for u in range(32):
            at = j * rows + base + u
            place = jnp.clip(position[at], 0, returned.shape[0] - 1)
            sorted_rows[pl.ds(at, 1), :] = returned[pl.ds(place, 1), :]
        at, part = pl.ds(base, 32), pl.ds(j * LANES, LANES)
        s_ref[at, part] = (
            store_rate * (head[at, part] * land[at, part].astype(jnp.float32))
            + recharge_gain * sorted_rows[pl.ds(j * rows + base, 32), :]
        )

    def fill_range(j, low, high):
        def body(g, _):
            fill(j, g)
            return 0

        lax.fori_loop(low, high, body, 0)

    groups, strips = rows // 32, cols // LANES
    fill_range(0, 0, groups)
    fill_range(strips - 1, 0, groups)
    strip_out[0] = jnp.transpose(s_ref[0:rows, 0:LANES])[0:8]
    strip_out[1] = jnp.transpose(s_ref[0:rows, east:cols])[LANES - 8 : LANES]
    for j in range(1, strips - 1):
        fill(j, 0)
        fill(j, groups - 1)
    ready()

    def copy(k):
        return halo_copy(k, steps, row, col, src, dst, send_sem, recv_sem)

    def landed(k):
        return halo_copy(k, [(0, 0)] * 8, row, col, src, dst, send_sem, recv_sem)

    each(go, lambda k: copy(k).start())
    for j in range(1, strips - 1):
        fill_range(j, 1, groups - 1)
    each(go, lambda k: copy(k).wait_send())
    each(come, lambda k: landed(k).wait_recv())
    first = lax.broadcasted_iota(jnp.int32, (8, LANES), 0) < 4
    near = lax.broadcasted_iota(jnp.int32, (8, LANES), 1) < LANES // 2
    for j in range(strips):
        part = slice(j * LANES, (j + 1) * LANES)
        s_ref[rows:high, part] = jnp.where(first, from_row[0, :, part], from_row[1, :, part])
    s_ref[rows:high, cols:wide] = jnp.where(
        first,
        jnp.where(near, corner[0], corner[1]),
        jnp.where(near, corner[2], corner[3]),
    )
    s_ref[0:rows, cols:wide] = jnp.transpose(
        jnp.concatenate(
            [strip_in[0], jnp.zeros((LANES - 16, rows), jnp.float32), strip_in[1]], axis=0
        )
    )


def source_kernel(position, returned, head, land, s_ref, *scratch):
    row, col = lax.axis_index("row"), lax.axis_index("col")
    steps, go, _ = neighbours(row, col)
    barrier = pltpu.get_barrier_semaphore()

    def greet(k):
        pl.semaphore_signal(
            barrier,
            inc=1,
            device_id=(row + steps[k][0], col + steps[k][1]),
            device_id_type=pl.DeviceIdType.MESH,
        )

    each(go, greet)

    def ready():
        pl.semaphore_wait(
            barrier, functools.reduce(lambda x, y: x + y, [f.astype(jnp.int32) for f in go])
        )

    spread_source(position, returned, head, land, s_ref, *scratch, ready)


def relax_kernel(
    pieces, source, head, trans_coef, land, mid_r, mid_c, stepped, out, saturation,
    t_ref, s_ref, fu, fd, fl, fr, a, b, held, read, write,
):
    rows, cols = head.shape
    high, wide = t_ref.shape
    each_rows = stepped.shape[0] // pieces
    parts = [pl.ds(c * each_rows, each_rows) for c in range(pieces)]
    reads = [
        pltpu.make_async_copy(stepped.at[p], held.at[p], read.at[c]) for c, p in enumerate(parts)
    ]
    writes = [
        pltpu.make_async_copy(held.at[p], saturation.at[p], write.at[c])
        for c, p in enumerate(parts)
    ]
    for copy in reads:
        copy.start()
    left = list(range(pieces))

    def pass_piece():
        if left:
            c = left.pop(0)
            reads[c].wait()
            writes[c].start()

    for f, (ref, centre) in enumerate(
        zip((t_ref, a, b), fixed_fields(head[...], trans_coef[...], land[...]))
    ):
        ref[0:rows, 0:cols] = centre
        ref[rows:high, 0:cols] = mid_r[f]
        ref[:, cols:wide] = mid_c[f]
    for g in range(wide // LANES):
        part = slice(g * LANES, (g + 1) * LANES)
        lo = slice((g - 1) % (wide // LANES) * LANES, (g - 1) % (wide // LANES) * LANES + LANES)
        hi = slice((g + 1) % (wide // LANES) * LANES, (g + 1) % (wide // LANES) * LANES + LANES)
        lane = lax.broadcasted_iota(jnp.int32, (high, LANES), 1)
        t = t_ref[:, part]
        tu = 0.5 * (t + pltpu.roll(t, 1, 0))
        td = 0.5 * (t + pltpu.roll(t, high - 1, 0))
        tl = jnp.where(lane == 0, pltpu.roll(t_ref[:, lo], 1, 1), pltpu.roll(t, 1, 1))
        tr = jnp.where(
            lane == LANES - 1,
            pltpu.roll(t_ref[:, hi], LANES - 1, 1),
            pltpu.roll(t, LANES - 1, 1),
        )
        lf = 0.5 * (t + tl)
        rt = 0.5 * (t + tr)
        inv = b[:, part] / (store_rate + (tu + td + lf + rt))
        fu[:, part] = tu * inv
        fd[:, part] = td * inv
        fl[:, part] = lf * inv
        fr[:, part] = rt * inv
        s_ref[:, part] = source[:, part] * inv
        if g > 1:
            pass_piece()
    now, later = a, b
    for sweep in range(SWEEPS):
        last = sweep == SWEEPS - 1
        for g in range(wide // LANES):
            if last and g * LANES >= cols:
                continue
            pass_piece()
            part = slice(g * LANES, (g + 1) * LANES)
            lo = (g - 1) % (wide // LANES) * LANES
            hi = (g + 1) % (wide // LANES) * LANES
            lane = lax.broadcasted_iota(jnp.int32, (high, LANES), 1)
            x = now[:, part]
            xl = jnp.where(
                lane == 0, pltpu.roll(now[:, lo : lo + LANES], 1, 1), pltpu.roll(x, 1, 1)
            )
            xr = jnp.where(
                lane == LANES - 1,
                pltpu.roll(now[:, hi : hi + LANES], LANES - 1, 1),
                pltpu.roll(x, LANES - 1, 1),
            )
            y = s_ref[:, part] + fu[:, part] * pltpu.roll(x, 1, 0)
            y = y + fd[:, part] * pltpu.roll(x, high - 1, 0)
            y = y + (fl[:, part] * xl + fr[:, part] * xr)
            if last:
                out[:, part] = y[0:rows]
            else:
                later[:, part] = y
        now, later = later, now
    while left:
        pass_piece()
    for copy in writes:
        copy.wait()


def on_device(precip, head, trans_coef, land, dest, moisture, ksat):
    tile_rows, tile_cols = precip.shape
    n_col = lax.axis_size("col")
    peers = lax.axis_size("row") * n_col
    me = lax.axis_index("row") * n_col + lax.axis_index("col")
    owned, layers, _ = moisture.shape
    blocks = tile_rows * tile_cols // LANES
    cap = (2 * blocks + peers - 1) // peers
    extra, hop = 2, 4
    depth = (19 * blocks // (16 * peers) + 1 + 7) // 8 * 8
    direct = depth - extra
    lines = 1 << (depth + hop - 1).bit_length()

    target = dest.T.reshape(blocks)
    owner = target // owned
    slot = target - owner * owned
    all_peers = jnp.arange(peers, dtype=jnp.int32)
    one_hot = owner[:, None] == all_peers[None, :]
    order = jnp.arange(blocks, dtype=jnp.int32)
    earlier = (order[None, :] < order[:, None]).astype(jnp.bfloat16)
    counts = jnp.dot(earlier, one_hot.astype(jnp.bfloat16), preferred_element_type=jnp.float32)
    sums = jnp.sum(one_hot.astype(jnp.float32), axis=0)
    over = jnp.maximum(sums - direct, 0.0)
    base = jnp.sum(jnp.where(all_peers[:, None] < all_peers[None, :], over[:, None], 0.0), axis=0)
    rank = jnp.sum(jnp.where(one_hot, counts, 0.0), axis=1).astype(jnp.int32)
    number = jnp.sum(jnp.where(one_hot, counts + base[None, :] - direct, 0.0), axis=1).astype(
        jnp.int32
    )
    spread = rank >= direct
    via = (jnp.maximum(number, 0) + me) % peers
    turn = jnp.clip(number // peers, 0, extra - 1)
    position = jnp.where(
        spread, peers * depth + via * extra + turn, owner * depth + rank
    )
    place = jnp.where(spread, via, owner)
    row_of = jnp.where(spread, direct + turn, rank)

    def table(where, row, width, value):
        hot = (where[:, None] == all_peers[None, :]).astype(jnp.float32)
        at = row[:, None] == jnp.arange(width, dtype=jnp.int32)[None, :]
        return lax.dot_general(
            hot,
            jnp.where(at, value.astype(jnp.float32)[:, None], 0.0),
            (((0,), (0,)), ((), ())),
            precision=lax.Precision.HIGHEST,
            preferred_element_type=jnp.float32,
        )

    source_of = jnp.minimum(table(place, row_of, depth, order).astype(jnp.int32), blocks - 1)
    label = table(owner, rank, LANES, slot - owned) + float(owned)
    sent = jnp.broadcast_to(jnp.pad(sums, (0, LANES - peers))[None, :], (peers, LANES))

    sources, labels, position, owner, rank = lax.optimization_barrier(
        (source_of.reshape(peers * depth), jnp.stack([label, sent], axis=1), position, owner, rank)
    )
    flat = moisture.reshape(owned * layers, LANES)
    vm = lambda *shape: pltpu.VMEM(shape, jnp.float32)
    iv = lambda *shape: pltpu.VMEM(shape, jnp.int32)
    sm = lambda *shape: pltpu.SMEM(shape, jnp.int32)
    dma = lambda n: pltpu.SemaphoreType.DMA((n,))
    chunks = 8
    tail = (peers * extra + depth - 1) // depth
    high, wide = tile_rows + 2 * SWEEPS, tile_cols + LANES
    for_source = [
        vm(blocks, LANES),
        vm(2, 8, tile_rows),
        vm(2, 8, tile_cols),
        vm(2, 8, tile_rows),
        vm(4, 8, LANES),
        dma(8),
        dma(8),
    ]
    source, stepped, fits, mid_r, mid_c = pl.pallas_call(
        functools.partial(column_kernel, cap, extra, hop, chunks),
        out_shape=[
            f32(high, wide),
            f32(owned * layers, LANES),
            f32(1, 1),
            f32(3, 2 * SWEEPS, tile_cols),
            f32(3, high, LANES),
        ],
        in_specs=[SM, SM] + [VM] * 5 + [pl.BlockSpec(memory_space=pl.ANY), VM],
        out_specs=[VM, pl.BlockSpec(memory_space=pl.ANY), VM, VM, VM],
        scratch_shapes=[
            vm((peers + tail) * depth, LANES),
            vm(blocks, LANES),
            vm(blocks, LANES),
            vm(peers, 2, depth, LANES),
            vm(peers, 2, lines, LANES),
            vm(peers, 2, LANES),
        ]
        + [vm(owned * layers, LANES)] * 3
        + [vm(owned, LANES)] * 3
        + [
            vm(peers, 2 * hop, LANES),
            vm(peers, 2 * hop, LANES),
            vm(peers, depth, LANES),
            vm(peers, hop, LANES),
            vm(peers, hop, LANES),
            vm(peers, extra, LANES),
            vm(peers, extra, LANES),
            vm(depth, LANES),
            vm(depth, LANES),
            vm(depth, LANES),
            iv(8, LANES),
            iv(extra * peers, LANES),
            iv(peers, LANES),
            iv(8, LANES),
            iv(owned // LANES, LANES),
            vm(2, 24, tile_cols),
            vm(2, 24, tile_rows),
            vm(2, 24, tile_cols),
            vm(2, 24, tile_rows),
            vm(4, 24, LANES),
            sm(peers, LANES),
            sm(8, LANES),
            sm(8, LANES),
            sm(extra * peers, LANES),
            sm(owned // LANES, LANES),
            dma(5),
            dma(chunks),
            dma(chunks),
        ]
        + [dma(peers)] * 12
        + [dma(6), dma(8), dma(8)]
        + for_source,
        compiler_params=pltpu.CompilerParams(
            collective_id=4, has_side_effects=True, vmem_limit_bytes=58 * 2**20
        ),
    )(sources, position, labels, precip, head, trans_coef, land, flat, ksat)


    def relax(source, stepped):
        pieces = 16
        surface, saturation = pl.pallas_call(
            functools.partial(relax_kernel, pieces),
            out_shape=[f32(tile_rows, tile_cols), f32(owned * layers, LANES)],
            in_specs=[VM] * 6 + [pl.BlockSpec(memory_space=pl.ANY)],
            out_specs=[VM, pl.BlockSpec(memory_space=pl.ANY)],
            scratch_shapes=[vm(high, wide)] * 8
            + [vm(owned * layers, LANES), dma(pieces), dma(pieces)],
            compiler_params=pltpu.CompilerParams(vmem_limit_bytes=40 * 2**20),
        )(source, head, trans_coef, land, mid_r, mid_c, stepped)
        return saturation.reshape(owned, layers, LANES), surface

    def hopped():
        return relax(source, stepped)

    def whole():
        step = 128
        layered = pl.BlockSpec((layers, step, LANES), lambda i: (0, i, 0))
        single = pl.BlockSpec((step, LANES), lambda i: (i, 0))
        natural = pl.BlockSpec((step * layers, LANES), lambda i: (i, 0))
        s0, sx, sy, rec0, rec_x, rec_y = pl.pallas_call(
            functools.partial(factor_kernel, layers, 32),
            grid=(owned // step,),
            out_shape=[f32(layers, owned, LANES)] * 3 + [f32(owned, LANES)] * 3,
            in_specs=[natural, single],
            out_specs=[layered] * 3 + [single] * 3,
        )(flat, ksat)
        slots_of = table(owner, rank, cap, order).astype(jnp.int32).reshape(peers * cap)
        outgoing = pl.pallas_call(
            functools.partial(pack_kernel, peers, cap),
            out_shape=f32(peers, 2 * cap + 8, LANES),
            in_specs=[SM, VM, VM, VM, VM],
            out_specs=VM,
            scratch_shapes=[pltpu.VMEM((blocks, LANES), jnp.float32)] * 2,
        )(slots_of, labels[:, 0], precip, head, land)
        arrived = lax.all_to_all(outgoing, ("row", "col"), split_axis=0, concat_axis=0, tiled=True)
        places = arrived[:, 2 * cap, :cap].astype(jnp.int32).reshape(peers * cap)
        answer, infil, sig = pl.pallas_call(
            functools.partial(owner_kernel, peers, cap),
            out_shape=[f32(peers, cap, LANES), f32(owned, LANES), f32(owned, LANES)],
            in_specs=[SM, VM, VM, VM, VM],
            out_specs=[VM] * 3,
            scratch_shapes=[pltpu.VMEM((owned + 8, LANES), jnp.float32)] * 3,
        )(places, arrived, rec0, rec_x, rec_y)
        back = lax.all_to_all(answer, ("row", "col"), split_axis=0, concat_axis=0, tiled=True)
        saturation = pl.pallas_call(
            functools.partial(saturation_kernel, layers),
            grid=(owned // step,),
            out_shape=f32(owned * layers, LANES),
            in_specs=[layered] * 3 + [single] * 2,
            out_specs=natural,
        )(s0, sx, sy, infil, sig)
        source = pl.pallas_call(
            source_kernel,
            out_shape=f32(high, wide),
            in_specs=[SM] + [VM] * 3,
            out_specs=VM,
            scratch_shapes=for_source,
            compiler_params=pltpu.CompilerParams(collective_id=2, has_side_effects=True),
        )(owner * cap + rank, back.reshape(-1, LANES), head, land)
        return relax(source, saturation)

    return lax.cond(fits.reshape(()) > 0.5, hopped, whole)


def solution(mesh):
    tile = P("row", "col")
    placed = (
        tile,
        tile,
        tile,
        tile,
        tile,
        P(("row", "col"), None, None),
        P(("row", "col"), None),
    )
    return jax.shard_map(
        on_device,
        mesh=mesh,
        in_specs=placed,
        out_specs=(P(("row", "col"), None, None), P("row", "col")),
        check_vma=False,
    )
```

```python
import functools
import math

import jax
import jax.numpy as jnp
from jax import lax
from jax.experimental import pallas as pl
from jax.experimental.pallas import tpu as pltpu
from jax.sharding import PartitionSpec as P

SWEEPS = 4
LANES = 128

layer_depth = 0.1
step_ratio = 0.1
residual_water = 0.05
pore_range = 0.4
diff_length = 0.5
couple_rate = 0.05
recharge_gain = 20.0
store_rate = 0.2

VM = pl.BlockSpec(memory_space=pltpu.VMEM)
SM = pl.BlockSpec(memory_space=pltpu.SMEM)


def f32(*shape):
    return jax.ShapeDtypeStruct(shape, jnp.float32)


def factor_rows(layers, moist, ksat, base_row, group):
    rows = pl.ds(pl.multiple_of(base_row, group), group)
    ks = ksat[rows, :]
    ratios, reds, xs = [], [], []
    before = None
    for k in range(layers):
        m = moist[pl.ds(base_row * layers + k, group, stride=layers), :]
        w = (m - residual_water) * (1.0 / pore_range)
        s = ks * math.exp(-(k + 0.5) * layer_depth)
        sw2 = s * (w * w)
        hs = sw2 * (1.5 / pore_range)
        d = s * (0.2 * diff_length / (2.0 * layer_depth)) + sw2 * (
            diff_length / (2.0 * layer_depth)
        )
        hc = 0.5 * (sw2 * w)
        cur = (m, hs, d, hc)
        if before is None:
            before = cur
            g_up = q_up = nsub = None
            continue
        m0, hs0, d0, hc0 = before
        g = d0 + d
        q = (hc0 + hc) - g * (m - m0)
        if g_up is None:
            pivot = step_ratio + g + hs0
            inv = 1.0 / pivot
            reds.append(-q * inv)
            xs.append(inv)
        else:
            pivot = step_ratio + g_up + g - nsub * ratios[-1]
            inv = 1.0 / pivot
            reds.append(((q_up - q) + nsub * reds[-1]) * inv)
            xs.append(nsub * inv * xs[-1])
        ratios.append((g - hs) * inv)
        nsub = hs0 + g
        g_up, q_up = g, q
        before = cur
    m, hs, d, hc = before
    bottom = 2.0 * hc + couple_rate * (m - residual_water)
    pivot = step_ratio + g_up + hs + couple_rate - nsub * ratios[-1]
    inv = 1.0 / pivot
    change = ((q_up - bottom) + nsub * reds[-1]) * inv
    cx = nsub * inv * xs[-1]
    cy = (couple_rate * pore_range) * inv
    gain = 2.0 * hs + couple_rate
    recharge = (
        bottom + gain * change,
        gain * cx,
        gain * cy - couple_rate * pore_range,
    )
    unit = 1.0 / pore_range
    terms = [None] * layers
    for k in range(layers - 1, -1, -1):
        if k < layers - 1:
            change = reds[k] + ratios[k] * change
            cx = xs[k] + ratios[k] * cx
            cy = ratios[k] * cy
        m = moist[pl.ds(base_row * layers + k, group, stride=layers), :]
        terms[k] = ((m + change - residual_water) * unit, cx * unit, cy * unit)
    return recharge, terms


def within(index, size):
    if size & (size - 1) == 0:
        return jnp.bitwise_and(index, size - 1)
    return jnp.clip(index, 0, size - 1)


def fixed_fields(head, trans_coef, land):
    share = land.astype(jnp.float32)
    return trans_coef * (1.0 + 0.5 * jnp.tanh(head)), head * share, share


def neighbours(row, col):
    n_row, n_col = lax.axis_size("row"), lax.axis_size("col")
    up, down = row > 0, row < n_row - 1
    left, right = col > 0, col < n_col - 1
    steps = [(-1, 0), (1, 0), (0, -1), (0, 1), (-1, -1), (-1, 1), (1, -1), (1, 1)]
    go = [up, down, left, right, up & left, up & right, down & left, down & right]
    come = [down, up, right, left, down & right, down & left, up & right, up & left]
    return steps, go, come


def each(flags, act):
    for k, flag in enumerate(flags):
        pl.when(flag)(functools.partial(act, k))


def halo_copy(k, steps, row, col, src, dst, send_sem, recv_sem):
    return pltpu.make_async_remote_copy(
        src_ref=src[k],
        dst_ref=dst[k],
        send_sem=send_sem.at[k],
        recv_sem=recv_sem.at[k],
        device_id=(row + steps[k][0], col + steps[k][1]),
        device_id_type=pl.DeviceIdType.MESH,
    )


def column_kernel(
    cap, extra, hop, chunks, src, position, labels, precip, head, trans_coef, land, moisture, ksat,
    s_ref, saturation, fits, mid_r, mid_c, returned,
    infil, sigs, out, allbuf, labs, moist, sx, sy, rec0, rec_x, rec_y,
    mid_out, arr2, ans, ans2, arr4, out5, arr5, g0, gx, gy, src_v, ret_v, slots_v, slot2_v, inv_v,
    row_out, strip_out, from_row, strip_in, corner,
    slots_s, slot2_s, src_s, ret_s, inv_s,
    move, read, write, send0, recv0, send1, recv1, send2, recv2, send3, recv3, send4, recv4, send5, recv5, own,
    send_h, recv_h, *for_source,
):
    rows, cols = precip.shape
    peers, _, lines, _ = allbuf.shape
    depth = out.shape[2]
    direct = depth - extra
    owned = rec0.shape[0]
    layers = moist.shape[0] // owned
    n_col = lax.axis_size("col")
    row, col = lax.axis_index("row"), lax.axis_index("col")
    me = row * n_col + col
    barrier = pltpu.get_barrier_semaphore()
    part_rows = owned // chunks

    def fetch(c):
        part = pl.ds(c * part_rows * layers, part_rows * layers)
        return pltpu.make_async_copy(moisture.at[part], moist.at[part], read.at[c])

    def flush(c):
        part = pl.ds(c * part_rows * layers, part_rows * layers)
        return pltpu.make_async_copy(moist.at[part], saturation.at[part], write.at[c])

    def where_is(k):
        p = lax.rem(me + k, peers)
        return p, (p // n_col, lax.rem(p, n_col))

    def greet(k, _):
        pl.semaphore_signal(
            barrier, inc=1, device_id=where_is(k)[1], device_id_type=pl.DeviceIdType.MESH
        )
        return 0

    lax.fori_loop(1, peers, greet, 0)
    for c in range(chunks):
        fetch(c).start()

    def exchange(src, dst, send, recv, self_sem):
        def copy(k):
            p, place = where_is(k)
            return pltpu.make_async_remote_copy(
                src_ref=src(p),
                dst_ref=dst(me),
                send_sem=send.at[k],
                recv_sem=recv.at[k],
                device_id=place,
                device_id_type=pl.DeviceIdType.MESH,
            )

        here = pltpu.make_async_copy(src(me), dst(me), self_sem)

        def start(low, high):
            def body(k, _):
                copy(k).start()
                return 0

            lax.fori_loop(low, high, body, 0)

        def wait():
            def body(k, _):
                copy(k).wait()
                return 0

            lax.fori_loop(1, peers, body, 0)
            here.wait()

        return copy, here, start, wait

    for j in range(cols // LANES):
        part = pl.ds(j * LANES, LANES)
        infil[pl.ds(j * rows, rows), :] = precip[:, part] * land[:, part].astype(jnp.float32)
        sigs[pl.ds(j * rows, rows), :] = jax.nn.sigmoid(head[:, part])

    def pack(p):
        for r in range(depth):
            block = within(src[p, r], infil.shape[0])
            out[p, 0, pl.ds(r, 1), :] = infil[pl.ds(block, 1), :]
            out[p, 1, pl.ds(r, 1), :] = sigs[pl.ds(block, 1), :]

    _, here0, start0, wait0 = exchange(
        lambda p: labels.at[p], lambda p: labs.at[p], send0, recv0, own.at[5]
    )
    copy1, here1, _, _ = exchange(
        lambda p: out.at[p], lambda p: allbuf.at[p, :, pl.ds(0, depth)], send1, recv1, own.at[0]
    )
    pl.semaphore_wait(barrier, peers - 1)
    def ship(k, _):
        k = peers - k
        pack(where_is(k)[0])
        copy1(k).start()
        return 0

    ahead = min(5, peers)
    lax.fori_loop(1, ahead, ship, 0)
    here0.start()
    start0(1, peers)
    lax.fori_loop(ahead, peers, ship, 0)
    pack(me)
    here1.start()

    steps, go, come = neighbours(row, col)
    east, south = cols - LANES, rows - 8
    for side, at in enumerate((0, south)):
        edge = pl.ds(at, 8)
        for f, field in enumerate(fixed_fields(head[edge, :], trans_coef[edge, :], land[edge, :])):
            row_out[side, pl.ds(8 * f, 8), :] = field
    for side, at in enumerate((0, east)):
        edge = pl.ds(at, LANES)
        keep = slice(0, 8) if side == 0 else slice(LANES - 8, LANES)
        for f, field in enumerate(fixed_fields(head[:, edge], trans_coef[:, edge], land[:, edge])):
            strip_out[side, pl.ds(8 * f, 8), :] = jnp.transpose(field)[keep]
    halo_dst = [from_row.at[0], from_row.at[1], strip_in.at[0], strip_in.at[1]] + [
        corner.at[c] for c in range(4)
    ]
    halo_src = [row_out.at[0], row_out.at[1], strip_out.at[0], strip_out.at[1]] + [
        row_out.at[c // 2, :, pl.ds((c % 2) * east, LANES)] for c in range(4)
    ]
    for k in range(8):

        @pl.when(jnp.logical_not(come[k]))
        def _(ref=halo_dst[k]):
            ref[...] = jnp.zeros(ref.shape, jnp.float32)

    def halo(k):
        return halo_copy(k, steps, row, col, halo_src, halo_dst, send_h, recv_h)

    each(go, lambda k: halo(k).start())

    group = 32

    def factor(c, _):
        fetch(c).wait()

        def body(i, _):
            base_row = pl.multiple_of(c * part_rows + i * group, group)
            at = pl.ds(base_row, group)
            recharge, terms = factor_rows(layers, moist, ksat, base_row, group)
            for ref, value in zip((rec0, rec_x, rec_y), recharge):
                ref[at, :] = value
            for k in range(layers):
                for ref, value in zip((moist, sx, sy), terms[k]):
                    ref[pl.ds(base_row * layers + k, group, stride=layers), :] = value
            return 0

        lax.fori_loop(0, part_rows // group, body, 0)
        return 0

    lax.fori_loop(0, chunks, factor, 0)
    wait0()

    shape = (peers, LANES)
    lane = lax.broadcasted_iota(jnp.int32, shape, 1)
    sub = lax.broadcasted_iota(jnp.int32, shape, 0)
    lab = labs[:, 0, :]
    count = labs[:, 1, :]
    over = jnp.maximum(count - direct, 0.0)
    tri = lax.broadcasted_iota(jnp.int32, (LANES, LANES), 0) < lax.broadcasted_iota(
        jnp.int32, (LANES, LANES), 1
    )
    base = jnp.dot(
        over, tri.astype(jnp.float32), precision=lax.Precision.HIGHEST,
        preferred_element_type=jnp.float32,
    )
    total = extra * peers
    before = (
        lax.broadcasted_iota(jnp.int32, (total, total), 1)
        < lax.broadcasted_iota(jnp.int32, (total, total), 0)
    ).astype(jnp.float32)

    def number(m):
        gap = m - sub
        return jnp.where(gap < 0, gap + peers, gap).astype(jnp.float32)

    def holds(j, first, many, t):
        j = j + float(t * peers)
        return jnp.where((first <= j) & (j < first + many), 1.0, 0.0)

    def prefix(v):
        return jnp.dot(before, v, preferred_element_type=jnp.float32)

    flane = lane.astype(jnp.float32)
    code = sub.astype(jnp.float32) * 8.0
    via = jnp.concatenate([holds(number(me), base, over, t) for t in range(extra)], axis=0)
    rank = prefix(via)
    codes = jnp.concatenate([code + float(t) for t in range(extra)], axis=0)
    lanes = jnp.concatenate([flane] * extra, axis=0)
    back = jnp.sum(via * (lanes * hop + rank), axis=1, keepdims=True)
    ret_v[...] = jnp.broadcast_to(back, (total, LANES)).astype(jnp.int32)
    pad = jnp.zeros((8 - hop, LANES), jnp.float32)
    picks = [
        jnp.sum(jnp.where(rank == float(e), via * codes, 0.0), axis=0, keepdims=True)
        for e in range(hop)
    ]
    src_v[...] = jnp.concatenate(picks + [pad], axis=0).astype(jnp.int32)
    mine = jnp.where(lane == me, 1.0, 0.0)
    first = jnp.sum(base * mine, axis=1, keepdims=True)
    many = jnp.sum(over * mine, axis=1, keepdims=True)
    inside = jnp.where(lane < peers, 1.0, 0.0)
    step = number(lane)
    took = [holds(step, first, many, t) * inside for t in range(extra)]
    value = []
    for t in range(extra):
        at = step + float(t * peers) - first
        v = jnp.zeros(shape, jnp.float32)
        for r in range(cap - direct):
            v = jnp.where(at == float(r), lab[:, direct + r : direct + r + 1] - float(owned), v)
        value.append(v)
    took = jnp.concatenate(took, axis=0)
    rank = prefix(took)
    value = jnp.concatenate(value, axis=0)
    picks = [
        jnp.sum(jnp.where(rank == float(e), took * value, 0.0), axis=0, keepdims=True)
        for e in range(hop)
    ]
    hopped = jnp.concatenate(picks + [pad], axis=0) + float(owned)
    slot2_v[...] = hopped.astype(jnp.int32)
    slots_v[...] = lab.astype(jnp.int32)
    moves = [
        pltpu.make_async_copy(src_v, src_s, move.at[0]),
        pltpu.make_async_copy(slots_v, slots_s, move.at[1]),
        pltpu.make_async_copy(slot2_v, slot2_s, move.at[2]),
        pltpu.make_async_copy(ret_v, ret_s, move.at[3]),
    ]
    for m in moves:
        m.start()
    g0[...] = jnp.zeros(g0.shape, jnp.float32)
    gx[...] = jnp.zeros(gx.shape, jnp.float32)
    gy[...] = jnp.zeros(gy.shape, jnp.float32)
    for m in moves:
        m.wait()

    def answer(q):
        for r in range(direct):
            slot = within(slots_s[q, r], owned)
            g0[pl.ds(r, 1), :] = rec0[pl.ds(slot, 1), :]
            gx[pl.ds(r, 1), :] = rec_x[pl.ds(slot, 1), :]
            gy[pl.ds(r, 1), :] = rec_y[pl.ds(slot, 1), :]
        ans[q] = (
            g0[...]
            + allbuf[q, 0, pl.ds(0, depth), :] * gx[...]
            + allbuf[q, 1, pl.ds(0, depth), :] * gy[...]
        )

    here1.wait()
    answer(me)

    def receive(k, _):
        k = peers - k
        copy1(k).wait_recv()
        answer(lax.rem(me + peers - k, peers))
        return 0

    lax.fori_loop(1, peers, receive, 0)

    def pass_on(d, _):
        for e in range(hop):
            q = src_s[e, d]
            s = jnp.clip(q // 8, 0, peers - 1)
            t = jnp.clip(q - s * 8, 0, extra - 1)
            mid_out[d, pl.ds(e, 1), :] = allbuf[s, 0, pl.ds(direct + t, 1), :]
            mid_out[d, pl.ds(hop + e, 1), :] = allbuf[s, 1, pl.ds(direct + t, 1), :]
        return 0

    lax.fori_loop(0, peers, pass_on, 0)
    _, here2, start2, wait2 = exchange(
        lambda p: mid_out.at[p], lambda p: arr2.at[p], send2, recv2, own.at[1]
    )
    _, here3, start3, wait3 = exchange(
        lambda p: ans.at[p],
        lambda p: returned.at[pl.ds(pl.multiple_of(p * depth, 8), depth)],
        send3, recv3, own.at[2]
    )
    _, here4, start4, wait4 = exchange(
        lambda p: ans2.at[p], lambda p: arr4.at[p], send4, recv4, own.at[3]
    )
    _, here5, start5, wait5 = exchange(
        lambda p: out5.at[p], lambda p: arr5.at[p], send5, recv5, own.at[4]
    )
    thirds = [1, peers // 3, 2 * peers // 3, peers]
    here2.start()
    start2(1, peers)
    here3.start()
    start3(thirds[0], thirds[1])

    columns = jnp.transpose(
        jnp.concatenate([hopped, jnp.zeros((LANES - 8, LANES), jnp.float32)], axis=0)
    )
    place = sub.astype(jnp.float32) * float(lines)
    for g in range(owned // LANES):
        want = flane + float(g * LANES)
        found = jnp.zeros(shape, jnp.float32)
        for r in range(direct):
            found = jnp.where(lab[:, r : r + 1] == want, place + float(r), found)
        for e in range(hop):
            found = jnp.where(
                columns[0:peers, e : e + 1] == want, place + float(depth + e), found
            )
        inv_v[pl.ds(g, 1), :] = jnp.sum(found, axis=0, keepdims=True).astype(jnp.int32)
    turn = pltpu.make_async_copy(inv_v, inv_s, move.at[4])
    turn.start()

    def widest(m, most):
        n = number(m)
        seen = functools.reduce(lambda x, y: x + y, [holds(n, base, over, t) for t in range(extra)])
        return jnp.maximum(most, jnp.sum(seen, axis=0, keepdims=True))

    most = lax.fori_loop(0, peers, widest, jnp.zeros((1, LANES), jnp.float32))
    spread = jnp.max(jnp.sum(over, axis=1, keepdims=True), axis=0, keepdims=True)
    bad = jnp.maximum(
        jnp.where(jnp.max(most, axis=1, keepdims=True) > float(hop), 1.0, 0.0),
        jnp.where(spread > float(total), 1.0, 0.0),
    )
    fits[...] = jnp.broadcast_to(1.0 - bad, fits.shape)

    def landed(k):
        return pltpu.make_async_remote_copy(
            src_ref=halo_src[k],
            dst_ref=halo_dst[k],
            send_sem=send_h.at[k],
            recv_sem=recv_h.at[k],
            device_id=(row, col),
            device_id_type=pl.DeviceIdType.MESH,
        )

    each(go, lambda k: halo(k).wait_send())
    each(come, lambda k: landed(k).wait_recv())
    upper = lax.broadcasted_iota(jnp.int32, (8, LANES), 0) < 4
    near = lax.broadcasted_iota(jnp.int32, (8, LANES), 1) < LANES // 2
    for f in range(3):
        eight = pl.ds(8 * f, 8)
        for j in range(cols // LANES):
            part = pl.ds(j * LANES, LANES)
            mid_r[f, :, part] = jnp.where(upper, from_row[0, eight, part], from_row[1, eight, part])
        mid_c[f, pl.ds(rows, 8), :] = jnp.where(
            upper,
            jnp.where(near, corner[0, eight, :], corner[1, eight, :]),
            jnp.where(near, corner[2, eight, :], corner[3, eight, :]),
        )
        mid_c[f, pl.ds(0, rows), :] = jnp.transpose(
            jnp.concatenate(
                [
                    strip_in[0, eight, :],
                    jnp.zeros((LANES - 16, rows), jnp.float32),
                    strip_in[1, eight, :],
                ],
                axis=0,
            )
        )
    turn.wait()
    wait2()

    def answer2(m, _):
        for e in range(hop):
            slot = within(slot2_s[e, m], owned)
            inf, sg = arr2[m, pl.ds(e, 1), :], arr2[m, pl.ds(hop + e, 1), :]
            ans2[m, pl.ds(e, 1), :] = (
                rec0[pl.ds(slot, 1), :]
                + inf * rec_x[pl.ds(slot, 1), :]
                + sg * rec_y[pl.ds(slot, 1), :]
            )
            allbuf[m, 0, pl.ds(depth + e, 1), :] = inf
            allbuf[m, 1, pl.ds(depth + e, 1), :] = sg
        return 0

    lax.fori_loop(0, peers, answer2, 0)
    here4.start()
    start4(1, peers)
    start3(thirds[1], thirds[2])

    def finish(c, _):
        def body(i, _):
            for u in range(8):
                n = c * part_rows + i * 8 + u
                v = inv_s[n // LANES, lax.rem(n, LANES)]
                p = jnp.minimum(lax.shift_right_logical(v, bits), peers - 1)
                r = jnp.bitwise_and(v, lines - 1)
                inf = allbuf[p, 0, pl.ds(r, 1), :]
                sg = allbuf[p, 1, pl.ds(r, 1), :]
                at = pl.ds(pl.multiple_of(n * layers, layers), layers)
                moist[at, :] = moist[at, :] + inf * sx[at, :] + sg * sy[at, :]
            return 0

        lax.fori_loop(0, part_rows // 8, body, 0)
        flush(c).start()
        return 0

    bits = lines.bit_length() - 1
    lax.fori_loop(0, chunks // 2, finish, 0)
    wait4()

    def hand_back(s, _):
        for t in range(extra):
            at = jnp.clip(ret_s[t * peers + s, 0], 0, peers * hop - 1)
            d = at // hop
            out5[s, pl.ds(t, 1), :] = arr4[d, pl.ds(at - d * hop, 1), :]
        return 0

    lax.fori_loop(0, peers, hand_back, 0)
    here5.start()
    start5(1, peers)
    start3(thirds[2], thirds[3])
    lax.fori_loop(chunks // 2, chunks, finish, 0)

    wait5()
    for i in range(total):
        returned[pl.ds(peers * depth + i, 1), :] = arr5[i // extra, pl.ds(i % extra, 1), :]
    wait3()
    spread_source(
        position, returned, head, land, s_ref, *for_source, ready=lambda: None
    )

    def sent(k, _):
        copy1(k).wait_send()
        return 0

    lax.fori_loop(1, peers, sent, 0)
    for c in range(chunks):
        flush(c).wait()


def pack_kernel(peers, per_peer, src, labels, precip, head, land, out, infil, heads):
    rows, cols = precip.shape
    for j in range(cols // LANES):
        part = pl.ds(j * LANES, LANES)
        infil[pl.ds(j * rows, rows), :] = precip[:, part] * land[:, part].astype(jnp.float32)
        heads[pl.ds(j * rows, rows), :] = head[:, part]

    def body(p, _):
        for r in range(per_peer):
            block = src[p * per_peer + r]
            out[p, pl.ds(r, 1), :] = infil[pl.ds(block, 1), :]
            out[p, pl.ds(per_peer + r, 1), :] = heads[pl.ds(block, 1), :]
        out[p, pl.ds(2 * per_peer, 8), :] = jnp.broadcast_to(labels[pl.ds(p, 1), :], (8, LANES))
        return 0

    lax.fori_loop(0, peers, body, 0)


def owner_kernel(
    peers, per_peer, slots, arrived, rec0, rec_x, rec_y, answer, infil, sig, own_i, own_h, rec
):
    owned = rec0.shape[0]

    def scatter(p, _):
        for r in range(per_peer):
            slot = slots[p * per_peer + r]
            own_i[pl.ds(slot, 1), :] = arrived[p, pl.ds(r, 1), :]
            own_h[pl.ds(slot, 1), :] = arrived[p, pl.ds(per_peer + r, 1), :]
        return 0

    lax.fori_loop(0, peers, scatter, 0)
    rec[pl.ds(owned, 8), :] = jnp.zeros((8, LANES), jnp.float32)

    def combine(g, _):
        part = pl.ds(g * 64, 64)
        inf = own_i[part, :]
        sg = jax.nn.sigmoid(own_h[part, :])
        infil[part, :] = inf
        sig[part, :] = sg
        rec[part, :] = rec0[part, :] + inf * rec_x[part, :] + sg * rec_y[part, :]
        return 0

    lax.fori_loop(0, owned // 64, combine, 0)

    def gather(p, _):
        for r in range(per_peer):
            slot = slots[p * per_peer + r]
            answer[p, pl.ds(r, 1), :] = rec[pl.ds(slot, 1), :]
        return 0

    lax.fori_loop(0, peers, gather, 0)


def factor_kernel(layers, group, moist, ksat, s0, sx, sy, rec0, rec_x, rec_y):
    def body(step, _):
        base_row = step * group
        rows = pl.ds(pl.multiple_of(base_row, group), group)
        recharge, terms = factor_rows(layers, moist, ksat, base_row, group)
        for ref, value in zip((rec0, rec_x, rec_y), recharge):
            ref[rows, :] = value
        for k in range(layers):
            for ref, value in zip((s0, sx, sy), terms[k]):
                ref[k, rows, :] = value
        return 0

    lax.fori_loop(0, ksat.shape[0] // group, body, 0)


def saturation_kernel(layers, s0, sx, sy, infil, sig, out):
    count = infil.shape[0]
    group = 32

    def body(step, _):
        rows = pl.ds(pl.multiple_of(step * group, group), group)
        inf = infil[rows, :]
        sg = sig[rows, :]
        for k in range(layers):
            out[pl.ds(step * group * layers + k, group, stride=layers), :] = (
                s0[k, rows, :] + inf * sx[k, rows, :] + sg * sy[k, rows, :]
            )
        return 0

    lax.fori_loop(0, count // group, body, 0)


def spread_source(
    position, returned, head, land, s_ref,
    sorted_rows, strip_out, from_row, strip_in, corner, send_sem, recv_sem, ready,
):
    rows, cols = head.shape
    high, wide = s_ref.shape
    row, col = lax.axis_index("row"), lax.axis_index("col")
    steps, go, come = neighbours(row, col)
    east, south = cols - LANES, rows - 8
    src = [
        s_ref.at[pl.ds(0, 8), pl.ds(0, cols)],
        s_ref.at[pl.ds(south, 8), pl.ds(0, cols)],
        strip_out.at[0],
        strip_out.at[1],
    ] + [s_ref.at[pl.ds(y, 8), pl.ds(x, LANES)] for y in (0, south) for x in (0, east)]
    dst = [from_row.at[0], from_row.at[1], strip_in.at[0], strip_in.at[1]] + [
        corner.at[c] for c in range(4)
    ]
    for k in range(8):

        @pl.when(jnp.logical_not(come[k]))
        def _(ref=dst[k]):
            ref[...] = jnp.zeros(ref.shape, jnp.float32)

    def fill(j, g):
        base = pl.multiple_of(g * 32, 32)
        for u in range(32):
            at = j * rows + base + u
            place = jnp.clip(position[at], 0, returned.shape[0] - 1)
            sorted_rows[pl.ds(at, 1), :] = returned[pl.ds(place, 1), :]
        at, part = pl.ds(base, 32), pl.ds(j * LANES, LANES)
        s_ref[at, part] = (
            store_rate * (head[at, part] * land[at, part].astype(jnp.float32))
            + recharge_gain * sorted_rows[pl.ds(j * rows + base, 32), :]
        )

    def fill_range(j, low, high):
        def body(g, _):
            fill(j, g)
            return 0

        lax.fori_loop(low, high, body, 0)

    groups, strips = rows // 32, cols // LANES
    fill_range(0, 0, groups)
    fill_range(strips - 1, 0, groups)
    strip_out[0] = jnp.transpose(s_ref[0:rows, 0:LANES])[0:8]
    strip_out[1] = jnp.transpose(s_ref[0:rows, east:cols])[LANES - 8 : LANES]
    for j in range(1, strips - 1):
        fill(j, 0)
        fill(j, groups - 1)
    ready()

    def copy(k):
        return halo_copy(k, steps, row, col, src, dst, send_sem, recv_sem)

    def landed(k):
        return halo_copy(k, [(0, 0)] * 8, row, col, src, dst, send_sem, recv_sem)

    each(go, lambda k: copy(k).start())
    for j in range(1, strips - 1):
        fill_range(j, 1, groups - 1)
    each(go, lambda k: copy(k).wait_send())
    each(come, lambda k: landed(k).wait_recv())
    first = lax.broadcasted_iota(jnp.int32, (8, LANES), 0) < 4
    near = lax.broadcasted_iota(jnp.int32, (8, LANES), 1) < LANES // 2
    for j in range(strips):
        part = slice(j * LANES, (j + 1) * LANES)
        s_ref[rows:high, part] = jnp.where(first, from_row[0, :, part], from_row[1, :, part])
    s_ref[rows:high, cols:wide] = jnp.where(
        first,
        jnp.where(near, corner[0], corner[1]),
        jnp.where(near, corner[2], corner[3]),
    )
    s_ref[0:rows, cols:wide] = jnp.transpose(
        jnp.concatenate(
            [strip_in[0], jnp.zeros((LANES - 16, rows), jnp.float32), strip_in[1]], axis=0
        )
    )


def source_kernel(position, returned, head, land, s_ref, *scratch):
    row, col = lax.axis_index("row"), lax.axis_index("col")
    steps, go, _ = neighbours(row, col)
    barrier = pltpu.get_barrier_semaphore()

    def greet(k):
        pl.semaphore_signal(
            barrier,
            inc=1,
            device_id=(row + steps[k][0], col + steps[k][1]),
            device_id_type=pl.DeviceIdType.MESH,
        )

    each(go, greet)

    def ready():
        pl.semaphore_wait(
            barrier, functools.reduce(lambda x, y: x + y, [f.astype(jnp.int32) for f in go])
        )

    spread_source(position, returned, head, land, s_ref, *scratch, ready)


def relax_kernel(
    pieces, source, head, trans_coef, land, mid_r, mid_c, stepped, out, saturation,
    t_ref, s_ref, fu, fd, fl, fr, a, b, held, read, write,
):
    rows, cols = head.shape
    high, wide = t_ref.shape
    each_rows = stepped.shape[0] // pieces
    parts = [pl.ds(c * each_rows, each_rows) for c in range(pieces)]
    reads = [
        pltpu.make_async_copy(stepped.at[p], held.at[p], read.at[c]) for c, p in enumerate(parts)
    ]
    writes = [
        pltpu.make_async_copy(held.at[p], saturation.at[p], write.at[c])
        for c, p in enumerate(parts)
    ]
    for copy in reads:
        copy.start()
    left = list(range(pieces))

    def pass_piece():
        if left:
            c = left.pop(0)
            reads[c].wait()
            writes[c].start()

    for f, (ref, centre) in enumerate(
        zip((t_ref, a, b), fixed_fields(head[...], trans_coef[...], land[...]))
    ):
        ref[0:rows, 0:cols] = centre
        ref[rows:high, 0:cols] = mid_r[f]
        ref[:, cols:wide] = mid_c[f]
    for g in range(wide // LANES):
        part = slice(g * LANES, (g + 1) * LANES)
        lo = slice((g - 1) % (wide // LANES) * LANES, (g - 1) % (wide // LANES) * LANES + LANES)
        hi = slice((g + 1) % (wide // LANES) * LANES, (g + 1) % (wide // LANES) * LANES + LANES)
        lane = lax.broadcasted_iota(jnp.int32, (high, LANES), 1)
        t = t_ref[:, part]
        tu = 0.5 * (t + pltpu.roll(t, 1, 0))
        td = 0.5 * (t + pltpu.roll(t, high - 1, 0))
        tl = jnp.where(lane == 0, pltpu.roll(t_ref[:, lo], 1, 1), pltpu.roll(t, 1, 1))
        tr = jnp.where(
            lane == LANES - 1,
            pltpu.roll(t_ref[:, hi], LANES - 1, 1),
            pltpu.roll(t, LANES - 1, 1),
        )
        lf = 0.5 * (t + tl)
        rt = 0.5 * (t + tr)
        inv = b[:, part] / (store_rate + (tu + td + lf + rt))
        fu[:, part] = tu * inv
        fd[:, part] = td * inv
        fl[:, part] = lf * inv
        fr[:, part] = rt * inv
        s_ref[:, part] = source[:, part] * inv
        if g > 1:
            pass_piece()
    now, later = a, b
    for sweep in range(SWEEPS):
        last = sweep == SWEEPS - 1
        for g in range(wide // LANES):
            if last and g * LANES >= cols:
                continue
            pass_piece()
            part = slice(g * LANES, (g + 1) * LANES)
            lo = (g - 1) % (wide // LANES) * LANES
            hi = (g + 1) % (wide // LANES) * LANES
            lane = lax.broadcasted_iota(jnp.int32, (high, LANES), 1)
            x = now[:, part]
            xl = jnp.where(
                lane == 0, pltpu.roll(now[:, lo : lo + LANES], 1, 1), pltpu.roll(x, 1, 1)
            )
            xr = jnp.where(
                lane == LANES - 1,
                pltpu.roll(now[:, hi : hi + LANES], LANES - 1, 1),
                pltpu.roll(x, LANES - 1, 1),
            )
            y = s_ref[:, part] + fu[:, part] * pltpu.roll(x, 1, 0)
            y = y + fd[:, part] * pltpu.roll(x, high - 1, 0)
            y = y + (fl[:, part] * xl + fr[:, part] * xr)
            if last:
                out[:, part] = y[0:rows]
            else:
                later[:, part] = y
        now, later = later, now
    while left:
        pass_piece()
    for copy in writes:
        copy.wait()


def on_device(precip, head, trans_coef, land, dest, moisture, ksat):
    tile_rows, tile_cols = precip.shape
    n_col = lax.axis_size("col")
    peers = lax.axis_size("row") * n_col
    me = lax.axis_index("row") * n_col + lax.axis_index("col")
    owned, layers, _ = moisture.shape
    blocks = tile_rows * tile_cols // LANES
    cap = (2 * blocks + peers - 1) // peers
    extra, hop = 2, 4
    depth = (19 * blocks // (16 * peers) + 1 + 7) // 8 * 8
    direct = depth - extra
    lines = 1 << (depth + hop - 1).bit_length()

    target = dest.T.reshape(blocks)
    owner = target // owned
    slot = target - owner * owned
    all_peers = jnp.arange(peers, dtype=jnp.int32)
    one_hot = owner[:, None] == all_peers[None, :]
    order = jnp.arange(blocks, dtype=jnp.int32)
    earlier = (order[None, :] < order[:, None]).astype(jnp.bfloat16)
    counts = jnp.dot(earlier, one_hot.astype(jnp.bfloat16), preferred_element_type=jnp.float32)
    sums = jnp.sum(one_hot.astype(jnp.float32), axis=0)
    over = jnp.maximum(sums - direct, 0.0)
    base = jnp.sum(jnp.where(all_peers[:, None] < all_peers[None, :], over[:, None], 0.0), axis=0)
    rank = jnp.sum(jnp.where(one_hot, counts, 0.0), axis=1).astype(jnp.int32)
    number = jnp.sum(jnp.where(one_hot, counts + base[None, :] - direct, 0.0), axis=1).astype(
        jnp.int32
    )
    spread = rank >= direct
    via = (jnp.maximum(number, 0) + me) % peers
    turn = jnp.clip(number // peers, 0, extra - 1)
    position = jnp.where(
        spread, peers * depth + via * extra + turn, owner * depth + rank
    )
    place = jnp.where(spread, via, owner)
    row_of = jnp.where(spread, direct + turn, rank)

    def table(where, row, width, value):
        hot = (where[:, None] == all_peers[None, :]).astype(jnp.float32)
        at = row[:, None] == jnp.arange(width, dtype=jnp.int32)[None, :]
        return lax.dot_general(
            hot,
            jnp.where(at, value.astype(jnp.float32)[:, None], 0.0),
            (((0,), (0,)), ((), ())),
            precision=lax.Precision.HIGHEST,
            preferred_element_type=jnp.float32,
        )

    source_of = jnp.minimum(table(place, row_of, depth, order).astype(jnp.int32), blocks - 1)
    label = table(owner, rank, LANES, slot - owned) + float(owned)
    sent = jnp.broadcast_to(jnp.pad(sums, (0, LANES - peers))[None, :], (peers, LANES))

    sources, labels, position, owner, rank = lax.optimization_barrier(
        (source_of, jnp.stack([label, sent], axis=1), position, owner, rank)
    )
    flat = moisture.reshape(owned * layers, LANES)
    vm = lambda *shape: pltpu.VMEM(shape, jnp.float32)
    iv = lambda *shape: pltpu.VMEM(shape, jnp.int32)
    sm = lambda *shape: pltpu.SMEM(shape, jnp.int32)
    dma = lambda n: pltpu.SemaphoreType.DMA((n,))
    chunks = 8
    tail = (peers * extra + depth - 1) // depth
    high, wide = tile_rows + 2 * SWEEPS, tile_cols + LANES
    for_source = [
        vm(blocks, LANES),
        vm(2, 8, tile_rows),
        vm(2, 8, tile_cols),
        vm(2, 8, tile_rows),
        vm(4, 8, LANES),
        dma(8),
        dma(8),
    ]
    source, stepped, fits, mid_r, mid_c = pl.pallas_call(
        functools.partial(column_kernel, cap, extra, hop, chunks),
        out_shape=[
            f32(high, wide),
            f32(owned * layers, LANES),
            f32(1, 1),
            f32(3, 2 * SWEEPS, tile_cols),
            f32(3, high, LANES),
        ],
        in_specs=[SM, SM] + [VM] * 5 + [pl.BlockSpec(memory_space=pl.ANY), VM],
        out_specs=[VM, pl.BlockSpec(memory_space=pl.ANY), VM, VM, VM],
        scratch_shapes=[
            vm((peers + tail) * depth, LANES),
            vm(blocks, LANES),
            vm(blocks, LANES),
            vm(peers, 2, depth, LANES),
            vm(peers, 2, lines, LANES),
            vm(peers, 2, LANES),
        ]
        + [vm(owned * layers, LANES)] * 3
        + [vm(owned, LANES)] * 3
        + [
            vm(peers, 2 * hop, LANES),
            vm(peers, 2 * hop, LANES),
            vm(peers, depth, LANES),
            vm(peers, hop, LANES),
            vm(peers, hop, LANES),
            vm(peers, extra, LANES),
            vm(peers, extra, LANES),
            vm(depth, LANES),
            vm(depth, LANES),
            vm(depth, LANES),
            iv(8, LANES),
            iv(extra * peers, LANES),
            iv(peers, LANES),
            iv(8, LANES),
            iv(owned // LANES, LANES),
            vm(2, 24, tile_cols),
            vm(2, 24, tile_rows),
            vm(2, 24, tile_cols),
            vm(2, 24, tile_rows),
            vm(4, 24, LANES),
            sm(peers, LANES),
            sm(8, LANES),
            sm(8, LANES),
            sm(extra * peers, LANES),
            sm(owned // LANES, LANES),
            dma(5),
            dma(chunks),
            dma(chunks),
        ]
        + [dma(peers)] * 12
        + [dma(6), dma(8), dma(8)]
        + for_source,
        compiler_params=pltpu.CompilerParams(
            collective_id=4, has_side_effects=True, vmem_limit_bytes=58 * 2**20
        ),
    )(sources, position, labels, precip, head, trans_coef, land, flat, ksat)


    def relax(source, stepped):
        pieces = 16
        surface, saturation = pl.pallas_call(
            functools.partial(relax_kernel, pieces),
            out_shape=[f32(tile_rows, tile_cols), f32(owned * layers, LANES)],
            in_specs=[VM] * 6 + [pl.BlockSpec(memory_space=pl.ANY)],
            out_specs=[VM, pl.BlockSpec(memory_space=pl.ANY)],
            scratch_shapes=[vm(high, wide)] * 8
            + [vm(owned * layers, LANES), dma(pieces), dma(pieces)],
            compiler_params=pltpu.CompilerParams(vmem_limit_bytes=40 * 2**20),
        )(source, head, trans_coef, land, mid_r, mid_c, stepped)
        return saturation.reshape(owned, layers, LANES), surface

    def hopped():
        return relax(source, stepped)

    def whole():
        step = 128
        layered = pl.BlockSpec((layers, step, LANES), lambda i: (0, i, 0))
        single = pl.BlockSpec((step, LANES), lambda i: (i, 0))
        natural = pl.BlockSpec((step * layers, LANES), lambda i: (i, 0))
        s0, sx, sy, rec0, rec_x, rec_y = pl.pallas_call(
            functools.partial(factor_kernel, layers, 32),
            grid=(owned // step,),
            out_shape=[f32(layers, owned, LANES)] * 3 + [f32(owned, LANES)] * 3,
            in_specs=[natural, single],
            out_specs=[layered] * 3 + [single] * 3,
        )(flat, ksat)
        slots_of = table(owner, rank, cap, order).astype(jnp.int32).reshape(peers * cap)
        outgoing = pl.pallas_call(
            functools.partial(pack_kernel, peers, cap),
            out_shape=f32(peers, 2 * cap + 8, LANES),
            in_specs=[SM, VM, VM, VM, VM],
            out_specs=VM,
            scratch_shapes=[pltpu.VMEM((blocks, LANES), jnp.float32)] * 2,
        )(slots_of, labels[:, 0], precip, head, land)
        arrived = lax.all_to_all(outgoing, ("row", "col"), split_axis=0, concat_axis=0, tiled=True)
        places = arrived[:, 2 * cap, :cap].astype(jnp.int32).reshape(peers * cap)
        answer, infil, sig = pl.pallas_call(
            functools.partial(owner_kernel, peers, cap),
            out_shape=[f32(peers, cap, LANES), f32(owned, LANES), f32(owned, LANES)],
            in_specs=[SM, VM, VM, VM, VM],
            out_specs=[VM] * 3,
            scratch_shapes=[pltpu.VMEM((owned + 8, LANES), jnp.float32)] * 3,
        )(places, arrived, rec0, rec_x, rec_y)
        back = lax.all_to_all(answer, ("row", "col"), split_axis=0, concat_axis=0, tiled=True)
        saturation = pl.pallas_call(
            functools.partial(saturation_kernel, layers),
            grid=(owned // step,),
            out_shape=f32(owned * layers, LANES),
            in_specs=[layered] * 3 + [single] * 2,
            out_specs=natural,
        )(s0, sx, sy, infil, sig)
        source = pl.pallas_call(
            source_kernel,
            out_shape=f32(high, wide),
            in_specs=[SM] + [VM] * 3,
            out_specs=VM,
            scratch_shapes=for_source,
            compiler_params=pltpu.CompilerParams(collective_id=2, has_side_effects=True),
        )(owner * cap + rank, back.reshape(-1, LANES), head, land)
        return relax(source, saturation)

    return lax.cond(fits.reshape(()) > 0.5, hopped, whole)


def solution(mesh):
    tile = P("row", "col")
    placed = (
        tile,
        tile,
        tile,
        tile,
        tile,
        P(("row", "col"), None, None),
        P(("row", "col"), None),
    )
    return jax.shard_map(
        on_device,
        mesh=mesh,
        in_specs=placed,
        out_specs=(P(("row", "col"), None, None), P("row", "col")),
        check_vma=False,
    )
```

```python
import functools
import math

import jax
import jax.numpy as jnp
from jax import lax
from jax.experimental import pallas as pl
from jax.experimental.pallas import tpu as pltpu
from jax.sharding import PartitionSpec as P

SWEEPS = 4
LANES = 128

layer_depth = 0.1
step_ratio = 0.1
residual_water = 0.05
pore_range = 0.4
diff_length = 0.5
couple_rate = 0.05
recharge_gain = 20.0
store_rate = 0.2

VM = pl.BlockSpec(memory_space=pltpu.VMEM)
SM = pl.BlockSpec(memory_space=pltpu.SMEM)


def f32(*shape):
    return jax.ShapeDtypeStruct(shape, jnp.float32)


def factor_rows(layers, moist, ksat, base_row, group):
    rows = pl.ds(pl.multiple_of(base_row, group), group)
    ks = ksat[rows, :]
    ratios, reds, xs = [], [], []
    before = None
    for k in range(layers):
        m = moist[pl.ds(base_row * layers + k, group, stride=layers), :]
        w = (m - residual_water) * (1.0 / pore_range)
        s = ks * math.exp(-(k + 0.5) * layer_depth)
        sw2 = s * (w * w)
        hs = sw2 * (1.5 / pore_range)
        d = s * (0.2 * diff_length / (2.0 * layer_depth)) + sw2 * (
            diff_length / (2.0 * layer_depth)
        )
        hc = 0.5 * (sw2 * w)
        cur = (m, hs, d, hc)
        if before is None:
            before = cur
            g_up = q_up = nsub = None
            continue
        m0, hs0, d0, hc0 = before
        g = d0 + d
        q = (hc0 + hc) - g * (m - m0)
        if g_up is None:
            pivot = step_ratio + g + hs0
            inv = 1.0 / pivot
            reds.append(-q * inv)
            xs.append(inv)
        else:
            pivot = step_ratio + g_up + g - nsub * ratios[-1]
            inv = 1.0 / pivot
            reds.append(((q_up - q) + nsub * reds[-1]) * inv)
            xs.append(nsub * inv * xs[-1])
        ratios.append((g - hs) * inv)
        nsub = hs0 + g
        g_up, q_up = g, q
        before = cur
    m, hs, d, hc = before
    bottom = 2.0 * hc + couple_rate * (m - residual_water)
    pivot = step_ratio + g_up + hs + couple_rate - nsub * ratios[-1]
    inv = 1.0 / pivot
    change = ((q_up - bottom) + nsub * reds[-1]) * inv
    cx = nsub * inv * xs[-1]
    cy = (couple_rate * pore_range) * inv
    gain = 2.0 * hs + couple_rate
    recharge = (
        bottom + gain * change,
        gain * cx,
        gain * cy - couple_rate * pore_range,
    )
    unit = 1.0 / pore_range
    terms = [None] * layers
    for k in range(layers - 1, -1, -1):
        if k < layers - 1:
            change = reds[k] + ratios[k] * change
            cx = xs[k] + ratios[k] * cx
            cy = ratios[k] * cy
        m = moist[pl.ds(base_row * layers + k, group, stride=layers), :]
        terms[k] = ((m + change - residual_water) * unit, cx * unit, cy * unit)
    return recharge, terms


def within(index, size):
    if size & (size - 1) == 0:
        return jnp.bitwise_and(index, size - 1)
    return jnp.clip(index, 0, size - 1)


def fixed_fields(head, trans_coef, land):
    share = land.astype(jnp.float32)
    return trans_coef * (1.0 + 0.5 * jnp.tanh(head)), head * share, share


def neighbours(row, col):
    n_row, n_col = lax.axis_size("row"), lax.axis_size("col")
    up, down = row > 0, row < n_row - 1
    left, right = col > 0, col < n_col - 1
    steps = [(-1, 0), (1, 0), (0, -1), (0, 1), (-1, -1), (-1, 1), (1, -1), (1, 1)]
    go = [up, down, left, right, up & left, up & right, down & left, down & right]
    come = [down, up, right, left, down & right, down & left, up & right, up & left]
    return steps, go, come


def each(flags, act):
    for k, flag in enumerate(flags):
        pl.when(flag)(functools.partial(act, k))


def halo_copy(k, steps, row, col, src, dst, send_sem, recv_sem):
    return pltpu.make_async_remote_copy(
        src_ref=src[k],
        dst_ref=dst[k],
        send_sem=send_sem.at[k],
        recv_sem=recv_sem.at[k],
        device_id=(row + steps[k][0], col + steps[k][1]),
        device_id_type=pl.DeviceIdType.MESH,
    )


def column_kernel(
    cap, extra, hop, chunks, src, position, labels, precip, head, trans_coef, land, moisture, ksat,
    s_ref, saturation, fits, mid_r, mid_c, returned,
    infil, sigs, out, out0, allbuf, labs, moist, sx, sy, rec0, rec_x, rec_y,
    mid_out, arr2, ans, ans2, arr4, out5, arr5, g0, gx, gy, src_v, ret_v, slots_v, slot2_v, inv_v,
    row_out, strip_out, from_row, strip_in, corner,
    slots_s, slot2_s, src_s, ret_s, inv_s,
    move, read, write, send0, recv0, send1, recv1, send2, recv2, send3, recv3, send4, recv4, send5, recv5, own,
    send_h, recv_h, *for_source,
):
    rows, cols = precip.shape
    peers, _, lines, _ = allbuf.shape
    depth = out.shape[2]
    direct = depth
    owned = rec0.shape[0]
    layers = moist.shape[0] // owned
    n_col = lax.axis_size("col")
    row, col = lax.axis_index("row"), lax.axis_index("col")
    me = row * n_col + col
    barrier = pltpu.get_barrier_semaphore()
    part_rows = owned // chunks

    def fetch(c):
        part = pl.ds(c * part_rows * layers, part_rows * layers)
        return pltpu.make_async_copy(moisture.at[part], moist.at[part], read.at[c])

    def flush(c):
        part = pl.ds(c * part_rows * layers, part_rows * layers)
        return pltpu.make_async_copy(moist.at[part], saturation.at[part], write.at[c])

    def where_is(k):
        p = lax.rem(me + k, peers)
        return p, (p // n_col, lax.rem(p, n_col))

    def greet(k, _):
        pl.semaphore_signal(
            barrier, inc=1, device_id=where_is(k)[1], device_id_type=pl.DeviceIdType.MESH
        )
        return 0

    lax.fori_loop(1, peers, greet, 0)
    for c in range(chunks):
        fetch(c).start()

    def exchange(src, dst, send, recv, self_sem):
        def copy(k):
            p, place = where_is(k)
            return pltpu.make_async_remote_copy(
                src_ref=src(p),
                dst_ref=dst(me),
                send_sem=send.at[k],
                recv_sem=recv.at[k],
                device_id=place,
                device_id_type=pl.DeviceIdType.MESH,
            )

        here = pltpu.make_async_copy(src(me), dst(me), self_sem)

        def start(low, high):
            def body(k, _):
                copy(k).start()
                return 0

            lax.fori_loop(low, high, body, 0)

        def wait():
            def body(k, _):
                copy(k).wait()
                return 0

            lax.fori_loop(1, peers, body, 0)
            here.wait()

        return copy, here, start, wait

    for j in range(cols // LANES):
        part = pl.ds(j * LANES, LANES)
        infil[pl.ds(j * rows, rows), :] = precip[:, part] * land[:, part].astype(jnp.float32)
        sigs[pl.ds(j * rows, rows), :] = jax.nn.sigmoid(head[:, part])

    def pack(p):
        for r in range(depth):
            block = within(src[p, r], infil.shape[0])
            out[p, 0, pl.ds(r, 1), :] = infil[pl.ds(block, 1), :]
            out[p, 1, pl.ds(r, 1), :] = sigs[pl.ds(block, 1), :]

    _, here0, start0, wait0 = exchange(
        lambda p: out0.at[p], lambda p: labs.at[p], send0, recv0, own.at[5]
    )
    def pack_first(p, _):
        for t in range(2):
            out0[p, pl.ds(t, 1), :] = labels[p, pl.ds(t, 1), :]
        for t in range(extra):
            block = within(src[p, depth + t], infil.shape[0])
            out0[p, pl.ds(2 + t, 1), :] = infil[pl.ds(block, 1), :]
            out0[p, pl.ds(2 + extra + t, 1), :] = sigs[pl.ds(block, 1), :]
        return 0

    copy1, here1, _, _ = exchange(
        lambda p: out.at[p], lambda p: allbuf.at[p, :, pl.ds(0, depth)], send1, recv1, own.at[0]
    )
    pl.semaphore_wait(barrier, peers - 1)
    def ship(k, _):
        k = peers - k
        pack(where_is(k)[0])
        copy1(k).start()
        return 0

    ahead = min(5, peers)
    lax.fori_loop(1, ahead, ship, 0)
    lax.fori_loop(0, peers, pack_first, 0)
    here0.start()
    start0(1, peers)
    lax.fori_loop(ahead, peers, ship, 0)
    pack(me)
    here1.start()

    steps, go, come = neighbours(row, col)
    east, south = cols - LANES, rows - 8
    for side, at in enumerate((0, south)):
        edge = pl.ds(at, 8)
        for f, field in enumerate(fixed_fields(head[edge, :], trans_coef[edge, :], land[edge, :])):
            row_out[side, pl.ds(8 * f, 8), :] = field
    for side, at in enumerate((0, east)):
        edge = pl.ds(at, LANES)
        keep = slice(0, 8) if side == 0 else slice(LANES - 8, LANES)
        for f, field in enumerate(fixed_fields(head[:, edge], trans_coef[:, edge], land[:, edge])):
            strip_out[side, pl.ds(8 * f, 8), :] = jnp.transpose(field)[keep]
    halo_dst = [from_row.at[0], from_row.at[1], strip_in.at[0], strip_in.at[1]] + [
        corner.at[c] for c in range(4)
    ]
    halo_src = [row_out.at[0], row_out.at[1], strip_out.at[0], strip_out.at[1]] + [
        row_out.at[c // 2, :, pl.ds((c % 2) * east, LANES)] for c in range(4)
    ]
    for k in range(8):

        @pl.when(jnp.logical_not(come[k]))
        def _(ref=halo_dst[k]):
            ref[...] = jnp.zeros(ref.shape, jnp.float32)

    def halo(k):
        return halo_copy(k, steps, row, col, halo_src, halo_dst, send_h, recv_h)

    each(go, lambda k: halo(k).start())

    group = 32

    def factor(c, _):
        fetch(c).wait()

        def body(i, _):
            base_row = pl.multiple_of(c * part_rows + i * group, group)
            at = pl.ds(base_row, group)
            recharge, terms = factor_rows(layers, moist, ksat, base_row, group)
            for ref, value in zip((rec0, rec_x, rec_y), recharge):
                ref[at, :] = value
            for k in range(layers):
                for ref, value in zip((moist, sx, sy), terms[k]):
                    ref[pl.ds(base_row * layers + k, group, stride=layers), :] = value
            return 0

        lax.fori_loop(0, part_rows // group, body, 0)
        return 0

    lax.fori_loop(0, chunks, factor, 0)
    wait0()

    shape = (peers, LANES)
    lane = lax.broadcasted_iota(jnp.int32, shape, 1)
    sub = lax.broadcasted_iota(jnp.int32, shape, 0)
    lab = labs[:, 0, :]
    count = labs[:, 1, :]
    over = jnp.maximum(count - direct, 0.0)
    tri = lax.broadcasted_iota(jnp.int32, (LANES, LANES), 0) < lax.broadcasted_iota(
        jnp.int32, (LANES, LANES), 1
    )
    base = jnp.dot(
        over, tri.astype(jnp.float32), precision=lax.Precision.HIGHEST,
        preferred_element_type=jnp.float32,
    )
    total = extra * peers
    before = (
        lax.broadcasted_iota(jnp.int32, (total, total), 1)
        < lax.broadcasted_iota(jnp.int32, (total, total), 0)
    ).astype(jnp.float32)

    def number(m):
        gap = m - sub
        return jnp.where(gap < 0, gap + peers, gap).astype(jnp.float32)

    def holds(j, first, many, t):
        j = j + float(t * peers)
        return jnp.where((first <= j) & (j < first + many), 1.0, 0.0)

    def prefix(v):
        return jnp.dot(before, v, preferred_element_type=jnp.float32)

    flane = lane.astype(jnp.float32)
    code = sub.astype(jnp.float32) * 8.0
    via = jnp.concatenate([holds(number(me), base, over, t) for t in range(extra)], axis=0)
    rank = prefix(via)
    codes = jnp.concatenate([code + float(t) for t in range(extra)], axis=0)
    lanes = jnp.concatenate([flane] * extra, axis=0)
    back = jnp.sum(via * (lanes * hop + rank), axis=1, keepdims=True)
    ret_v[...] = jnp.broadcast_to(back, (total, LANES)).astype(jnp.int32)
    pad = jnp.zeros((8 - hop, LANES), jnp.float32)
    picks = [
        jnp.sum(jnp.where(rank == float(e), via * codes, 0.0), axis=0, keepdims=True)
        for e in range(hop)
    ]
    src_v[...] = jnp.concatenate(picks + [pad], axis=0).astype(jnp.int32)
    mine = jnp.where(lane == me, 1.0, 0.0)
    first = jnp.sum(base * mine, axis=1, keepdims=True)
    many = jnp.sum(over * mine, axis=1, keepdims=True)
    inside = jnp.where(lane < peers, 1.0, 0.0)
    step = number(lane)
    took = [holds(step, first, many, t) * inside for t in range(extra)]
    value = []
    for t in range(extra):
        at = step + float(t * peers) - first
        v = jnp.zeros(shape, jnp.float32)
        for r in range(cap - direct):
            v = jnp.where(at == float(r), lab[:, direct + r : direct + r + 1] - float(owned), v)
        value.append(v)
    took = jnp.concatenate(took, axis=0)
    rank = prefix(took)
    value = jnp.concatenate(value, axis=0)
    picks = [
        jnp.sum(jnp.where(rank == float(e), took * value, 0.0), axis=0, keepdims=True)
        for e in range(hop)
    ]
    hopped = jnp.concatenate(picks + [pad], axis=0) + float(owned)
    slot2_v[...] = hopped.astype(jnp.int32)
    slots_v[...] = lab.astype(jnp.int32)
    moves = [
        pltpu.make_async_copy(src_v, src_s, move.at[0]),
        pltpu.make_async_copy(slots_v, slots_s, move.at[1]),
        pltpu.make_async_copy(slot2_v, slot2_s, move.at[2]),
        pltpu.make_async_copy(ret_v, ret_s, move.at[3]),
    ]
    for m in moves:
        m.start()
    g0[...] = jnp.zeros(g0.shape, jnp.float32)
    gx[...] = jnp.zeros(gx.shape, jnp.float32)
    gy[...] = jnp.zeros(gy.shape, jnp.float32)
    for m in moves:
        m.wait()

    def answer(q):
        for r in range(direct):
            slot = within(slots_s[q, r], owned)
            g0[pl.ds(r, 1), :] = rec0[pl.ds(slot, 1), :]
            gx[pl.ds(r, 1), :] = rec_x[pl.ds(slot, 1), :]
            gy[pl.ds(r, 1), :] = rec_y[pl.ds(slot, 1), :]
        ans[q] = (
            g0[...]
            + allbuf[q, 0, pl.ds(0, depth), :] * gx[...]
            + allbuf[q, 1, pl.ds(0, depth), :] * gy[...]
        )

    def pass_on(d, _):
        for e in range(hop):
            q = src_s[e, d]
            s = jnp.clip(q // 8, 0, peers - 1)
            t = jnp.clip(q - s * 8, 0, extra - 1)
            mid_out[d, pl.ds(e, 1), :] = labs[s, pl.ds(2 + t, 1), :]
            mid_out[d, pl.ds(hop + e, 1), :] = labs[s, pl.ds(2 + extra + t, 1), :]
        return 0

    lax.fori_loop(0, peers, pass_on, 0)
    _, here2, start2, wait2 = exchange(
        lambda p: mid_out.at[p], lambda p: arr2.at[p], send2, recv2, own.at[1]
    )
    here2.start()
    start2(1, peers)
    here1.wait()
    answer(me)

    def receive(k, _):
        k = peers - k
        copy1(k).wait_recv()
        answer(lax.rem(me + peers - k, peers))
        return 0

    lax.fori_loop(1, peers, receive, 0)

    _, here3, start3, wait3 = exchange(
        lambda p: ans.at[p],
        lambda p: returned.at[pl.ds(pl.multiple_of(p * depth, 8), depth)],
        send3, recv3, own.at[2]
    )
    _, here4, start4, wait4 = exchange(
        lambda p: ans2.at[p], lambda p: arr4.at[p], send4, recv4, own.at[3]
    )
    _, here5, start5, wait5 = exchange(
        lambda p: out5.at[p], lambda p: arr5.at[p], send5, recv5, own.at[4]
    )

    wait2()

    def answer2(m, _):
        for e in range(hop):
            slot = within(slot2_s[e, m], owned)
            inf, sg = arr2[m, pl.ds(e, 1), :], arr2[m, pl.ds(hop + e, 1), :]
            ans2[m, pl.ds(e, 1), :] = (
                rec0[pl.ds(slot, 1), :]
                + inf * rec_x[pl.ds(slot, 1), :]
                + sg * rec_y[pl.ds(slot, 1), :]
            )
            allbuf[m, 0, pl.ds(depth + e, 1), :] = inf
            allbuf[m, 1, pl.ds(depth + e, 1), :] = sg
        return 0

    lax.fori_loop(0, peers, answer2, 0)
    here4.start()
    start4(1, peers)
    here3.start()
    start3(1, 3 * peers // 4)

    columns = jnp.transpose(
        jnp.concatenate([hopped, jnp.zeros((LANES - 8, LANES), jnp.float32)], axis=0)
    )
    place = sub.astype(jnp.float32) * float(lines)
    for g in range(owned // LANES):
        want = flane + float(g * LANES)
        found = jnp.zeros(shape, jnp.float32)
        for r in range(direct):
            found = jnp.where(lab[:, r : r + 1] == want, place + float(r), found)
        for e in range(hop):
            found = jnp.where(
                columns[0:peers, e : e + 1] == want, place + float(depth + e), found
            )
        inv_v[pl.ds(g, 1), :] = jnp.sum(found, axis=0, keepdims=True).astype(jnp.int32)
    turn = pltpu.make_async_copy(inv_v, inv_s, move.at[4])
    turn.start()

    def widest(m, most):
        n = number(m)
        seen = functools.reduce(lambda x, y: x + y, [holds(n, base, over, t) for t in range(extra)])
        return jnp.maximum(most, jnp.sum(seen, axis=0, keepdims=True))

    most = lax.fori_loop(0, peers, widest, jnp.zeros((1, LANES), jnp.float32))
    spread = jnp.max(jnp.sum(over, axis=1, keepdims=True), axis=0, keepdims=True)
    bad = jnp.maximum(
        jnp.where(jnp.max(most, axis=1, keepdims=True) > float(hop), 1.0, 0.0),
        jnp.where(spread > float(total), 1.0, 0.0),
    )
    fits[...] = jnp.broadcast_to(1.0 - bad, fits.shape)

    def landed(k):
        return pltpu.make_async_remote_copy(
            src_ref=halo_src[k],
            dst_ref=halo_dst[k],
            send_sem=send_h.at[k],
            recv_sem=recv_h.at[k],
            device_id=(row, col),
            device_id_type=pl.DeviceIdType.MESH,
        )

    each(go, lambda k: halo(k).wait_send())
    each(come, lambda k: landed(k).wait_recv())
    upper = lax.broadcasted_iota(jnp.int32, (8, LANES), 0) < 4
    near = lax.broadcasted_iota(jnp.int32, (8, LANES), 1) < LANES // 2
    for f in range(3):
        eight = pl.ds(8 * f, 8)
        for j in range(cols // LANES):
            part = pl.ds(j * LANES, LANES)
            mid_r[f, :, part] = jnp.where(upper, from_row[0, eight, part], from_row[1, eight, part])
        mid_c[f, pl.ds(rows, 8), :] = jnp.where(
            upper,
            jnp.where(near, corner[0, eight, :], corner[1, eight, :]),
            jnp.where(near, corner[2, eight, :], corner[3, eight, :]),
        )
        mid_c[f, pl.ds(0, rows), :] = jnp.transpose(
            jnp.concatenate(
                [
                    strip_in[0, eight, :],
                    jnp.zeros((LANES - 16, rows), jnp.float32),
                    strip_in[1, eight, :],
                ],
                axis=0,
            )
        )
    turn.wait()

    def finish(c, _):
        def body(i, _):
            for u in range(8):
                n = c * part_rows + i * 8 + u
                v = inv_s[n // LANES, lax.rem(n, LANES)]
                p = jnp.minimum(lax.shift_right_logical(v, bits), peers - 1)
                r = jnp.bitwise_and(v, lines - 1)
                inf = allbuf[p, 0, pl.ds(r, 1), :]
                sg = allbuf[p, 1, pl.ds(r, 1), :]
                at = pl.ds(pl.multiple_of(n * layers, layers), layers)
                moist[at, :] = moist[at, :] + inf * sx[at, :] + sg * sy[at, :]
            return 0

        lax.fori_loop(0, part_rows // 8, body, 0)
        flush(c).start()
        return 0

    bits = lines.bit_length() - 1
    lax.fori_loop(0, chunks // 2, finish, 0)
    wait4()

    def hand_back(s, _):
        for t in range(extra):
            at = jnp.clip(ret_s[t * peers + s, 0], 0, peers * hop - 1)
            d = at // hop
            out5[s, pl.ds(t, 1), :] = arr4[d, pl.ds(at - d * hop, 1), :]
        return 0

    lax.fori_loop(0, peers, hand_back, 0)
    here5.start()
    start5(1, peers)
    start3(3 * peers // 4, peers)
    lax.fori_loop(chunks // 2, chunks, finish, 0)

    wait5()
    for i in range(total):
        returned[pl.ds(peers * depth + i, 1), :] = arr5[i // extra, pl.ds(i % extra, 1), :]
    wait3()
    spread_source(
        position, returned, head, land, s_ref, *for_source, ready=lambda: None
    )

    def sent(k, _):
        copy1(k).wait_send()
        return 0

    lax.fori_loop(1, peers, sent, 0)
    for c in range(chunks):
        flush(c).wait()


def pack_kernel(peers, per_peer, src, labels, precip, head, land, out, infil, heads):
    rows, cols = precip.shape
    for j in range(cols // LANES):
        part = pl.ds(j * LANES, LANES)
        infil[pl.ds(j * rows, rows), :] = precip[:, part] * land[:, part].astype(jnp.float32)
        heads[pl.ds(j * rows, rows), :] = head[:, part]

    def body(p, _):
        for r in range(per_peer):
            block = src[p * per_peer + r]
            out[p, pl.ds(r, 1), :] = infil[pl.ds(block, 1), :]
            out[p, pl.ds(per_peer + r, 1), :] = heads[pl.ds(block, 1), :]
        out[p, pl.ds(2 * per_peer, 8), :] = jnp.broadcast_to(labels[pl.ds(p, 1), :], (8, LANES))
        return 0

    lax.fori_loop(0, peers, body, 0)


def owner_kernel(
    peers, per_peer, slots, arrived, rec0, rec_x, rec_y, answer, infil, sig, own_i, own_h, rec
):
    owned = rec0.shape[0]

    def scatter(p, _):
        for r in range(per_peer):
            slot = slots[p * per_peer + r]
            own_i[pl.ds(slot, 1), :] = arrived[p, pl.ds(r, 1), :]
            own_h[pl.ds(slot, 1), :] = arrived[p, pl.ds(per_peer + r, 1), :]
        return 0

    lax.fori_loop(0, peers, scatter, 0)
    rec[pl.ds(owned, 8), :] = jnp.zeros((8, LANES), jnp.float32)

    def combine(g, _):
        part = pl.ds(g * 64, 64)
        inf = own_i[part, :]
        sg = jax.nn.sigmoid(own_h[part, :])
        infil[part, :] = inf
        sig[part, :] = sg
        rec[part, :] = rec0[part, :] + inf * rec_x[part, :] + sg * rec_y[part, :]
        return 0

    lax.fori_loop(0, owned // 64, combine, 0)

    def gather(p, _):
        for r in range(per_peer):
            slot = slots[p * per_peer + r]
            answer[p, pl.ds(r, 1), :] = rec[pl.ds(slot, 1), :]
        return 0

    lax.fori_loop(0, peers, gather, 0)


def factor_kernel(layers, group, moist, ksat, s0, sx, sy, rec0, rec_x, rec_y):
    def body(step, _):
        base_row = step * group
        rows = pl.ds(pl.multiple_of(base_row, group), group)
        recharge, terms = factor_rows(layers, moist, ksat, base_row, group)
        for ref, value in zip((rec0, rec_x, rec_y), recharge):
            ref[rows, :] = value
        for k in range(layers):
            for ref, value in zip((s0, sx, sy), terms[k]):
                ref[k, rows, :] = value
        return 0

    lax.fori_loop(0, ksat.shape[0] // group, body, 0)


def saturation_kernel(layers, s0, sx, sy, infil, sig, out):
    count = infil.shape[0]
    group = 32

    def body(step, _):
        rows = pl.ds(pl.multiple_of(step * group, group), group)
        inf = infil[rows, :]
        sg = sig[rows, :]
        for k in range(layers):
            out[pl.ds(step * group * layers + k, group, stride=layers), :] = (
                s0[k, rows, :] + inf * sx[k, rows, :] + sg * sy[k, rows, :]
            )
        return 0

    lax.fori_loop(0, count // group, body, 0)


def spread_source(
    position, returned, head, land, s_ref,
    sorted_rows, strip_out, from_row, strip_in, corner, send_sem, recv_sem, ready,
):
    rows, cols = head.shape
    high, wide = s_ref.shape
    row, col = lax.axis_index("row"), lax.axis_index("col")
    steps, go, come = neighbours(row, col)
    east, south = cols - LANES, rows - 8
    src = [
        s_ref.at[pl.ds(0, 8), pl.ds(0, cols)],
        s_ref.at[pl.ds(south, 8), pl.ds(0, cols)],
        strip_out.at[0],
        strip_out.at[1],
    ] + [s_ref.at[pl.ds(y, 8), pl.ds(x, LANES)] for y in (0, south) for x in (0, east)]
    dst = [from_row.at[0], from_row.at[1], strip_in.at[0], strip_in.at[1]] + [
        corner.at[c] for c in range(4)
    ]
    for k in range(8):

        @pl.when(jnp.logical_not(come[k]))
        def _(ref=dst[k]):
            ref[...] = jnp.zeros(ref.shape, jnp.float32)

    def fill(j, g):
        base = pl.multiple_of(g * 32, 32)
        for u in range(32):
            at = j * rows + base + u
            place = jnp.clip(position[at], 0, returned.shape[0] - 1)
            sorted_rows[pl.ds(at, 1), :] = returned[pl.ds(place, 1), :]
        at, part = pl.ds(base, 32), pl.ds(j * LANES, LANES)
        s_ref[at, part] = (
            store_rate * (head[at, part] * land[at, part].astype(jnp.float32))
            + recharge_gain * sorted_rows[pl.ds(j * rows + base, 32), :]
        )

    def fill_range(j, low, high):
        def body(g, _):
            fill(j, g)
            return 0

        lax.fori_loop(low, high, body, 0)

    groups, strips = rows // 32, cols // LANES
    fill_range(0, 0, groups)
    fill_range(strips - 1, 0, groups)
    strip_out[0] = jnp.transpose(s_ref[0:rows, 0:LANES])[0:8]
    strip_out[1] = jnp.transpose(s_ref[0:rows, east:cols])[LANES - 8 : LANES]
    for j in range(1, strips - 1):
        fill(j, 0)
        fill(j, groups - 1)
    ready()

    def copy(k):
        return halo_copy(k, steps, row, col, src, dst, send_sem, recv_sem)

    def landed(k):
        return halo_copy(k, [(0, 0)] * 8, row, col, src, dst, send_sem, recv_sem)

    each(go, lambda k: copy(k).start())
    for j in range(1, strips - 1):
        fill_range(j, 1, groups - 1)
    each(go, lambda k: copy(k).wait_send())
    each(come, lambda k: landed(k).wait_recv())
    first = lax.broadcasted_iota(jnp.int32, (8, LANES), 0) < 4
    near = lax.broadcasted_iota(jnp.int32, (8, LANES), 1) < LANES // 2
    for j in range(strips):
        part = slice(j * LANES, (j + 1) * LANES)
        s_ref[rows:high, part] = jnp.where(first, from_row[0, :, part], from_row[1, :, part])
    s_ref[rows:high, cols:wide] = jnp.where(
        first,
        jnp.where(near, corner[0], corner[1]),
        jnp.where(near, corner[2], corner[3]),
    )
    s_ref[0:rows, cols:wide] = jnp.transpose(
        jnp.concatenate(
            [strip_in[0], jnp.zeros((LANES - 16, rows), jnp.float32), strip_in[1]], axis=0
        )
    )


def source_kernel(position, returned, head, land, s_ref, *scratch):
    row, col = lax.axis_index("row"), lax.axis_index("col")
    steps, go, _ = neighbours(row, col)
    barrier = pltpu.get_barrier_semaphore()

    def greet(k):
        pl.semaphore_signal(
            barrier,
            inc=1,
            device_id=(row + steps[k][0], col + steps[k][1]),
            device_id_type=pl.DeviceIdType.MESH,
        )

    each(go, greet)

    def ready():
        pl.semaphore_wait(
            barrier, functools.reduce(lambda x, y: x + y, [f.astype(jnp.int32) for f in go])
        )

    spread_source(position, returned, head, land, s_ref, *scratch, ready)


def relax_kernel(
    pieces, source, head, trans_coef, land, mid_r, mid_c, stepped, out, saturation,
    t_ref, s_ref, fu, fd, fl, fr, a, b, held, read, write,
):
    rows, cols = head.shape
    high, wide = t_ref.shape
    each_rows = stepped.shape[0] // pieces
    parts = [pl.ds(c * each_rows, each_rows) for c in range(pieces)]
    reads = [
        pltpu.make_async_copy(stepped.at[p], held.at[p], read.at[c]) for c, p in enumerate(parts)
    ]
    writes = [
        pltpu.make_async_copy(held.at[p], saturation.at[p], write.at[c])
        for c, p in enumerate(parts)
    ]
    for copy in reads:
        copy.start()
    left = list(range(pieces))

    def pass_piece():
        if left:
            c = left.pop(0)
            reads[c].wait()
            writes[c].start()

    for f, (ref, centre) in enumerate(
        zip((t_ref, a, b), fixed_fields(head[...], trans_coef[...], land[...]))
    ):
        ref[0:rows, 0:cols] = centre
        ref[rows:high, 0:cols] = mid_r[f]
        ref[:, cols:wide] = mid_c[f]
    for g in range(wide // LANES):
        part = slice(g * LANES, (g + 1) * LANES)
        lo = slice((g - 1) % (wide // LANES) * LANES, (g - 1) % (wide // LANES) * LANES + LANES)
        hi = slice((g + 1) % (wide // LANES) * LANES, (g + 1) % (wide // LANES) * LANES + LANES)
        lane = lax.broadcasted_iota(jnp.int32, (high, LANES), 1)
        t = t_ref[:, part]
        tu = 0.5 * (t + pltpu.roll(t, 1, 0))
        td = 0.5 * (t + pltpu.roll(t, high - 1, 0))
        tl = jnp.where(lane == 0, pltpu.roll(t_ref[:, lo], 1, 1), pltpu.roll(t, 1, 1))
        tr = jnp.where(
            lane == LANES - 1,
            pltpu.roll(t_ref[:, hi], LANES - 1, 1),
            pltpu.roll(t, LANES - 1, 1),
        )
        lf = 0.5 * (t + tl)
        rt = 0.5 * (t + tr)
        inv = b[:, part] / (store_rate + (tu + td + lf + rt))
        fu[:, part] = tu * inv
        fd[:, part] = td * inv
        fl[:, part] = lf * inv
        fr[:, part] = rt * inv
        s_ref[:, part] = source[:, part] * inv
        if g > 1:
            pass_piece()
    now, later = a, b
    for sweep in range(SWEEPS):
        last = sweep == SWEEPS - 1
        for g in range(wide // LANES):
            if last and g * LANES >= cols:
                continue
            pass_piece()
            part = slice(g * LANES, (g + 1) * LANES)
            lo = (g - 1) % (wide // LANES) * LANES
            hi = (g + 1) % (wide // LANES) * LANES
            lane = lax.broadcasted_iota(jnp.int32, (high, LANES), 1)
            x = now[:, part]
            xl = jnp.where(
                lane == 0, pltpu.roll(now[:, lo : lo + LANES], 1, 1), pltpu.roll(x, 1, 1)
            )
            xr = jnp.where(
                lane == LANES - 1,
                pltpu.roll(now[:, hi : hi + LANES], LANES - 1, 1),
                pltpu.roll(x, LANES - 1, 1),
            )
            y = s_ref[:, part] + fu[:, part] * pltpu.roll(x, 1, 0)
            y = y + fd[:, part] * pltpu.roll(x, high - 1, 0)
            y = y + (fl[:, part] * xl + fr[:, part] * xr)
            if last:
                out[:, part] = y[0:rows]
            else:
                later[:, part] = y
        now, later = later, now
    while left:
        pass_piece()
    for copy in writes:
        copy.wait()


def on_device(precip, head, trans_coef, land, dest, moisture, ksat):
    tile_rows, tile_cols = precip.shape
    n_col = lax.axis_size("col")
    peers = lax.axis_size("row") * n_col
    me = lax.axis_index("row") * n_col + lax.axis_index("col")
    owned, layers, _ = moisture.shape
    blocks = tile_rows * tile_cols // LANES
    cap = (2 * blocks + peers - 1) // peers
    extra, hop = 1, 4
    depth = (19 * blocks // (16 * peers) + 1 + 7) // 8 * 8
    direct = depth
    lines = 1 << (depth + hop - 1).bit_length()

    target = dest.T.reshape(blocks)
    owner = target // owned
    slot = target - owner * owned
    all_peers = jnp.arange(peers, dtype=jnp.int32)
    one_hot = owner[:, None] == all_peers[None, :]
    order = jnp.arange(blocks, dtype=jnp.int32)
    earlier = (order[None, :] < order[:, None]).astype(jnp.bfloat16)
    counts = jnp.dot(earlier, one_hot.astype(jnp.bfloat16), preferred_element_type=jnp.float32)
    sums = jnp.sum(one_hot.astype(jnp.float32), axis=0)
    over = jnp.maximum(sums - direct, 0.0)
    base = jnp.sum(jnp.where(all_peers[:, None] < all_peers[None, :], over[:, None], 0.0), axis=0)
    rank = jnp.sum(jnp.where(one_hot, counts, 0.0), axis=1).astype(jnp.int32)
    number = jnp.sum(jnp.where(one_hot, counts + base[None, :] - direct, 0.0), axis=1).astype(
        jnp.int32
    )
    spread = rank >= direct
    via = (jnp.maximum(number, 0) + me) % peers
    turn = jnp.clip(number // peers, 0, extra - 1)
    position = jnp.where(
        spread, peers * depth + via * extra + turn, owner * depth + rank
    )
    place = jnp.where(spread, via, owner)
    row_of = jnp.where(spread, direct + turn, rank)

    def table(where, row, width, value):
        hot = (where[:, None] == all_peers[None, :]).astype(jnp.float32)
        at = row[:, None] == jnp.arange(width, dtype=jnp.int32)[None, :]
        return lax.dot_general(
            hot,
            jnp.where(at, value.astype(jnp.float32)[:, None], 0.0),
            (((0,), (0,)), ((), ())),
            precision=lax.Precision.HIGHEST,
            preferred_element_type=jnp.float32,
        )

    source_of = jnp.minimum(table(place, row_of, depth + extra, order).astype(jnp.int32), blocks - 1)
    label = table(owner, rank, LANES, slot - owned) + float(owned)
    sent = jnp.broadcast_to(jnp.pad(sums, (0, LANES - peers))[None, :], (peers, LANES))

    sources, labels, position, owner, rank = lax.optimization_barrier(
        (source_of, jnp.stack([label, sent], axis=1), position, owner, rank)
    )
    flat = moisture.reshape(owned * layers, LANES)
    vm = lambda *shape: pltpu.VMEM(shape, jnp.float32)
    iv = lambda *shape: pltpu.VMEM(shape, jnp.int32)
    sm = lambda *shape: pltpu.SMEM(shape, jnp.int32)
    dma = lambda n: pltpu.SemaphoreType.DMA((n,))
    chunks = 8
    tail = (peers * extra + depth - 1) // depth
    high, wide = tile_rows + 2 * SWEEPS, tile_cols + LANES
    for_source = [
        vm(blocks, LANES),
        vm(2, 8, tile_rows),
        vm(2, 8, tile_cols),
        vm(2, 8, tile_rows),
        vm(4, 8, LANES),
        dma(8),
        dma(8),
    ]
    source, stepped, fits, mid_r, mid_c = pl.pallas_call(
        functools.partial(column_kernel, cap, extra, hop, chunks),
        out_shape=[
            f32(high, wide),
            f32(owned * layers, LANES),
            f32(1, 1),
            f32(3, 2 * SWEEPS, tile_cols),
            f32(3, high, LANES),
        ],
        in_specs=[SM, SM] + [VM] * 5 + [pl.BlockSpec(memory_space=pl.ANY), VM],
        out_specs=[VM, pl.BlockSpec(memory_space=pl.ANY), VM, VM, VM],
        scratch_shapes=[
            vm((peers + tail) * depth, LANES),
            vm(blocks, LANES),
            vm(blocks, LANES),
            vm(peers, 2, depth, LANES),
            vm(peers, 2 + 2 * extra, LANES),
            vm(peers, 2, lines, LANES),
            vm(peers, 2 + 2 * extra, LANES),
        ]
        + [vm(owned * layers, LANES)] * 3
        + [vm(owned, LANES)] * 3
        + [
            vm(peers, 2 * hop, LANES),
            vm(peers, 2 * hop, LANES),
            vm(peers, depth, LANES),
            vm(peers, hop, LANES),
            vm(peers, hop, LANES),
            vm(peers, extra, LANES),
            vm(peers, extra, LANES),
            vm(depth, LANES),
            vm(depth, LANES),
            vm(depth, LANES),
            iv(8, LANES),
            iv(extra * peers, LANES),
            iv(peers, LANES),
            iv(8, LANES),
            iv(owned // LANES, LANES),
            vm(2, 24, tile_cols),
            vm(2, 24, tile_rows),
            vm(2, 24, tile_cols),
            vm(2, 24, tile_rows),
            vm(4, 24, LANES),
            sm(peers, LANES),
            sm(8, LANES),
            sm(8, LANES),
            sm(extra * peers, LANES),
            sm(owned // LANES, LANES),
            dma(5),
            dma(chunks),
            dma(chunks),
        ]
        + [dma(peers)] * 12
        + [dma(6), dma(8), dma(8)]
        + for_source,
        compiler_params=pltpu.CompilerParams(
            collective_id=4, has_side_effects=True, vmem_limit_bytes=58 * 2**20
        ),
    )(sources, position, labels, precip, head, trans_coef, land, flat, ksat)


    def relax(source, stepped):
        pieces = 16
        surface, saturation = pl.pallas_call(
            functools.partial(relax_kernel, pieces),
            out_shape=[f32(tile_rows, tile_cols), f32(owned * layers, LANES)],
            in_specs=[VM] * 6 + [pl.BlockSpec(memory_space=pl.ANY)],
            out_specs=[VM, pl.BlockSpec(memory_space=pl.ANY)],
            scratch_shapes=[vm(high, wide)] * 8
            + [vm(owned * layers, LANES), dma(pieces), dma(pieces)],
            compiler_params=pltpu.CompilerParams(vmem_limit_bytes=40 * 2**20),
        )(source, head, trans_coef, land, mid_r, mid_c, stepped)
        return saturation.reshape(owned, layers, LANES), surface

    def hopped():
        return relax(source, stepped)

    def whole():
        step = 128
        layered = pl.BlockSpec((layers, step, LANES), lambda i: (0, i, 0))
        single = pl.BlockSpec((step, LANES), lambda i: (i, 0))
        natural = pl.BlockSpec((step * layers, LANES), lambda i: (i, 0))
        s0, sx, sy, rec0, rec_x, rec_y = pl.pallas_call(
            functools.partial(factor_kernel, layers, 32),
            grid=(owned // step,),
            out_shape=[f32(layers, owned, LANES)] * 3 + [f32(owned, LANES)] * 3,
            in_specs=[natural, single],
            out_specs=[layered] * 3 + [single] * 3,
        )(flat, ksat)
        slots_of = table(owner, rank, cap, order).astype(jnp.int32).reshape(peers * cap)
        outgoing = pl.pallas_call(
            functools.partial(pack_kernel, peers, cap),
            out_shape=f32(peers, 2 * cap + 8, LANES),
            in_specs=[SM, VM, VM, VM, VM],
            out_specs=VM,
            scratch_shapes=[pltpu.VMEM((blocks, LANES), jnp.float32)] * 2,
        )(slots_of, labels[:, 0], precip, head, land)
        arrived = lax.all_to_all(outgoing, ("row", "col"), split_axis=0, concat_axis=0, tiled=True)
        places = arrived[:, 2 * cap, :cap].astype(jnp.int32).reshape(peers * cap)
        answer, infil, sig = pl.pallas_call(
            functools.partial(owner_kernel, peers, cap),
            out_shape=[f32(peers, cap, LANES), f32(owned, LANES), f32(owned, LANES)],
            in_specs=[SM, VM, VM, VM, VM],
            out_specs=[VM] * 3,
            scratch_shapes=[pltpu.VMEM((owned + 8, LANES), jnp.float32)] * 3,
        )(places, arrived, rec0, rec_x, rec_y)
        back = lax.all_to_all(answer, ("row", "col"), split_axis=0, concat_axis=0, tiled=True)
        saturation = pl.pallas_call(
            functools.partial(saturation_kernel, layers),
            grid=(owned // step,),
            out_shape=f32(owned * layers, LANES),
            in_specs=[layered] * 3 + [single] * 2,
            out_specs=natural,
        )(s0, sx, sy, infil, sig)
        source = pl.pallas_call(
            source_kernel,
            out_shape=f32(high, wide),
            in_specs=[SM] + [VM] * 3,
            out_specs=VM,
            scratch_shapes=for_source,
            compiler_params=pltpu.CompilerParams(collective_id=2, has_side_effects=True),
        )(owner * cap + rank, back.reshape(-1, LANES), head, land)
        return relax(source, saturation)

    return lax.cond(fits.reshape(()) > 0.5, hopped, whole)


def solution(mesh):
    tile = P("row", "col")
    placed = (
        tile,
        tile,
        tile,
        tile,
        tile,
        P(("row", "col"), None, None),
        P(("row", "col"), None),
    )
    return jax.shard_map(
        on_device,
        mesh=mesh,
        in_specs=placed,
        out_specs=(P(("row", "col"), None, None), P("row", "col")),
        check_vma=False,
    )
```

```python
import functools
import math

import jax
import jax.numpy as jnp
from jax import lax
from jax.experimental import pallas as pl
from jax.experimental.pallas import tpu as pltpu
from jax.sharding import PartitionSpec as P

SWEEPS = 4
LANES = 128

layer_depth = 0.1
step_ratio = 0.1
residual_water = 0.05
pore_range = 0.4
diff_length = 0.5
couple_rate = 0.05
recharge_gain = 20.0
store_rate = 0.2

VM = pl.BlockSpec(memory_space=pltpu.VMEM)
SM = pl.BlockSpec(memory_space=pltpu.SMEM)


def f32(*shape):
    return jax.ShapeDtypeStruct(shape, jnp.float32)


def factor_rows(layers, moist, ksat, base_row, group):
    rows = pl.ds(pl.multiple_of(base_row, group), group)
    ks = ksat[rows, :]
    ratios, reds, xs = [], [], []
    before = None
    for k in range(layers):
        m = moist[pl.ds(base_row * layers + k, group, stride=layers), :]
        w = (m - residual_water) * (1.0 / pore_range)
        s = ks * math.exp(-(k + 0.5) * layer_depth)
        sw2 = s * (w * w)
        hs = sw2 * (1.5 / pore_range)
        d = s * (0.2 * diff_length / (2.0 * layer_depth)) + sw2 * (
            diff_length / (2.0 * layer_depth)
        )
        hc = 0.5 * (sw2 * w)
        cur = (m, hs, d, hc)
        if before is None:
            before = cur
            g_up = q_up = nsub = None
            continue
        m0, hs0, d0, hc0 = before
        g = d0 + d
        q = (hc0 + hc) - g * (m - m0)
        if g_up is None:
            pivot = step_ratio + g + hs0
            inv = 1.0 / pivot
            reds.append(-q * inv)
            xs.append(inv)
        else:
            pivot = step_ratio + g_up + g - nsub * ratios[-1]
            inv = 1.0 / pivot
            reds.append(((q_up - q) + nsub * reds[-1]) * inv)
            xs.append(nsub * inv * xs[-1])
        ratios.append((g - hs) * inv)
        nsub = hs0 + g
        g_up, q_up = g, q
        before = cur
    m, hs, d, hc = before
    bottom = 2.0 * hc + couple_rate * (m - residual_water)
    pivot = step_ratio + g_up + hs + couple_rate - nsub * ratios[-1]
    inv = 1.0 / pivot
    change = ((q_up - bottom) + nsub * reds[-1]) * inv
    cx = nsub * inv * xs[-1]
    cy = (couple_rate * pore_range) * inv
    gain = 2.0 * hs + couple_rate
    recharge = (
        bottom + gain * change,
        gain * cx,
        gain * cy - couple_rate * pore_range,
    )
    unit = 1.0 / pore_range
    terms = [None] * layers
    for k in range(layers - 1, -1, -1):
        if k < layers - 1:
            change = reds[k] + ratios[k] * change
            cx = xs[k] + ratios[k] * cx
            cy = ratios[k] * cy
        m = moist[pl.ds(base_row * layers + k, group, stride=layers), :]
        terms[k] = ((m + change - residual_water) * unit, cx * unit, cy * unit)
    return recharge, terms


def within(index, size):
    if size & (size - 1) == 0:
        return jnp.bitwise_and(index, size - 1)
    return jnp.clip(index, 0, size - 1)


def fixed_fields(head, trans_coef, land):
    share = land.astype(jnp.float32)
    return trans_coef * (1.0 + 0.5 * jnp.tanh(head)), head * share, share


def neighbours(row, col):
    n_row, n_col = lax.axis_size("row"), lax.axis_size("col")
    up, down = row > 0, row < n_row - 1
    left, right = col > 0, col < n_col - 1
    steps = [(-1, 0), (1, 0), (0, -1), (0, 1), (-1, -1), (-1, 1), (1, -1), (1, 1)]
    go = [up, down, left, right, up & left, up & right, down & left, down & right]
    come = [down, up, right, left, down & right, down & left, up & right, up & left]
    return steps, go, come


def each(flags, act):
    for k, flag in enumerate(flags):
        pl.when(flag)(functools.partial(act, k))


def halo_copy(k, steps, row, col, src, dst, send_sem, recv_sem):
    return pltpu.make_async_remote_copy(
        src_ref=src[k],
        dst_ref=dst[k],
        send_sem=send_sem.at[k],
        recv_sem=recv_sem.at[k],
        device_id=(row + steps[k][0], col + steps[k][1]),
        device_id_type=pl.DeviceIdType.MESH,
    )


def column_kernel(
    cap, extra, hop, chunks, src, position, labels, precip, head, trans_coef, land, moisture, ksat,
    s_ref, saturation, fits, mid_r, mid_c, returned,
    infil, sigs, out, allbuf, labs, moist, sx, sy, rec0, rec_x, rec_y,
    mid_out, arr2, ans, ans2, arr4, out5, arr5, g0, gx, gy, src_v, ret_v, slots_v, slot2_v, inv_v,
    row_out, strip_out, from_row, strip_in, corner,
    slots_s, slot2_s, src_s, ret_s, inv_s,
    move, read, write, send0, recv0, send1, recv1, send2, recv2, send3, recv3, send4, recv4, send5, recv5, own,
    send_h, recv_h, *for_source,
):
    rows, cols = precip.shape
    peers, _, lines, _ = allbuf.shape
    depth = out.shape[2]
    direct = depth - extra
    owned = rec0.shape[0]
    layers = moist.shape[0] // owned
    n_col = lax.axis_size("col")
    row, col = lax.axis_index("row"), lax.axis_index("col")
    me = row * n_col + col
    barrier = pltpu.get_barrier_semaphore()
    part_rows = owned // chunks

    def fetch(c):
        part = pl.ds(c * part_rows * layers, part_rows * layers)
        return pltpu.make_async_copy(moisture.at[part], moist.at[part], read.at[c])

    def flush(c):
        part = pl.ds(c * part_rows * layers, part_rows * layers)
        return pltpu.make_async_copy(moist.at[part], saturation.at[part], write.at[c])

    def where_is(k):
        p = lax.rem(me + k, peers)
        return p, (p // n_col, lax.rem(p, n_col))

    def greet(k, _):
        pl.semaphore_signal(
            barrier, inc=1, device_id=where_is(k)[1], device_id_type=pl.DeviceIdType.MESH
        )
        return 0

    lax.fori_loop(1, peers, greet, 0)
    for c in range(chunks):
        fetch(c).start()

    def exchange(src, dst, send, recv, self_sem):
        def copy(k):
            p, place = where_is(k)
            return pltpu.make_async_remote_copy(
                src_ref=src(p),
                dst_ref=dst(me),
                send_sem=send.at[k],
                recv_sem=recv.at[k],
                device_id=place,
                device_id_type=pl.DeviceIdType.MESH,
            )

        here = pltpu.make_async_copy(src(me), dst(me), self_sem)

        def start(low, high):
            def body(k, _):
                copy(k).start()
                return 0

            lax.fori_loop(low, high, body, 0)

        def wait():
            def body(k, _):
                copy(k).wait()
                return 0

            lax.fori_loop(1, peers, body, 0)
            here.wait()

        return copy, here, start, wait

    for j in range(cols // LANES):
        part = pl.ds(j * LANES, LANES)
        infil[pl.ds(j * rows, rows), :] = precip[:, part] * land[:, part].astype(jnp.float32)
        sigs[pl.ds(j * rows, rows), :] = jax.nn.sigmoid(head[:, part])

    def pack(p):
        for r in range(depth):
            block = within(src[p, r], infil.shape[0])
            out[p, 0, pl.ds(r, 1), :] = infil[pl.ds(block, 1), :]
            out[p, 1, pl.ds(r, 1), :] = sigs[pl.ds(block, 1), :]

    _, here0, start0, wait0 = exchange(
        lambda p: labels.at[p], lambda p: labs.at[p], send0, recv0, own.at[5]
    )
    copy1, here1, _, _ = exchange(
        lambda p: out.at[p], lambda p: allbuf.at[p, :, pl.ds(0, depth)], send1, recv1, own.at[0]
    )
    pl.semaphore_wait(barrier, peers - 1)
    def ship(k, _):
        k = peers - k
        pack(where_is(k)[0])
        copy1(k).start()
        return 0

    ahead = min(5, peers)
    lax.fori_loop(1, ahead, ship, 0)
    here0.start()
    start0(1, peers)
    lax.fori_loop(ahead, peers, ship, 0)
    pack(me)
    here1.start()

    steps, go, come = neighbours(row, col)
    east, south = cols - LANES, rows - 8
    for side, at in enumerate((0, south)):
        edge = pl.ds(at, 8)
        for f, field in enumerate(fixed_fields(head[edge, :], trans_coef[edge, :], land[edge, :])):
            row_out[side, pl.ds(8 * f, 8), :] = field
    for side, at in enumerate((0, east)):
        edge = pl.ds(at, LANES)
        keep = slice(0, 8) if side == 0 else slice(LANES - 8, LANES)
        for f, field in enumerate(fixed_fields(head[:, edge], trans_coef[:, edge], land[:, edge])):
            strip_out[side, pl.ds(8 * f, 8), :] = jnp.transpose(field)[keep]
    halo_dst = [from_row.at[0], from_row.at[1], strip_in.at[0], strip_in.at[1]] + [
        corner.at[c] for c in range(4)
    ]
    halo_src = [row_out.at[0], row_out.at[1], strip_out.at[0], strip_out.at[1]] + [
        row_out.at[c // 2, :, pl.ds((c % 2) * east, LANES)] for c in range(4)
    ]
    for k in range(8):

        @pl.when(jnp.logical_not(come[k]))
        def _(ref=halo_dst[k]):
            ref[...] = jnp.zeros(ref.shape, jnp.float32)

    def halo(k):
        return halo_copy(k, steps, row, col, halo_src, halo_dst, send_h, recv_h)

    each(go, lambda k: halo(k).start())

    group = 32

    def factor(c, _):
        fetch(c).wait()

        def body(i, _):
            base_row = pl.multiple_of(c * part_rows + i * group, group)
            at = pl.ds(base_row, group)
            recharge, terms = factor_rows(layers, moist, ksat, base_row, group)
            for ref, value in zip((rec0, rec_x, rec_y), recharge):
                ref[at, :] = value
            for k in range(layers):
                for ref, value in zip((moist, sx, sy), terms[k]):
                    ref[pl.ds(base_row * layers + k, group, stride=layers), :] = value
            return 0

        lax.fori_loop(0, part_rows // group, body, 0)
        return 0

    lax.fori_loop(0, chunks, factor, 0)
    wait0()

    shape = (peers, LANES)
    lane = lax.broadcasted_iota(jnp.int32, shape, 1)
    sub = lax.broadcasted_iota(jnp.int32, shape, 0)
    lab = labs[:, 0, :]
    count = labs[:, 1, :]
    over = jnp.maximum(count - direct, 0.0)
    tri = lax.broadcasted_iota(jnp.int32, (LANES, LANES), 0) < lax.broadcasted_iota(
        jnp.int32, (LANES, LANES), 1
    )
    base = jnp.dot(
        over, tri.astype(jnp.float32), precision=lax.Precision.HIGHEST,
        preferred_element_type=jnp.float32,
    )
    total = extra * peers
    before = (
        lax.broadcasted_iota(jnp.int32, (total, total), 1)
        < lax.broadcasted_iota(jnp.int32, (total, total), 0)
    ).astype(jnp.float32)

    def number(m):
        gap = m - sub
        return jnp.where(gap < 0, gap + peers, gap).astype(jnp.float32)

    def holds(j, first, many, t):
        j = j + float(t * peers)
        return jnp.where((first <= j) & (j < first + many), 1.0, 0.0)

    def prefix(v):
        return jnp.dot(before, v, preferred_element_type=jnp.float32)

    flane = lane.astype(jnp.float32)
    code = sub.astype(jnp.float32) * 8.0
    via = jnp.concatenate([holds(number(me), base, over, t) for t in range(extra)], axis=0)
    rank = prefix(via)
    codes = jnp.concatenate([code + float(t) for t in range(extra)], axis=0)
    lanes = jnp.concatenate([flane] * extra, axis=0)
    back = jnp.sum(via * (lanes * hop + rank), axis=1, keepdims=True)
    ret_v[...] = jnp.broadcast_to(back, (total, LANES)).astype(jnp.int32)
    pad = jnp.zeros((8 - hop, LANES), jnp.float32)
    picks = [
        jnp.sum(jnp.where(rank == float(e), via * codes, 0.0), axis=0, keepdims=True)
        for e in range(hop)
    ]
    src_v[...] = jnp.concatenate(picks + [pad], axis=0).astype(jnp.int32)
    mine = jnp.where(lane == me, 1.0, 0.0)
    first = jnp.sum(base * mine, axis=1, keepdims=True)
    many = jnp.sum(over * mine, axis=1, keepdims=True)
    inside = jnp.where(lane < peers, 1.0, 0.0)
    step = number(lane)
    took = [holds(step, first, many, t) * inside for t in range(extra)]
    value = []
    for t in range(extra):
        at = step + float(t * peers) - first
        v = jnp.zeros(shape, jnp.float32)
        for r in range(cap - direct):
            v = jnp.where(at == float(r), lab[:, direct + r : direct + r + 1] - float(owned), v)
        value.append(v)
    took = jnp.concatenate(took, axis=0)
    rank = prefix(took)
    value = jnp.concatenate(value, axis=0)
    picks = [
        jnp.sum(jnp.where(rank == float(e), took * value, 0.0), axis=0, keepdims=True)
        for e in range(hop)
    ]
    hopped = jnp.concatenate(picks + [pad], axis=0) + float(owned)
    slot2_v[...] = hopped.astype(jnp.int32)
    slots_v[...] = lab.astype(jnp.int32)
    moves = [
        pltpu.make_async_copy(src_v, src_s, move.at[0]),
        pltpu.make_async_copy(slots_v, slots_s, move.at[1]),
        pltpu.make_async_copy(slot2_v, slot2_s, move.at[2]),
        pltpu.make_async_copy(ret_v, ret_s, move.at[3]),
    ]
    for m in moves:
        m.start()
    g0[...] = jnp.zeros(g0.shape, jnp.float32)
    gx[...] = jnp.zeros(gx.shape, jnp.float32)
    gy[...] = jnp.zeros(gy.shape, jnp.float32)
    for m in moves:
        m.wait()

    def answer(q):
        for r in range(direct):
            slot = within(slots_s[q, r], owned)
            g0[pl.ds(r, 1), :] = rec0[pl.ds(slot, 1), :]
            gx[pl.ds(r, 1), :] = rec_x[pl.ds(slot, 1), :]
            gy[pl.ds(r, 1), :] = rec_y[pl.ds(slot, 1), :]
        ans[q] = (
            g0[...]
            + allbuf[q, 0, pl.ds(0, depth), :] * gx[...]
            + allbuf[q, 1, pl.ds(0, depth), :] * gy[...]
        )

    here1.wait()
    answer(me)

    def receive(k, _):
        k = peers - k
        copy1(k).wait_recv()
        answer(lax.rem(me + peers - k, peers))
        return 0

    lax.fori_loop(1, peers, receive, 0)

    def pass_on(d, _):
        for e in range(hop):
            q = src_s[e, d]
            s = jnp.clip(q // 8, 0, peers - 1)
            t = jnp.clip(q - s * 8, 0, extra - 1)
            mid_out[d, pl.ds(e, 1), :] = allbuf[s, 0, pl.ds(direct + t, 1), :]
            mid_out[d, pl.ds(hop + e, 1), :] = allbuf[s, 1, pl.ds(direct + t, 1), :]
        return 0

    lax.fori_loop(0, peers, pass_on, 0)
    _, here2, start2, wait2 = exchange(
        lambda p: mid_out.at[p], lambda p: arr2.at[p], send2, recv2, own.at[1]
    )
    _, here3, start3, wait3 = exchange(
        lambda p: ans.at[p],
        lambda p: returned.at[pl.ds(pl.multiple_of(p * depth, 8), depth)],
        send3, recv3, own.at[2]
    )
    _, here4, start4, wait4 = exchange(
        lambda p: ans2.at[p], lambda p: arr4.at[p], send4, recv4, own.at[3]
    )
    _, here5, start5, wait5 = exchange(
        lambda p: out5.at[p], lambda p: arr5.at[p], send5, recv5, own.at[4]
    )
    thirds = [1, peers // 3, 2 * peers // 3, peers]
    here2.start()
    start2(1, peers)
    here3.start()
    start3(thirds[0], thirds[1])

    columns = jnp.transpose(
        jnp.concatenate([hopped, jnp.zeros((LANES - 8, LANES), jnp.float32)], axis=0)
    )
    place = sub.astype(jnp.float32) * float(lines)
    for g in range(owned // LANES):
        want = flane + float(g * LANES)
        found = jnp.zeros(shape, jnp.float32)
        for r in range(direct):
            found = jnp.where(lab[:, r : r + 1] == want, place + float(r), found)
        for e in range(hop):
            found = jnp.where(
                columns[0:peers, e : e + 1] == want, place + float(depth + e), found
            )
        inv_v[pl.ds(g, 1), :] = jnp.sum(found, axis=0, keepdims=True).astype(jnp.int32)
    turn = pltpu.make_async_copy(inv_v, inv_s, move.at[4])
    turn.start()

    def widest(m, most):
        n = number(m)
        seen = functools.reduce(lambda x, y: x + y, [holds(n, base, over, t) for t in range(extra)])
        return jnp.maximum(most, jnp.sum(seen, axis=0, keepdims=True))

    most = lax.fori_loop(0, peers, widest, jnp.zeros((1, LANES), jnp.float32))
    spread = jnp.max(jnp.sum(over, axis=1, keepdims=True), axis=0, keepdims=True)
    bad = jnp.maximum(
        jnp.where(jnp.max(most, axis=1, keepdims=True) > float(hop), 1.0, 0.0),
        jnp.where(spread > float(total), 1.0, 0.0),
    )
    fits[...] = jnp.broadcast_to(1.0 - bad, fits.shape)

    def landed(k):
        return pltpu.make_async_remote_copy(
            src_ref=halo_src[k],
            dst_ref=halo_dst[k],
            send_sem=send_h.at[k],
            recv_sem=recv_h.at[k],
            device_id=(row, col),
            device_id_type=pl.DeviceIdType.MESH,
        )

    each(go, lambda k: halo(k).wait_send())
    each(come, lambda k: landed(k).wait_recv())
    upper = lax.broadcasted_iota(jnp.int32, (8, LANES), 0) < 4
    near = lax.broadcasted_iota(jnp.int32, (8, LANES), 1) < LANES // 2
    for f in range(3):
        eight = pl.ds(8 * f, 8)
        for j in range(cols // LANES):
            part = pl.ds(j * LANES, LANES)
            mid_r[f, :, part] = jnp.where(upper, from_row[0, eight, part], from_row[1, eight, part])
        mid_c[f, pl.ds(rows, 8), :] = jnp.where(
            upper,
            jnp.where(near, corner[0, eight, :], corner[1, eight, :]),
            jnp.where(near, corner[2, eight, :], corner[3, eight, :]),
        )
        mid_c[f, pl.ds(0, rows), :] = jnp.transpose(
            jnp.concatenate(
                [
                    strip_in[0, eight, :],
                    jnp.zeros((LANES - 16, rows), jnp.float32),
                    strip_in[1, eight, :],
                ],
                axis=0,
            )
        )
    turn.wait()
    wait2()

    def answer2(m, _):
        for e in range(hop):
            slot = within(slot2_s[e, m], owned)
            inf, sg = arr2[m, pl.ds(e, 1), :], arr2[m, pl.ds(hop + e, 1), :]
            ans2[m, pl.ds(e, 1), :] = (
                rec0[pl.ds(slot, 1), :]
                + inf * rec_x[pl.ds(slot, 1), :]
                + sg * rec_y[pl.ds(slot, 1), :]
            )
            allbuf[m, 0, pl.ds(depth + e, 1), :] = inf
            allbuf[m, 1, pl.ds(depth + e, 1), :] = sg
        return 0

    lax.fori_loop(0, peers, answer2, 0)
    here4.start()
    start4(1, peers)
    start3(thirds[1], thirds[2])

    def finish(c, _):
        def body(i, _):
            for u in range(8):
                n = c * part_rows + i * 8 + u
                v = inv_s[n // LANES, lax.rem(n, LANES)]
                p = jnp.minimum(lax.shift_right_logical(v, bits), peers - 1)
                r = jnp.bitwise_and(v, lines - 1)
                inf = allbuf[p, 0, pl.ds(r, 1), :]
                sg = allbuf[p, 1, pl.ds(r, 1), :]
                at = pl.ds(pl.multiple_of(n * layers, layers), layers)
                moist[at, :] = moist[at, :] + inf * sx[at, :] + sg * sy[at, :]
            return 0

        lax.fori_loop(0, part_rows // 8, body, 0)
        flush(c).start()
        return 0

    bits = lines.bit_length() - 1
    lax.fori_loop(0, chunks // 2, finish, 0)
    wait4()

    def hand_back(s, _):
        for t in range(extra):
            at = jnp.clip(ret_s[t * peers + s, 0], 0, peers * hop - 1)
            d = at // hop
            out5[s, pl.ds(t, 1), :] = arr4[d, pl.ds(at - d * hop, 1), :]
        return 0

    lax.fori_loop(0, peers, hand_back, 0)
    here5.start()
    start5(1, peers)
    start3(thirds[2], thirds[3])
    lax.fori_loop(chunks // 2, chunks, finish, 0)

    wait5()
    for i in range(total):
        returned[pl.ds(peers * depth + i, 1), :] = arr5[i // extra, pl.ds(i % extra, 1), :]
    wait3()
    spread_source(
        position, returned, head, land, s_ref, *for_source, ready=lambda: None
    )

    def sent(k, _):
        copy1(k).wait_send()
        return 0

    lax.fori_loop(1, peers, sent, 0)
    for c in range(chunks):
        flush(c).wait()


def pack_kernel(peers, per_peer, src, labels, precip, head, land, out, infil, heads):
    rows, cols = precip.shape
    for j in range(cols // LANES):
        part = pl.ds(j * LANES, LANES)
        infil[pl.ds(j * rows, rows), :] = precip[:, part] * land[:, part].astype(jnp.float32)
        heads[pl.ds(j * rows, rows), :] = head[:, part]

    def body(p, _):
        for r in range(per_peer):
            block = src[p * per_peer + r]
            out[p, pl.ds(r, 1), :] = infil[pl.ds(block, 1), :]
            out[p, pl.ds(per_peer + r, 1), :] = heads[pl.ds(block, 1), :]
        out[p, pl.ds(2 * per_peer, 8), :] = jnp.broadcast_to(labels[pl.ds(p, 1), :], (8, LANES))
        return 0

    lax.fori_loop(0, peers, body, 0)


def owner_kernel(
    peers, per_peer, slots, arrived, rec0, rec_x, rec_y, answer, infil, sig, own_i, own_h, rec
):
    owned = rec0.shape[0]

    def scatter(p, _):
        for r in range(per_peer):
            slot = slots[p * per_peer + r]
            own_i[pl.ds(slot, 1), :] = arrived[p, pl.ds(r, 1), :]
            own_h[pl.ds(slot, 1), :] = arrived[p, pl.ds(per_peer + r, 1), :]
        return 0

    lax.fori_loop(0, peers, scatter, 0)
    rec[pl.ds(owned, 8), :] = jnp.zeros((8, LANES), jnp.float32)

    def combine(g, _):
        part = pl.ds(g * 64, 64)
        inf = own_i[part, :]
        sg = jax.nn.sigmoid(own_h[part, :])
        infil[part, :] = inf
        sig[part, :] = sg
        rec[part, :] = rec0[part, :] + inf * rec_x[part, :] + sg * rec_y[part, :]
        return 0

    lax.fori_loop(0, owned // 64, combine, 0)

    def gather(p, _):
        for r in range(per_peer):
            slot = slots[p * per_peer + r]
            answer[p, pl.ds(r, 1), :] = rec[pl.ds(slot, 1), :]
        return 0

    lax.fori_loop(0, peers, gather, 0)


def factor_kernel(layers, group, moist, ksat, s0, sx, sy, rec0, rec_x, rec_y):
    def body(step, _):
        base_row = step * group
        rows = pl.ds(pl.multiple_of(base_row, group), group)
        recharge, terms = factor_rows(layers, moist, ksat, base_row, group)
        for ref, value in zip((rec0, rec_x, rec_y), recharge):
            ref[rows, :] = value
        for k in range(layers):
            for ref, value in zip((s0, sx, sy), terms[k]):
                ref[k, rows, :] = value
        return 0

    lax.fori_loop(0, ksat.shape[0] // group, body, 0)


def saturation_kernel(layers, s0, sx, sy, infil, sig, out):
    count = infil.shape[0]
    group = 32

    def body(step, _):
        rows = pl.ds(pl.multiple_of(step * group, group), group)
        inf = infil[rows, :]
        sg = sig[rows, :]
        for k in range(layers):
            out[pl.ds(step * group * layers + k, group, stride=layers), :] = (
                s0[k, rows, :] + inf * sx[k, rows, :] + sg * sy[k, rows, :]
            )
        return 0

    lax.fori_loop(0, count // group, body, 0)


def spread_source(
    position, returned, head, land, s_ref,
    sorted_rows, strip_out, from_row, strip_in, corner, send_sem, recv_sem, ready,
):
    rows, cols = head.shape
    high, wide = s_ref.shape
    row, col = lax.axis_index("row"), lax.axis_index("col")
    steps, go, come = neighbours(row, col)
    east, south = cols - LANES, rows - 8
    src = [
        s_ref.at[pl.ds(0, 8), pl.ds(0, cols)],
        s_ref.at[pl.ds(south, 8), pl.ds(0, cols)],
        strip_out.at[0],
        strip_out.at[1],
    ] + [s_ref.at[pl.ds(y, 8), pl.ds(x, LANES)] for y in (0, south) for x in (0, east)]
    dst = [from_row.at[0], from_row.at[1], strip_in.at[0], strip_in.at[1]] + [
        corner.at[c] for c in range(4)
    ]
    for k in range(8):

        @pl.when(jnp.logical_not(come[k]))
        def _(ref=dst[k]):
            ref[...] = jnp.zeros(ref.shape, jnp.float32)

    def fill(j, g):
        base = pl.multiple_of(g * 32, 32)
        for u in range(32):
            at = j * rows + base + u
            place = jnp.clip(position[at], 0, returned.shape[0] - 1)
            sorted_rows[pl.ds(at, 1), :] = returned[pl.ds(place, 1), :]
        at, part = pl.ds(base, 32), pl.ds(j * LANES, LANES)
        s_ref[at, part] = (
            store_rate * (head[at, part] * land[at, part].astype(jnp.float32))
            + recharge_gain * sorted_rows[pl.ds(j * rows + base, 32), :]
        )

    def fill_range(j, low, high):
        def body(g, _):
            fill(j, g)
            return 0

        lax.fori_loop(low, high, body, 0)

    groups, strips = rows // 32, cols // LANES
    fill_range(0, 0, groups)
    fill_range(strips - 1, 0, groups)
    strip_out[0] = jnp.transpose(s_ref[0:rows, 0:LANES])[0:8]
    strip_out[1] = jnp.transpose(s_ref[0:rows, east:cols])[LANES - 8 : LANES]
    for j in range(1, strips - 1):
        fill(j, 0)
        fill(j, groups - 1)
    ready()

    def copy(k):
        return halo_copy(k, steps, row, col, src, dst, send_sem, recv_sem)

    def landed(k):
        return halo_copy(k, [(0, 0)] * 8, row, col, src, dst, send_sem, recv_sem)

    each(go, lambda k: copy(k).start())
    for j in range(1, strips - 1):
        fill_range(j, 1, groups - 1)
    each(go, lambda k: copy(k).wait_send())
    each(come, lambda k: landed(k).wait_recv())
    first = lax.broadcasted_iota(jnp.int32, (8, LANES), 0) < 4
    near = lax.broadcasted_iota(jnp.int32, (8, LANES), 1) < LANES // 2
    for j in range(strips):
        part = slice(j * LANES, (j + 1) * LANES)
        s_ref[rows:high, part] = jnp.where(first, from_row[0, :, part], from_row[1, :, part])
    s_ref[rows:high, cols:wide] = jnp.where(
        first,
        jnp.where(near, corner[0], corner[1]),
        jnp.where(near, corner[2], corner[3]),
    )
    s_ref[0:rows, cols:wide] = jnp.transpose(
        jnp.concatenate(
            [strip_in[0], jnp.zeros((LANES - 16, rows), jnp.float32), strip_in[1]], axis=0
        )
    )


def source_kernel(position, returned, head, land, s_ref, *scratch):
    row, col = lax.axis_index("row"), lax.axis_index("col")
    steps, go, _ = neighbours(row, col)
    barrier = pltpu.get_barrier_semaphore()

    def greet(k):
        pl.semaphore_signal(
            barrier,
            inc=1,
            device_id=(row + steps[k][0], col + steps[k][1]),
            device_id_type=pl.DeviceIdType.MESH,
        )

    each(go, greet)

    def ready():
        pl.semaphore_wait(
            barrier, functools.reduce(lambda x, y: x + y, [f.astype(jnp.int32) for f in go])
        )

    spread_source(position, returned, head, land, s_ref, *scratch, ready)


def relax_kernel(
    pieces, source, head, trans_coef, land, mid_r, mid_c, stepped, out, saturation,
    t_ref, s_ref, fu, fd, fl, fr, a, b, held, read, write,
):
    rows, cols = head.shape
    high, wide = t_ref.shape
    each_rows = stepped.shape[0] // pieces
    parts = [pl.ds(c * each_rows, each_rows) for c in range(pieces)]
    reads = [
        pltpu.make_async_copy(stepped.at[p], held.at[p], read.at[c]) for c, p in enumerate(parts)
    ]
    writes = [
        pltpu.make_async_copy(held.at[p], saturation.at[p], write.at[c])
        for c, p in enumerate(parts)
    ]
    for copy in reads:
        copy.start()
    left = list(range(pieces))

    def pass_piece():
        if left:
            c = left.pop(0)
            reads[c].wait()
            writes[c].start()

    for f, (ref, centre) in enumerate(
        zip((t_ref, a, b), fixed_fields(head[...], trans_coef[...], land[...]))
    ):
        ref[0:rows, 0:cols] = centre
        ref[rows:high, 0:cols] = mid_r[f]
        ref[:, cols:wide] = mid_c[f]
    for g in range(wide // LANES):
        part = slice(g * LANES, (g + 1) * LANES)
        lo = slice((g - 1) % (wide // LANES) * LANES, (g - 1) % (wide // LANES) * LANES + LANES)
        hi = slice((g + 1) % (wide // LANES) * LANES, (g + 1) % (wide // LANES) * LANES + LANES)
        lane = lax.broadcasted_iota(jnp.int32, (high, LANES), 1)
        t = t_ref[:, part]
        tu = 0.5 * (t + pltpu.roll(t, 1, 0))
        td = 0.5 * (t + pltpu.roll(t, high - 1, 0))
        tl = jnp.where(lane == 0, pltpu.roll(t_ref[:, lo], 1, 1), pltpu.roll(t, 1, 1))
        tr = jnp.where(
            lane == LANES - 1,
            pltpu.roll(t_ref[:, hi], LANES - 1, 1),
            pltpu.roll(t, LANES - 1, 1),
        )
        lf = 0.5 * (t + tl)
        rt = 0.5 * (t + tr)
        inv = b[:, part] / (store_rate + (tu + td + lf + rt))
        fu[:, part] = tu * inv
        fd[:, part] = td * inv
        fl[:, part] = lf * inv
        fr[:, part] = rt * inv
        s_ref[:, part] = source[:, part] * inv
        pass_piece()
        if g > 1:
            pass_piece()
    now, later = a, b
    for sweep in range(SWEEPS):
        last = sweep == SWEEPS - 1
        for g in range(wide // LANES):
            if last and g * LANES >= cols:
                continue
            pass_piece()
            part = slice(g * LANES, (g + 1) * LANES)
            lo = (g - 1) % (wide // LANES) * LANES
            hi = (g + 1) % (wide // LANES) * LANES
            lane = lax.broadcasted_iota(jnp.int32, (high, LANES), 1)
            x = now[:, part]
            xl = jnp.where(
                lane == 0, pltpu.roll(now[:, lo : lo + LANES], 1, 1), pltpu.roll(x, 1, 1)
            )
            xr = jnp.where(
                lane == LANES - 1,
                pltpu.roll(now[:, hi : hi + LANES], LANES - 1, 1),
                pltpu.roll(x, LANES - 1, 1),
            )
            y = s_ref[:, part] + fu[:, part] * pltpu.roll(x, 1, 0)
            y = y + fd[:, part] * pltpu.roll(x, high - 1, 0)
            y = y + (fl[:, part] * xl + fr[:, part] * xr)
            if last:
                out[:, part] = y[0:rows]
            else:
                later[:, part] = y
        now, later = later, now
    while left:
        pass_piece()
    for copy in writes:
        copy.wait()


def on_device(precip, head, trans_coef, land, dest, moisture, ksat):
    tile_rows, tile_cols = precip.shape
    n_col = lax.axis_size("col")
    peers = lax.axis_size("row") * n_col
    me = lax.axis_index("row") * n_col + lax.axis_index("col")
    owned, layers, _ = moisture.shape
    blocks = tile_rows * tile_cols // LANES
    cap = (2 * blocks + peers - 1) // peers
    extra, hop = 2, 4
    depth = (19 * blocks // (16 * peers) + 1 + 7) // 8 * 8
    direct = depth - extra
    lines = 1 << (depth + hop - 1).bit_length()

    target = dest.T.reshape(blocks)
    owner = target // owned
    slot = target - owner * owned
    all_peers = jnp.arange(peers, dtype=jnp.int32)
    one_hot = owner[:, None] == all_peers[None, :]
    order = jnp.arange(blocks, dtype=jnp.int32)
    earlier = (order[None, :] < order[:, None]).astype(jnp.bfloat16)
    counts = jnp.dot(earlier, one_hot.astype(jnp.bfloat16), preferred_element_type=jnp.float32)
    sums = jnp.sum(one_hot.astype(jnp.float32), axis=0)
    over = jnp.maximum(sums - direct, 0.0)
    base = jnp.sum(jnp.where(all_peers[:, None] < all_peers[None, :], over[:, None], 0.0), axis=0)
    rank = jnp.sum(jnp.where(one_hot, counts, 0.0), axis=1).astype(jnp.int32)
    number = jnp.sum(jnp.where(one_hot, counts + base[None, :] - direct, 0.0), axis=1).astype(
        jnp.int32
    )
    spread = rank >= direct
    via = (jnp.maximum(number, 0) + me) % peers
    turn = jnp.clip(number // peers, 0, extra - 1)
    position = jnp.where(
        spread, peers * depth + via * extra + turn, owner * depth + rank
    )
    place = jnp.where(spread, via, owner)
    row_of = jnp.where(spread, direct + turn, rank)

    def table(where, row, width, value):
        hot = (where[:, None] == all_peers[None, :]).astype(jnp.float32)
        at = row[:, None] == jnp.arange(width, dtype=jnp.int32)[None, :]
        return lax.dot_general(
            hot,
            jnp.where(at, value.astype(jnp.float32)[:, None], 0.0),
            (((0,), (0,)), ((), ())),
            precision=lax.Precision.HIGHEST,
            preferred_element_type=jnp.float32,
        )

    source_of = jnp.minimum(table(place, row_of, depth, order).astype(jnp.int32), blocks - 1)
    label = table(owner, rank, LANES, slot - owned) + float(owned)
    sent = jnp.broadcast_to(jnp.pad(sums, (0, LANES - peers))[None, :], (peers, LANES))

    sources, labels, position, owner, rank = lax.optimization_barrier(
        (source_of, jnp.stack([label, sent], axis=1), position, owner, rank)
    )
    flat = moisture.reshape(owned * layers, LANES)
    vm = lambda *shape: pltpu.VMEM(shape, jnp.float32)
    iv = lambda *shape: pltpu.VMEM(shape, jnp.int32)
    sm = lambda *shape: pltpu.SMEM(shape, jnp.int32)
    dma = lambda n: pltpu.SemaphoreType.DMA((n,))
    chunks = 8
    tail = (peers * extra + depth - 1) // depth
    high, wide = tile_rows + 2 * SWEEPS, tile_cols + LANES
    for_source = [
        vm(blocks, LANES),
        vm(2, 8, tile_rows),
        vm(2, 8, tile_cols),
        vm(2, 8, tile_rows),
        vm(4, 8, LANES),
        dma(8),
        dma(8),
    ]
    source, stepped, fits, mid_r, mid_c = pl.pallas_call(
        functools.partial(column_kernel, cap, extra, hop, chunks),
        out_shape=[
            f32(high, wide),
            f32(owned * layers, LANES),
            f32(1, 1),
            f32(3, 2 * SWEEPS, tile_cols),
            f32(3, high, LANES),
        ],
        in_specs=[SM, SM] + [VM] * 5 + [pl.BlockSpec(memory_space=pl.ANY), VM],
        out_specs=[VM, pl.BlockSpec(memory_space=pl.ANY), VM, VM, VM],
        scratch_shapes=[
            vm((peers + tail) * depth, LANES),
            vm(blocks, LANES),
            vm(blocks, LANES),
            vm(peers, 2, depth, LANES),
            vm(peers, 2, lines, LANES),
            vm(peers, 2, LANES),
        ]
        + [vm(owned * layers, LANES)] * 3
        + [vm(owned, LANES)] * 3
        + [
            vm(peers, 2 * hop, LANES),
            vm(peers, 2 * hop, LANES),
            vm(peers, depth, LANES),
            vm(peers, hop, LANES),
            vm(peers, hop, LANES),
            vm(peers, extra, LANES),
            vm(peers, extra, LANES),
            vm(depth, LANES),
            vm(depth, LANES),
            vm(depth, LANES),
            iv(8, LANES),
            iv(extra * peers, LANES),
            iv(peers, LANES),
            iv(8, LANES),
            iv(owned // LANES, LANES),
            vm(2, 24, tile_cols),
            vm(2, 24, tile_rows),
            vm(2, 24, tile_cols),
            vm(2, 24, tile_rows),
            vm(4, 24, LANES),
            sm(peers, LANES),
            sm(8, LANES),
            sm(8, LANES),
            sm(extra * peers, LANES),
            sm(owned // LANES, LANES),
            dma(5),
            dma(chunks),
            dma(chunks),
        ]
        + [dma(peers)] * 12
        + [dma(6), dma(8), dma(8)]
        + for_source,
        compiler_params=pltpu.CompilerParams(
            collective_id=4, has_side_effects=True, vmem_limit_bytes=58 * 2**20
        ),
    )(sources, position, labels, precip, head, trans_coef, land, flat, ksat)


    def relax(source, stepped):
        pieces = 16
        surface, saturation = pl.pallas_call(
            functools.partial(relax_kernel, pieces),
            out_shape=[f32(tile_rows, tile_cols), f32(owned * layers, LANES)],
            in_specs=[VM] * 6 + [pl.BlockSpec(memory_space=pl.ANY)],
            out_specs=[VM, pl.BlockSpec(memory_space=pl.ANY)],
            scratch_shapes=[vm(high, wide)] * 8
            + [vm(owned * layers, LANES), dma(pieces), dma(pieces)],
            compiler_params=pltpu.CompilerParams(vmem_limit_bytes=40 * 2**20),
        )(source, head, trans_coef, land, mid_r, mid_c, stepped)
        return saturation.reshape(owned, layers, LANES), surface

    def hopped():
        return relax(source, stepped)

    def whole():
        step = 128
        layered = pl.BlockSpec((layers, step, LANES), lambda i: (0, i, 0))
        single = pl.BlockSpec((step, LANES), lambda i: (i, 0))
        natural = pl.BlockSpec((step * layers, LANES), lambda i: (i, 0))
        s0, sx, sy, rec0, rec_x, rec_y = pl.pallas_call(
            functools.partial(factor_kernel, layers, 32),
            grid=(owned // step,),
            out_shape=[f32(layers, owned, LANES)] * 3 + [f32(owned, LANES)] * 3,
            in_specs=[natural, single],
            out_specs=[layered] * 3 + [single] * 3,
        )(flat, ksat)
        slots_of = table(owner, rank, cap, order).astype(jnp.int32).reshape(peers * cap)
        outgoing = pl.pallas_call(
            functools.partial(pack_kernel, peers, cap),
            out_shape=f32(peers, 2 * cap + 8, LANES),
            in_specs=[SM, VM, VM, VM, VM],
            out_specs=VM,
            scratch_shapes=[pltpu.VMEM((blocks, LANES), jnp.float32)] * 2,
        )(slots_of, labels[:, 0], precip, head, land)
        arrived = lax.all_to_all(outgoing, ("row", "col"), split_axis=0, concat_axis=0, tiled=True)
        places = arrived[:, 2 * cap, :cap].astype(jnp.int32).reshape(peers * cap)
        answer, infil, sig = pl.pallas_call(
            functools.partial(owner_kernel, peers, cap),
            out_shape=[f32(peers, cap, LANES), f32(owned, LANES), f32(owned, LANES)],
            in_specs=[SM, VM, VM, VM, VM],
            out_specs=[VM] * 3,
            scratch_shapes=[pltpu.VMEM((owned + 8, LANES), jnp.float32)] * 3,
        )(places, arrived, rec0, rec_x, rec_y)
        back = lax.all_to_all(answer, ("row", "col"), split_axis=0, concat_axis=0, tiled=True)
        saturation = pl.pallas_call(
            functools.partial(saturation_kernel, layers),
            grid=(owned // step,),
            out_shape=f32(owned * layers, LANES),
            in_specs=[layered] * 3 + [single] * 2,
            out_specs=natural,
        )(s0, sx, sy, infil, sig)
        source = pl.pallas_call(
            source_kernel,
            out_shape=f32(high, wide),
            in_specs=[SM] + [VM] * 3,
            out_specs=VM,
            scratch_shapes=for_source,
            compiler_params=pltpu.CompilerParams(collective_id=2, has_side_effects=True),
        )(owner * cap + rank, back.reshape(-1, LANES), head, land)
        return relax(source, saturation)

    return lax.cond(fits.reshape(()) > 0.5, hopped, whole)


def solution(mesh):
    tile = P("row", "col")
    placed = (
        tile,
        tile,
        tile,
        tile,
        tile,
        P(("row", "col"), None, None),
        P(("row", "col"), None),
    )
    return jax.shard_map(
        on_device,
        mesh=mesh,
        in_specs=placed,
        out_specs=(P(("row", "col"), None, None), P("row", "col")),
        check_vma=False,
    )
```
